128 devices in a mesh: tm: 64 (over y, z, x), sens: 2 (over core).
Axes of the slice: x: 4, y: 4, z: 4, core: 2. Of those that a mesh axis runs over, the one named last changes fastest.
Arguments:
- telemetry: float32 [32768, 512], P('tm', 'sens'), may hold values from -6 to 6
- present: int32 [2048, 8], P('tm', 'sens'), may hold values 0 or 1
- transition: float32 [128, 128], replicated, may hold values from -1 to 1, as said below
- sensing: float32 [512, 128], P('sens'), may hold values from -3 to 3, as said below
- filter_gain: float32 [128, 512], P(None, 'sens'), may hold values from -1 to 1, as said below
- smooth_gain: float32 [128, 128], replicated, may hold values from -1 to 1, as said below
- initial_state: float32 [128], replicated, may hold values from -6 to 6
Outputs:
- new_transition: float32 [128, 128], replicated
- new_sensing: float32 [512, 128], P('sens')
- smoothed: float32 [32768, 128], P('tm')
The draws below stay inside these ranges and needn't reach their ends.
Inputs may be any that keep to these rules, and one draw needn't show every extreme that they name: `transition`: the previous iteration's estimate of the transition matrix; every entry lies between -1 and 1. `sensing`: the previous iteration's estimate of the observation matrix; every entry lies between -3 and 3. `filter_gain`: the previous iteration's steady filter gain; every entry lies between -1 and 1. `smooth_gain`: the previous iteration's steady smoother gain; every entry lies between -1 and 1.
All inputs are finite; a program needn't handle non-finite values. No bound on the sum of `present` on one device may be relied on, other than what follows from the above.
Results may differ from the reference program's by a relative error of at most 0.014.
Values sent between devices are 32-bit elements; how exact they have to be, the bound alone decides.
No kernel may reach another device: no remote copies, remote signals or barrier semaphores. Data moves between devices by JAX's collectives and lax.ppermute only.
A program may use at most 128 MiB of HBM per device.

```python
import math
import jax
import jax.numpy as jnp
from jax import lax

S = 128
NS = 512
NB = 8
SEG = 16
TM_DEV = 512
STEPS = 32768


def slow_channels(key):
    slow_count = S // 2
    ranking = jax.random.permutation(jax.random.fold_in(key, 101), S)
    slow_mask = ranking < slow_count
    fast_count = float(S - slow_count)
    return (slow_mask, fast_count, float(slow_count))


def slow_rotation(key, slow_mask, slow_count):
    noise = jax.random.truncated_normal(key, -3.0, 3.0, (S, S), jnp.float32)
    skew = (noise - noise.T) * (0.5 / (TM_DEV * math.sqrt(2.0 * slow_count)))
    slow_pair = jnp.logical_and(slow_mask[:, None], slow_mask[None, :])
    return jnp.where(slow_pair, skew, 0.0)


def state_matrix(key, tag, low_rate, high_rate):
    slow_mask, fast_count, slow_count = slow_channels(key)
    subkeys = jax.random.split(jax.random.fold_in(key, tag), 4)
    spread = jnp.exp(jax.random.uniform(subkeys[0], (S,), jnp.float32, math.log(0.2), math.log(2.0)))
    slow_rate = jnp.exp(-spread / STEPS)
    fast_rate = jax.random.uniform(subkeys[1], (S,), jnp.float32, low_rate, high_rate)
    noise = jax.random.truncated_normal(subkeys[2], -3.0, 3.0, (S, S), jnp.float32)
    diagonal = jnp.eye(S, dtype=bool)
    slow_row = slow_mask[:, None]
    fast_col = jnp.logical_not(slow_mask)[None, :]
    fast_pair = jnp.logical_and(jnp.logical_and(jnp.logical_not(slow_row), fast_col), jnp.logical_not(diagonal))
    slow_fast = jnp.logical_and(slow_row, fast_col)
    rates = jnp.where(slow_mask, slow_rate, fast_rate)
    result = jnp.where(diagonal, rates[None, :], 0.0)
    result = result + jnp.where(fast_pair, noise * (0.15 / math.sqrt(fast_count)), 0.0)
    result = result + jnp.where(slow_fast, noise * (0.5 / math.sqrt(fast_count * STEPS)), 0.0)
    result = result + slow_rotation(subkeys[3], slow_mask, slow_count)
    return result.astype(jnp.float32)


def draw_transition(key, part):
    return state_matrix(key, 1, 0.3, 0.55)


def draw_sensing(key, part):
    slow_mask, fast_count, slow_count = slow_channels(key)
    noise = jax.random.truncated_normal(jax.random.fold_in(key, 2), -3.0, 3.0, (NS, S), jnp.float32)
    column_scale = jnp.where(slow_mask, 1.0 / math.sqrt(slow_count * STEPS), 1.0 / math.sqrt(fast_count))
    return (noise * column_scale[None, :]).astype(jnp.float32)


def draw_filter_gain(key, part):
    slow_mask, fast_count, slow_count = slow_channels(key)
    noise = jax.random.truncated_normal(jax.random.fold_in(key, 3), -3.0, 3.0, (S, NS), jnp.float32)
    row_scale = jnp.where(slow_mask, 1.0 / math.sqrt(NS * STEPS), 0.08 / math.sqrt(NS))
    return (noise * row_scale[:, None]).astype(jnp.float32)


def draw_smooth_gain(key, part):
    return state_matrix(key, 4, 0.2, 0.45)


def place_ends(values, rng, least, top_value):
    dims = values.shape
    index_at = [jax.random.randint(jax.random.fold_in(rng, axis), (), 0, dims[axis]) for axis in range(len(dims))]
    values = values.at[tuple(index_at)].set(least)
    longest = dims.index(max(dims))
    index_at[longest] = (index_at[longest] + 1) % dims[longest]
    return values.at[tuple(index_at)].set(top_value)


def shard_levels(stream_key, extent, pieces, smallest, top_value):
    def one(dim, parts):
        draws = jax.random.uniform(jax.random.fold_in(jax.random.fold_in(stream_key, 6), dim), (parts,), jnp.float32, smallest / len(pieces), top_value / len(pieces))
        return jnp.repeat(jnp.exp(draws), extent[dim] // parts).reshape((-1,) + (1,) * (len(extent) - dim - 1))

    level = one(*pieces[0])
    for cut in pieces[1:]:
        level = level * one(*cut)
    return level


def scatter_about(own_key, extent, scale, bound, pieces=(), kind=jnp.bfloat16):
    drawn = jax.random.normal(own_key, extent, jnp.float32) * scale
    if len(pieces) > 0:
        drawn = shard_levels(own_key, extent, pieces, -0.22, 0.18) * drawn
    return jnp.clip(drawn, min=-bound, max=bound).astype(kind)


def setup_inputs(seed: int = 0) -> dict:
    streams_of = jax.random.split(jax.random.key(seed), 8)
    return {
        "telemetry": scatter_about(streams_of[0], (STEPS, NS), 1.0, 6.0, ((0, 64), (1, 2)), jnp.float32),
        "present": place_ends((jax.random.randint(streams_of[1], (STEPS // SEG, NB), 0, 4) < 3).astype(jnp.int32), jax.random.fold_in(streams_of[1], 1), 0, 1),
        "transition": draw_transition(jax.random.fold_in(streams_of[7], 71), 0),
        "sensing": draw_sensing(jax.random.fold_in(streams_of[7], 71), 0),
        "filter_gain": draw_filter_gain(jax.random.fold_in(streams_of[7], 71), 0),
        "smooth_gain": draw_smooth_gain(jax.random.fold_in(streams_of[7], 71), 0),
        "initial_state": scatter_about(streams_of[6], (S,), 1.0, 6.0, (), jnp.float32),
    }


HIGHEST = lax.Precision.HIGHEST
RIDGE = 0.001

def solve_rows(gram, cross, ridge_term):
    factor = jnp.linalg.cholesky(gram + ridge_term * jnp.eye(gram.shape[0], dtype=jnp.float32))
    return jax.scipy.linalg.cho_solve((factor, True), cross.T).T

def reference(telemetry, present, transition, sensing, filter_gain, smooth_gain, initial_state):
    block_size = NS // NB
    step_flags = jnp.repeat(present.astype(jnp.float32), SEG, axis=0)

    def forward(carried, step_input):
        observed, flag_row = step_input
        predicted = jnp.dot(transition, carried, precision=HIGHEST)
        sensor_flags = jnp.repeat(flag_row, block_size)
        residual = sensor_flags * (observed - jnp.dot(sensing, predicted, precision=HIGHEST))
        updated = predicted + jnp.dot(filter_gain, residual, precision=HIGHEST)
        return (updated, updated)
    unused_last, filtered = lax.scan(forward, initial_state.astype(jnp.float32), (telemetry, step_flags))
    mixing = jnp.dot(smooth_gain, transition, precision=HIGHEST)
    drives = filtered - jnp.dot(filtered, mixing.T, precision=HIGHEST)

    def backward(following, drive_row):
        current = jnp.dot(smooth_gain, following, precision=HIGHEST) + drive_row
        return (current, current)
    final_state = jnp.dot(transition, filtered[-1], precision=HIGHEST)
    unused_first, smoothed = lax.scan(backward, final_state, drives, reverse=True)
    ridge_term = RIDGE * STEPS
    earlier_rows = smoothed[:-1]
    later_rows = smoothed[1:]
    lag_gram = jnp.dot(earlier_rows.T, earlier_rows, precision=HIGHEST)
    lag_cross = jnp.dot(later_rows.T, earlier_rows, precision=HIGHEST)
    new_transition = solve_rows(lag_gram, lag_cross, ridge_term)
    masked = telemetry * jnp.repeat(step_flags, block_size, axis=1)

    def block_update(block_index):
        block_flags = lax.dynamic_index_in_dim(step_flags, block_index, 1, keepdims=False)
        block_gram = jnp.dot((smoothed * block_flags[:, None]).T, smoothed, precision=HIGHEST)
        block_rows = lax.dynamic_slice_in_dim(masked, block_index * block_size, block_size, 1)
        block_cross = jnp.dot(block_rows.T, smoothed, precision=HIGHEST)
        return solve_rows(block_gram, block_cross, ridge_term)
    new_sensing = lax.map(block_update, jnp.arange(NB, dtype=jnp.int32)).reshape(NS, S)
    return (new_transition, new_sensing, smoothed)
```

```python
import functools

import jax
import jax.numpy as jnp
from jax import lax
from jax.experimental import pallas as pl
from jax.experimental.pallas import tpu as pltpu
from jax.sharding import PartitionSpec as P

RIDGE = 0.001
F32 = jnp.float32
BF16 = jnp.bfloat16
W = 128
SEGS = 16
LEN = 16
ROWS = SEGS * LEN
PACK = W + 8
VMEM_LIMIT = 56 * 1024 * 1024


def halves(value):
    high = value.astype(BF16)
    low = (value - high.astype(F32)).astype(BF16)
    return high, low


def wide(value):
    high, low = halves(value)
    return jnp.concatenate([high, low], axis=1)


def times(left_wide, right_wide):
    stacked = jnp.concatenate([right_wide, right_wide], axis=0)
    out = jnp.dot(left_wide, stacked, preferred_element_type=F32)
    return out[:, :W] + out[:, W:]


def moved(rows, dev):
    return rows + times(wide(rows), dev)


def chained(first, second, second_wide):
    return first + second + times(wide(first), second_wide)


def identity():
    rows = lax.broadcasted_iota(jnp.int32, (W, W), 0)
    cols = lax.broadcasted_iota(jnp.int32, (W, W), 1)
    return jnp.where(rows == cols, 1.0, 0.0).astype(F32)


def call(kernel, out_shapes, n_smem, n_in, scratch=()):
    smem = [pl.BlockSpec(memory_space=pltpu.SMEM)] * n_smem
    vmem = [pl.BlockSpec(memory_space=pltpu.VMEM)] * n_in
    single = not isinstance(out_shapes, (list, tuple))
    outs = [out_shapes] if single else list(out_shapes)
    out_specs = [pl.BlockSpec(memory_space=pltpu.VMEM)] * len(outs)
    return pl.pallas_call(
        kernel,
        out_shape=outs[0] if single else tuple(outs),
        in_specs=smem + vmem,
        out_specs=out_specs[0] if single else tuple(out_specs),
        scratch_shapes=list(scratch),
        compiler_params=pltpu.CompilerParams(vmem_limit_bytes=VMEM_LIMIT),
    )


def shape(*dims, dtype=F32):
    return jax.ShapeDtypeStruct(dims, dtype)


def mask_of(flags, rows, segs):
    cols = flags.shape[1] * 64
    spread = (
        lax.broadcasted_iota(jnp.int32, (flags.shape[1], cols), 0)
        == lax.broadcasted_iota(jnp.int32, (flags.shape[1], cols), 1) // 64
    )
    by_sensor = jnp.dot(flags.astype(BF16), spread.astype(BF16), preferred_element_type=F32)
    repeat = (
        lax.broadcasted_iota(jnp.int32, (rows, segs), 0) // LEN
        == lax.broadcasted_iota(jnp.int32, (rows, segs), 1)
    )
    return jnp.dot(repeat.astype(BF16), by_sensor.astype(BF16), preferred_element_type=F32)


def push_kernel(where, tel, flags, gain, mine, theirs):
    gain_t = gain[...].T
    packed = wide(gain_t)
    fl = flags[...]
    for out, core in ((theirs, 1 - where[3]), (mine, where[3])):
        start = pl.multiple_of(core * ROWS, ROWS)
        seg_start = pl.multiple_of(core * SEGS, SEGS)
        mask = mask_of(flags[pl.ds(seg_start, SEGS), :], ROWS, SEGS)
        high, low = halves(tel[pl.ds(start, ROWS), :] * mask)
        total = jnp.dot(high, packed, preferred_element_type=F32) + jnp.dot(
            low, packed, preferred_element_type=F32
        )
        out[...] = total[:, :W] + total[:, W:]


def maps_kernel(
    where, flags_own, flags_other, trans, gain_own, gain_other, sense_own, sense_other,
    powers, tree, whole, removed, single,
):
    a = trans[...]
    a_wide = wide(a)
    lane = lax.broadcasted_iota(jnp.int32, (W, 2 * W), 1) // 64
    for side, (gain, sense) in enumerate(((gain_own, sense_own), (gain_other, sense_other))):
        seen = times(wide(sense[...]), a_wide)
        seen_high, seen_low = halves(seen.T)
        gain_wide = wide(gain[...].T)
        for g in range(4):
            zero = jnp.zeros_like(seen_high)
            part = jnp.dot(
                jnp.where(lane == g, seen_high, zero), gain_wide, preferred_element_type=F32
            ) + jnp.dot(jnp.where(lane == g, seen_low, zero), gain_wide, preferred_element_type=F32)
            removed[side * 4 + g] = part[:, :W] + part[:, W:]
    base = a.T - identity()
    single[...] = base
    batch = 4

    def group(i, carry):
        devs = []
        for j in range(batch):
            k = i * batch + j
            row = where[3] * SEGS + k
            dev = single[...]
            for g in range(4):
                dev = dev - flags_own[row, g] * removed[g]
                dev = dev - flags_other[row, g] * removed[4 + g]
            devs.append(dev)
        for level in range(4):
            for j in range(batch):
                packed = wide(devs[j])
                powers[i * batch + j, level] = packed
                devs[j] = 2.0 * devs[j] + times(packed, packed)
        for j in range(batch):
            powers[i * batch + j, 4] = wide(devs[j])
            whole[i * batch + j] = devs[j]
        return carry

    lax.fori_loop(0, SEGS // batch, group, 0)
    count, base_at, source_at = SEGS, SEGS, 0
    while count > 1:
        for p in range(count // 2):
            second = whole[source_at + 2 * p + 1]
            joined = chained(whole[source_at + 2 * p], second, wide(second))
            whole[base_at + p] = joined
            tree[base_at - SEGS + p] = wide(joined)
        source_at = base_at
        count //= 2
        base_at += count


def seg_scan(rows, powers):
    row_at = lax.broadcasted_iota(jnp.int32, (ROWS, W), 0) % LEN
    for level in range(4):
        reach = 1 << level
        before = jnp.where(row_at >= reach, pltpu.roll(rows, reach, 0), 0.0)
        packed = wide(before)
        parts = [
            times(packed[k * LEN : (k + 1) * LEN], powers[k, level]) for k in range(SEGS)
        ]
        rows = rows + before + jnp.concatenate(parts, axis=0)
    return rows


def shift_kernel(mine, received, powers, tree, whole, inputs, ends, packed):
    rows = mine[...] + received[...]
    inputs[...] = rows
    reached = seg_scan(rows, powers)
    level = [reached[k * LEN + LEN - 1 : (k + 1) * LEN] for k in range(SEGS)]
    ends[0:SEGS] = jnp.concatenate(level, axis=0)
    maps = [powers[k, 4] for k in range(SEGS)]
    at, tree_at = SEGS, 0
    while len(level) > 1:
        level = [
            moved(jnp.broadcast_to(level[2 * p], (8, W)), maps[2 * p + 1])[0:1] + level[2 * p + 1]
            for p in range(len(level) // 2)
        ]
        maps = [tree[tree_at + p] for p in range(len(level))]
        tree_at += len(level)
        for p, row in enumerate(level):
            ends[at + p : at + p + 1] = row
        at += len(level)
    packed[0:W] = whole[2 * SEGS - 2]
    packed[W:PACK] = jnp.broadcast_to(level[0], (8, W))


def join2(first, second):
    second_dev = second[0:W]
    second_wide = wide(second_dev)
    dev = chained(first[0:W], second_dev, second_wide)
    row = moved(first[W:PACK], second_wide) + second[W:PACK]
    return dev, row


def pair_kernel(where, own, other, out):
    core = where[3]
    mine, theirs = own[...], other[...]
    first = jnp.where(core == 0, mine, theirs)
    second = jnp.where(core == 0, theirs, mine)
    dev, row = join2(first, second)
    out[0:W] = dev
    out[W:PACK] = row


def four_kernel(axis, where, own, r1, r2, r3, out, ordered):
    at = where[axis]
    for k, ref in enumerate((own, r1, r2, r3)):
        ordered[at ^ k] = ref[...]
    dev0, row0 = join2(ordered[0], ordered[1])
    dev1, row1 = join2(ordered[2], ordered[3])
    wide1 = wide(dev1)
    out[0:W] = chained(dev0, dev1, wide1)
    out[W:PACK] = moved(row0, wide1) + row1


def filter_kernel(
    where, y0, y1, y2, y3, z0, z1, z2, z3, x0, x1, x2, x3, c0, c1,
    initial, inputs, ends, powers, tree, gain_powers, drive_map, trans,
    drives, final, shift, ordered,
):
    state = jnp.broadcast_to(initial[...], (8, W))
    for axis, refs in ((0, (y0, y1, y2, y3)), (1, (z0, z1, z2, z3)), (2, (x0, x1, x2, x3)), (3, (c0, c1))):
        at = where[axis]
        for k, ref in enumerate(refs):
            ordered[4 * axis + (at ^ k)] = ref[...]
        for j in range(len(refs) - 1):
            slot = 4 * axis + j
            ahead = moved(state, wide(ordered[slot, 0:W])) + ordered[slot, W:PACK]
            state = jnp.where(j < at, ahead, state)
    starts = {0: state}
    for span, maps_at, ends_at in ((8, 12, 28), (4, 8, 24), (2, 0, 16), (1, -1, 0)):
        for begin in range(0, SEGS, 2 * span):
            p = begin // span
            dev = powers[p, 4] if span == 1 else tree[maps_at + p]
            starts[begin + span] = moved(starts[begin], dev) + ends[ends_at + p : ends_at + p + 1]
    entry = [moved(starts[k], powers[k, 0]) for k in range(SEGS)]
    spread = jnp.concatenate(
        [part for k in range(SEGS) for part in (entry[k], jnp.zeros((8, W), F32))], axis=0
    )
    row_at = lax.broadcasted_iota(jnp.int32, (ROWS, W), 0) % LEN
    rows = inputs[...] + jnp.where(row_at == 0, spread, 0.0)
    rows = seg_scan(rows, powers)
    drive = times(wide(rows), drive_map[...])
    drives[...] = drive
    last = jnp.broadcast_to(rows[ROWS - 1 : ROWS], (8, W))
    final_row = last + times(wide(last), wide(trans[...].T - identity()))
    final[...] = final_row
    top = (where[0] == 3) & (where[1] == 3) & (where[2] == 3) & (where[3] == 1)
    part = drive
    for level in (7, 6, 5, 4, 3):
        half = 1 << level
        part = part[:half] + moved(part[half:], gain_powers[level])
    for level in (2, 1, 0):
        half = 1 << level
        behind = pltpu.roll(part, 8 - half, 0)
        part = part + moved(behind, gain_powers[level])
    from_top = moved(final_row, gain_powers[8])
    shift[...] = jnp.broadcast_to(part[0:1], (8, W)) + jnp.where(top, from_top, 0.0)


def gain_kernel(smooth_gain, trans, gain_powers, drive_map):
    dev = smooth_gain[...].T - identity()
    adev = trans[...].T - identity()
    dev_wide = wide(dev)
    drive_map[...] = wide(-chained(adev, dev, dev_wide))
    for level in range(15):
        gain_powers[level] = dev_wide
        if level < 14:
            dev = 2.0 * dev + times(dev_wide, dev_wide)
            dev_wide = wide(dev)


def smooth_kernel(where, gathered, drives, final, gain_powers, smoothed, incoming):
    rows = gathered[...]
    bits = (
        where[3], where[2] & 1, where[2] >> 1, where[1] & 1, where[1] >> 1, where[0] & 1, where[0] >> 1
    )
    later = []
    for level in range(7):
        dist = 1 << level
        ahead = moved(rows, gain_powers[8 + level])
        later.append(rows[dist : dist + 1])
        other = pltpu.roll(rows, W - dist, 0)
        other_ahead = pltpu.roll(ahead, W - dist, 0)
        rows = jnp.where(bits[level] == 0, rows + other_ahead, other + ahead)
    state = jnp.zeros((8, W), F32)
    top = bits[0]
    for level in (6, 5, 4, 3, 2, 1, 0):
        nxt = moved(state, gain_powers[8 + level]) + later[level]
        state = jnp.where(bits[level] == 0, nxt, state)
        top = top & bits[level]
    state = jnp.where(top == 1, final[...], state)
    incoming[...] = state
    entry = moved(state, gain_powers[0])
    row_at = lax.broadcasted_iota(jnp.int32, (ROWS, W), 0)
    part = drives[...]
    part = part + jnp.where(row_at == ROWS - 1, jnp.broadcast_to(entry[0:1], (ROWS, W)), 0.0)
    for level in range(8):
        reach = 1 << level
        behind = jnp.where(row_at < ROWS - reach, pltpu.roll(part, ROWS - reach, 0), 0.0)
        part = part + moved(behind, gain_powers[level])
    smoothed[...] = part


def stats_kernel(where, tel, flags, own, other, smoothed, stats, full):
    core = where[3]
    full[pl.ds(pl.multiple_of(core * ROWS, ROWS), ROWS)] = own[0:ROWS]
    full[pl.ds(pl.multiple_of((1 - core) * ROWS, ROWS), ROWS)] = other[0:ROWS]
    rows = full[...]
    smoothed[...] = rows
    count = 2 * ROWS
    after = jnp.where(core == 1, own[ROWS : ROWS + 8], other[ROWS : ROWS + 8])
    row_at = lax.broadcasted_iota(jnp.int32, (count, W), 0)
    following = jnp.where(
        row_at == count - 1, jnp.broadcast_to(after[0:1], (count, W)), pltpu.roll(rows, count - 1, 0)
    )
    packed = wide(rows)
    packed_t = jnp.concatenate([rows.T.astype(BF16), (rows - rows.astype(BF16).astype(F32)).T.astype(BF16)], axis=0)
    last_chip = (where[0] == 3) & (where[1] == 3) & (where[2] == 3)
    lane_at = lax.broadcasted_iota(jnp.int32, (2 * W, count), 1)
    kept = jnp.where(last_chip & (lane_at == count - 1), jnp.zeros_like(packed_t), packed_t)

    def fold(out):
        return (out[:W, :W] + out[:W, W:]) + (out[W:, :W] + out[W:, W:])

    stats[0:W] = fold(jnp.dot(kept, packed, preferred_element_type=F32))
    stats[W : 2 * W] = fold(jnp.dot(kept, wide(following), preferred_element_type=F32))
    fl = flags[...]
    repeat = (
        lax.broadcasted_iota(jnp.int32, (2 * SEGS, count), 0)
        == lax.broadcasted_iota(jnp.int32, (2 * SEGS, count), 1) // LEN
    )
    lane_flags = lax.dot_general(
        fl.astype(BF16), repeat.astype(BF16), (((0,), (0,)), ((), ())), preferred_element_type=F32
    )
    for g in range(4):
        masked_t = packed_t * lane_flags[g : g + 1].astype(BF16)
        stats[(2 + g) * W : (3 + g) * W] = fold(jnp.dot(masked_t, packed, preferred_element_type=F32))
    high, low = halves(tel[...] * mask_of(fl, count, 2 * SEGS))
    cross = jnp.dot(packed_t, high, preferred_element_type=F32) + jnp.dot(
        packed_t, low, preferred_element_type=F32
    )
    cross = cross[:W] + cross[W:]
    stats[6 * W : 7 * W] = cross[:, :W]
    stats[7 * W : 8 * W] = cross[:, W:]


def solve_kernel(ridge, where, own, r1, r2, r3, new_transition, new_sensing, stats, left, right):
    at = where[2]
    for k, ref in enumerate((own, r1, r2, r3)):
        stats[at ^ k] = ref[...]
    eye = identity() * ridge
    left[0] = stats[0, 0:W] + eye
    right[0] = stats[0, W : 2 * W]
    for g in range(4):
        left[1 + g] = stats[1 + g // 2, (g % 2) * W : (g % 2 + 1) * W] + eye
        right[1 + g] = stats[3, (g // 2) * W : (g // 2 + 1) * W]
    row_at = lax.broadcasted_iota(jnp.int32, (W, W), 0)
    unit = 8

    def block(b, carry):
        base = pl.multiple_of(b * unit, unit)
        for j in range(unit):
            for p in range(5):
                lp, rp = left[p], right[p]
                lrow = left[p, pl.ds(base, unit)][j : j + 1]
                rrow = right[p, pl.ds(base, unit)][j : j + 1]
                scale = 1.0 / lrow[:, j : j + 1]
                lrow = lrow * scale
                rrow = rrow * scale
                column = jnp.broadcast_to(lp[:, j : j + 1], (W, W))
                here = row_at == base + j
                column = jnp.where(here, 0.0, column)
                left[p] = jnp.where(here, lrow, lp - column * lrow)
                right[p] = jnp.where(here, rrow, rp - column * rrow)
        for p in range(5):
            left[p] = pltpu.roll(left[p], W - unit, 1)
        return carry

    lax.fori_loop(0, W // unit, block, 0)
    new_transition[...] = right[0].T
    for g in range(4):
        new_sensing[g * 64 : (g + 1) * 64] = right[1 + g].T[(g % 2) * 64 : (g % 2 + 1) * 64]


STRIDE = {"x": 1, "z": 4, "y": 16}


def swap(value, axis, k):
    stride = STRIDE[axis]
    pairs = []
    for i in range(64):
        at = (i // stride) % 4
        pairs.append((i, i + ((at ^ k) - at) * stride))
    return lax.ppermute(value, "tm", pairs)


def swap_core(value):
    return lax.ppermute(value, "sens", [(0, 1), (1, 0)])


def three(value, axis):
    return [swap(value, axis, k) for k in (1, 2, 3)]


def piece(value, index, rows):
    return lax.dynamic_slice_in_dim(value, index * rows, rows, 0)


def scatter_sum(value, axis, at):
    rows = value.shape[0] // 4
    own = piece(value, at, rows)
    got = [swap(piece(value, at ^ k, rows), axis, k) for k in (1, 2, 3)]
    return (own + got[0]) + (got[1] + got[2])


def on_device(telemetry, present, transition, sensing, filter_gain, smooth_gain, initial_state):
    device = lax.axis_index("tm")
    core = lax.axis_index("sens")
    at_y, at_z, at_x = device // 16, (device // 4) % 4, device % 4
    where = jnp.stack([at_y, at_z, at_x, core]).astype(jnp.int32)
    flags = present.astype(F32)

    other_gain = swap_core(filter_gain)
    other_sensing = swap_core(sensing)
    other_flags = swap_core(flags)
    mine, theirs = call(push_kernel, [shape(ROWS, W)] * 2, 1, 3)(where, telemetry, flags, filter_gain)
    received = swap_core(theirs)
    powers, tree, whole = call(
        maps_kernel,
        [shape(SEGS, 5, W, 2 * W, dtype=BF16), shape(SEGS - 1, W, 2 * W, dtype=BF16), shape(2 * SEGS - 1, W, W)],
        3, 5,
        scratch=[pltpu.VMEM((8, W, W), F32), pltpu.VMEM((W, W), F32)],
    )(where, flags, other_flags, transition, filter_gain, other_gain, sensing, other_sensing)
    inputs, ends, packed = call(
        shift_kernel, [shape(ROWS, W), shape(32, W), shape(PACK, W)], 0, 5
    )(mine, received, powers, tree, whole)

    gain_powers, drive_map = call(
        gain_kernel, [shape(15, W, 2 * W, dtype=BF16), shape(W, 2 * W, dtype=BF16)], 0, 2
    )(smooth_gain, transition)

    by_core = [packed, swap_core(packed)]
    chip = call(pair_kernel, shape(PACK, W), 1, 2)(where, *by_core)
    ordered = [pltpu.VMEM((4, PACK, W), F32)]
    by_x = [chip] + three(chip, "x")
    row = call(functools.partial(four_kernel, 2), shape(PACK, W), 1, 4, ordered)(where, *by_x)
    by_z = [row] + three(row, "z")
    plane = call(functools.partial(four_kernel, 1), shape(PACK, W), 1, 4, ordered)(where, *by_z)
    by_y = [plane] + three(plane, "y")

    drives, final, shift = call(
        filter_kernel, [shape(ROWS, W), shape(8, W), shape(8, W)], 1, 14 + 8,
        [pltpu.VMEM((16, PACK, W), F32)],
    )(
        where, *by_y, *by_z, *by_x, *by_core, initial_state.reshape(1, W), inputs, ends, powers, tree,
        gain_powers, drive_map, transition,
    )
    gathered = shift[:1]
    gathered = jnp.concatenate([gathered, swap_core(gathered)], axis=0)
    for axis in ("x", "z", "y"):
        gathered = jnp.concatenate([gathered] + three(gathered, axis), axis=0)
    smoothed, incoming = call(smooth_kernel, [shape(ROWS, W), shape(8, W)], 1, 4)(
        where, gathered, drives, final, gain_powers
    )
    both = jnp.concatenate([smoothed, incoming], axis=0)
    other_both = swap_core(both)
    smoothed_out, stats = call(
        stats_kernel, [shape(2 * ROWS, W), shape(8 * W, W)], 1, 4, [pltpu.VMEM((2 * ROWS, W), F32)]
    )(where, telemetry, flags, both, other_both)

    part = scatter_sum(stats, "x", at_x)
    part = scatter_sum(part, "z", at_z)
    got = three(part, "y")
    part = (part + got[0]) + (got[1] + got[2])
    got = [part] + three(part, "z")
    stacked = jnp.stack(got)
    order = jnp.arange(4) ^ at_z
    part = jnp.concatenate([lax.dynamic_index_in_dim(stacked, at_z ^ j, 0, keepdims=False) for j in range(4)], axis=0)
    got = [part] + three(part, "x")
    ridge = RIDGE * telemetry.shape[0] * lax.axis_size("tm")
    new_transition, new_sensing = call(
        functools.partial(solve_kernel, ridge), [shape(W, W), shape(2 * W, W)], 1, 4,
        [pltpu.VMEM((4, 2 * W, W), F32), pltpu.VMEM((5, W, W), F32), pltpu.VMEM((5, W, W), F32)],
    )(where, *got)
    return new_transition, new_sensing, smoothed_out


def solution(mesh):
    placed = (P("tm", "sens"), P("tm", "sens"), P(), P("sens", None), P(None, "sens"), P(), P())
    return jax.shard_map(
        on_device,
        mesh=mesh,
        in_specs=placed,
        out_specs=(P(), P("sens", None), P("tm", None)),
        check_vma=False,
    )
```

```python
import functools

import jax
import jax.numpy as jnp
from jax import lax
from jax.experimental import pallas as pl
from jax.experimental.pallas import tpu as pltpu
from jax.sharding import PartitionSpec as P

RIDGE = 0.001
F32 = jnp.float32
BF16 = jnp.bfloat16
W = 128
SEGS = 16
LEN = 16
ROWS = SEGS * LEN
PACK = W + 8
SLAB = W // 4
CHUNK = W + SLAB + 8
VMEM_LIMIT = 56 * 1024 * 1024


def halves(value):
    high = value.astype(BF16)
    low = (value - high.astype(F32)).astype(BF16)
    return high, low


def wide(value):
    high, low = halves(value)
    return jnp.concatenate([high, low], axis=1)


def times(left_wide, right_wide):
    stacked = jnp.concatenate([right_wide, right_wide], axis=0)
    out = jnp.dot(left_wide, stacked, preferred_element_type=F32)
    return out[:, :W] + out[:, W:]


def moved(rows, dev):
    return rows + times(wide(rows), dev)


def chained(first, second, second_wide):
    return first + second + times(wide(first), second_wide)


def identity():
    rows = lax.broadcasted_iota(jnp.int32, (W, W), 0)
    cols = lax.broadcasted_iota(jnp.int32, (W, W), 1)
    return jnp.where(rows == cols, 1.0, 0.0).astype(F32)


def call(kernel, out_shapes, n_smem, n_in, scratch=()):
    smem = [pl.BlockSpec(memory_space=pltpu.SMEM)] * n_smem
    vmem = [pl.BlockSpec(memory_space=pltpu.VMEM)] * n_in
    single = not isinstance(out_shapes, (list, tuple))
    outs = [out_shapes] if single else list(out_shapes)
    out_specs = [pl.BlockSpec(memory_space=pltpu.VMEM)] * len(outs)
    return pl.pallas_call(
        kernel,
        out_shape=outs[0] if single else tuple(outs),
        in_specs=smem + vmem,
        out_specs=out_specs[0] if single else tuple(out_specs),
        scratch_shapes=list(scratch),
        compiler_params=pltpu.CompilerParams(vmem_limit_bytes=VMEM_LIMIT),
    )


def shape(*dims, dtype=F32):
    return jax.ShapeDtypeStruct(dims, dtype)


def mask_of(flags, rows, segs):
    cols = flags.shape[1] * 64
    spread = (
        lax.broadcasted_iota(jnp.int32, (flags.shape[1], cols), 0)
        == lax.broadcasted_iota(jnp.int32, (flags.shape[1], cols), 1) // 64
    )
    by_sensor = jnp.dot(flags.astype(BF16), spread.astype(BF16), preferred_element_type=F32)
    repeat = (
        lax.broadcasted_iota(jnp.int32, (rows, segs), 0) // LEN
        == lax.broadcasted_iota(jnp.int32, (rows, segs), 1)
    )
    return jnp.dot(repeat.astype(BF16), by_sensor.astype(BF16), preferred_element_type=F32)


def push_kernel(where, tel, flags, gain, mine, theirs):
    gain_t = gain[...].T
    packed = wide(gain_t)
    fl = flags[...]
    for out, core in ((theirs, 1 - where[3]), (mine, where[3])):
        start = pl.multiple_of(core * ROWS, ROWS)
        seg_start = pl.multiple_of(core * SEGS, SEGS)
        mask = mask_of(flags[pl.ds(seg_start, SEGS), :], ROWS, SEGS)
        high, low = halves(tel[pl.ds(start, ROWS), :] * mask)
        total = jnp.dot(high, packed, preferred_element_type=F32) + jnp.dot(
            low, packed, preferred_element_type=F32
        )
        out[...] = total[:, :W] + total[:, W:]


def maps_kernel(
    where, flags_own, flags_other, trans, gain_own, gain_other, sense_own, sense_other,
    powers, tree, whole, removed, single,
):
    a = trans[...]
    a_wide = wide(a)
    lane = lax.broadcasted_iota(jnp.int32, (W, 2 * W), 1) // 64
    for side, (gain, sense) in enumerate(((gain_own, sense_own), (gain_other, sense_other))):
        seen = times(wide(sense[...]), a_wide)
        seen_high, seen_low = halves(seen.T)
        gain_wide = wide(gain[...].T)
        for g in range(4):
            zero = jnp.zeros_like(seen_high)
            part = jnp.dot(
                jnp.where(lane == g, seen_high, zero), gain_wide, preferred_element_type=F32
            ) + jnp.dot(jnp.where(lane == g, seen_low, zero), gain_wide, preferred_element_type=F32)
            removed[side * 4 + g] = part[:, :W] + part[:, W:]
    base = a.T - identity()
    single[...] = base
    batch = 4

    def group(i, carry):
        devs = []
        for j in range(batch):
            k = i * batch + j
            row = where[3] * SEGS + k
            dev = single[...]
            for g in range(4):
                dev = dev - flags_own[row, g] * removed[g]
                dev = dev - flags_other[row, g] * removed[4 + g]
            devs.append(dev)
        for level in range(4):
            for j in range(batch):
                packed = wide(devs[j])
                powers[i * batch + j, level] = packed
                devs[j] = 2.0 * devs[j] + times(packed, packed)
        for j in range(batch):
            powers[i * batch + j, 4] = wide(devs[j])
            whole[i * batch + j] = devs[j]
        return carry

    lax.fori_loop(0, SEGS // batch, group, 0)
    count, base_at, source_at = SEGS, SEGS, 0
    while count > 1:
        for p in range(count // 2):
            second = whole[source_at + 2 * p + 1]
            joined = chained(whole[source_at + 2 * p], second, wide(second))
            whole[base_at + p] = joined
            tree[base_at - SEGS + p] = wide(joined)
        source_at = base_at
        count //= 2
        base_at += count


def seg_scan(rows, powers):
    row_at = lax.broadcasted_iota(jnp.int32, (ROWS, W), 0) % LEN
    for level in range(4):
        reach = 1 << level
        before = jnp.where(row_at >= reach, pltpu.roll(rows, reach, 0), 0.0)
        packed = wide(before)
        parts = [
            times(packed[k * LEN : (k + 1) * LEN], powers[k, level]) for k in range(SEGS)
        ]
        rows = rows + before + jnp.concatenate(parts, axis=0)
    return rows


def shift_kernel(mine, received, powers, tree, whole, inputs, ends, packed):
    rows = mine[...] + received[...]
    inputs[...] = rows
    reached = seg_scan(rows, powers)
    level = [reached[k * LEN + LEN - 1 : (k + 1) * LEN] for k in range(SEGS)]
    ends[0:SEGS] = jnp.concatenate(level, axis=0)
    maps = [powers[k, 4] for k in range(SEGS)]
    at, tree_at = SEGS, 0
    while len(level) > 1:
        level = [
            moved(jnp.broadcast_to(level[2 * p], (8, W)), maps[2 * p + 1])[0:1] + level[2 * p + 1]
            for p in range(len(level) // 2)
        ]
        maps = [tree[tree_at + p] for p in range(len(level))]
        tree_at += len(level)
        for p, row in enumerate(level):
            ends[at + p : at + p + 1] = row
        at += len(level)
    packed[0:W] = whole[2 * SEGS - 2]
    packed[W:PACK] = jnp.broadcast_to(level[0], (8, W))


def join2(first, second):
    second_dev = second[0:W]
    second_wide = wide(second_dev)
    dev = chained(first[0:W], second_dev, second_wide)
    row = moved(first[W:PACK], second_wide) + second[W:PACK]
    return dev, row


def pair_kernel(where, own, other, out):
    core = where[3]
    mine, theirs = own[...], other[...]
    first = jnp.where(core == 0, mine, theirs)
    second = jnp.where(core == 0, theirs, mine)
    dev, row = join2(first, second)
    out[0:W] = dev
    out[W:PACK] = row


def four_kernel(axis, where, own, r1, r2, r3, out, ordered):
    at = where[axis]
    for k, ref in enumerate((own, r1, r2, r3)):
        ordered[at ^ k] = ref[...]
    dev0, row0 = join2(ordered[0], ordered[1])
    dev1, row1 = join2(ordered[2], ordered[3])
    wide1 = wide(dev1)
    out[0:W] = chained(dev0, dev1, wide1)
    out[W:PACK] = moved(row0, wide1) + row1


def filter_kernel(
    where, y0, y1, y2, y3, z0, z1, z2, z3, x0, x1, x2, x3, c0, c1,
    initial, inputs, ends, powers, tree, gain_powers, drive_map, trans,
    drives, final, shift, ordered,
):
    state = jnp.broadcast_to(initial[...], (8, W))
    for axis, refs in ((0, (y0, y1, y2, y3)), (1, (z0, z1, z2, z3)), (2, (x0, x1, x2, x3)), (3, (c0, c1))):
        at = where[axis]
        for k, ref in enumerate(refs):
            ordered[4 * axis + (at ^ k)] = ref[...]
        for j in range(len(refs) - 1):
            slot = 4 * axis + j
            ahead = moved(state, wide(ordered[slot, 0:W])) + ordered[slot, W:PACK]
            state = jnp.where(j < at, ahead, state)
    starts = {0: state}
    for span, maps_at, ends_at in ((8, 12, 28), (4, 8, 24), (2, 0, 16), (1, -1, 0)):
        for begin in range(0, SEGS, 2 * span):
            p = begin // span
            dev = powers[p, 4] if span == 1 else tree[maps_at + p]
            starts[begin + span] = moved(starts[begin], dev) + ends[ends_at + p : ends_at + p + 1]
    entry = [moved(starts[k], powers[k, 0]) for k in range(SEGS)]
    spread = jnp.concatenate(
        [part for k in range(SEGS) for part in (entry[k], jnp.zeros((8, W), F32))], axis=0
    )
    row_at = lax.broadcasted_iota(jnp.int32, (ROWS, W), 0) % LEN
    rows = inputs[...] + jnp.where(row_at == 0, spread, 0.0)
    rows = seg_scan(rows, powers)
    drive = times(wide(rows), drive_map[...])
    drives[...] = drive
    last = jnp.broadcast_to(rows[ROWS - 1 : ROWS], (8, W))
    final_row = last + times(wide(last), wide(trans[...].T - identity()))
    final[...] = final_row
    top = (where[0] == 3) & (where[1] == 3) & (where[2] == 3) & (where[3] == 1)
    part = drive
    for level in (7, 6, 5, 4, 3):
        half = 1 << level
        part = part[:half] + moved(part[half:], gain_powers[level])
    for level in (2, 1, 0):
        half = 1 << level
        behind = pltpu.roll(part, 8 - half, 0)
        part = part + moved(behind, gain_powers[level])
    from_top = moved(final_row, gain_powers[8])
    shift[...] = jnp.broadcast_to(part[0:1], (8, W)) + jnp.where(top, from_top, 0.0)


def gain_kernel(smooth_gain, trans, gain_powers, drive_map):
    dev = smooth_gain[...].T - identity()
    adev = trans[...].T - identity()
    dev_wide = wide(dev)
    drive_map[...] = wide(-chained(adev, dev, dev_wide))
    for level in range(15):
        gain_powers[level] = dev_wide
        if level < 14:
            dev = 2.0 * dev + times(dev_wide, dev_wide)
            dev_wide = wide(dev)


def smooth_kernel(where, gathered, drives, final, gain_powers, smoothed, incoming):
    rows = gathered[...]
    bits = (
        where[3], where[2] & 1, where[2] >> 1, where[1] & 1, where[1] >> 1, where[0] & 1, where[0] >> 1
    )
    later = []
    for level in range(7):
        dist = 1 << level
        ahead = moved(rows, gain_powers[8 + level])
        later.append(rows[dist : dist + 1])
        other = pltpu.roll(rows, W - dist, 0)
        other_ahead = pltpu.roll(ahead, W - dist, 0)
        rows = jnp.where(bits[level] == 0, rows + other_ahead, other + ahead)
    state = jnp.zeros((8, W), F32)
    top = bits[0]
    for level in (6, 5, 4, 3, 2, 1, 0):
        nxt = moved(state, gain_powers[8 + level]) + later[level]
        state = jnp.where(bits[level] == 0, nxt, state)
        top = top & bits[level]
    state = jnp.where(top == 1, final[...], state)
    incoming[...] = state
    entry = moved(state, gain_powers[0])
    row_at = lax.broadcasted_iota(jnp.int32, (ROWS, W), 0)
    part = drives[...]
    part = part + jnp.where(row_at == ROWS - 1, jnp.broadcast_to(entry[0:1], (ROWS, W)), 0.0)
    for level in range(8):
        reach = 1 << level
        behind = jnp.where(row_at < ROWS - reach, pltpu.roll(part, ROWS - reach, 0), 0.0)
        part = part + moved(behind, gain_powers[level])
    smoothed[...] = part


def stats_kernel(where, tel, flags, own, other, smoothed, out0, out1, out2, out3, full, parts):
    core = where[3]
    full[pl.ds(pl.multiple_of(core * ROWS, ROWS), ROWS)] = own[0:ROWS]
    full[pl.ds(pl.multiple_of((1 - core) * ROWS, ROWS), ROWS)] = other[0:ROWS]
    rows = full[...]
    smoothed[...] = rows
    count = 2 * ROWS
    after = jnp.where(core == 1, own[ROWS : ROWS + 8], other[ROWS : ROWS + 8])
    row_at = lax.broadcasted_iota(jnp.int32, (count, W), 0)
    following = jnp.where(
        row_at == count - 1, jnp.broadcast_to(after[0:1], (count, W)), pltpu.roll(rows, count - 1, 0)
    )
    packed = wide(rows)
    packed_t = jnp.concatenate([rows.T.astype(BF16), (rows - rows.astype(BF16).astype(F32)).T.astype(BF16)], axis=0)
    last_chip = (where[0] == 3) & (where[1] == 3) & (where[2] == 3)
    lane_at = lax.broadcasted_iota(jnp.int32, (2 * W, count), 1)
    kept = jnp.where(last_chip & (lane_at == count - 1), jnp.zeros_like(packed_t), packed_t)

    def fold(out):
        return (out[:W, :W] + out[:W, W:]) + (out[W:, :W] + out[W:, W:])

    upper = lax.broadcasted_iota(jnp.int32, (W, W), 0) - lax.broadcasted_iota(jnp.int32, (W, W), 1)
    lag_gram = fold(jnp.dot(kept, packed, preferred_element_type=F32))
    lag_cross_t = fold(jnp.dot(kept, wide(following), preferred_element_type=F32))
    lag = jnp.where(jnp.logical_and(upper <= 0, core == 0), lag_gram, lag_cross_t)
    for j in range(4):
        parts[j, W : W + SLAB] = lag[j * SLAB : (j + 1) * SLAB]
        parts[j, W + SLAB :] = jnp.zeros((8, W), F32)
    fl = flags[...]
    repeat = (
        lax.broadcasted_iota(jnp.int32, (2 * SEGS, count), 0)
        == lax.broadcasted_iota(jnp.int32, (2 * SEGS, count), 1) // LEN
    )
    lane_flags = lax.dot_general(
        fl.astype(BF16), repeat.astype(BF16), (((0,), (0,)), ((), ())), preferred_element_type=F32
    )
    grams = []
    for g in range(4):
        masked_t = packed_t * lane_flags[g : g + 1].astype(BF16)
        grams.append(fold(jnp.dot(masked_t, packed, preferred_element_type=F32)))
    for tile in range(2):
        parts[tile, 0:W] = jnp.where(upper <= 0, grams[2 * tile], grams[2 * tile + 1])
        parts[0, W + SLAB + tile : W + SLAB + tile + 1] = jnp.sum(
            jnp.where(upper == 0, grams[2 * tile + 1], 0.0), axis=0, keepdims=True
        )
    high, low = halves(tel[...] * mask_of(fl, count, 2 * SEGS))
    cross = jnp.dot(packed_t, high, preferred_element_type=F32) + jnp.dot(
        packed_t, low, preferred_element_type=F32
    )
    cross = cross[:W] + cross[W:]
    parts[2, 0:W] = cross[:, :W]
    parts[3, 0:W] = cross[:, W:]
    for k, out in enumerate((out0, out1, out2, out3)):
        out[...] = parts[where[2] ^ k]


def inverses(matrices):
    unit = 8
    lane = lax.broadcasted_iota(jnp.int32, (W, W), 1)
    lane_head = lane[:unit]
    row_head = lax.broadcasted_iota(jnp.int32, (unit, W), 0)

    def block(b, held):
        heads = [m[:unit] for m in held]
        rests = [m[unit:] for m in held]
        for j in range(unit):
            for p in range(len(held)):
                head, rest = heads[p], rests[p]
                row = head[j : j + 1]
                scale = 1.0 / row[:, j : j + 1]
                row = jnp.where(lane_head[:1] == j, scale, row * scale)
                head_next = jnp.where(lane_head == j, 0.0, head) - head[:, j : j + 1] * row
                heads[p] = jnp.where(row_head == j, row, head_next)
                rests[p] = jnp.where(lane[unit:] == j, 0.0, rest) - rest[:, j : j + 1] * row
        return tuple(
            pltpu.roll(jnp.concatenate([rest, head], axis=0), W - unit, 1)
            for head, rest in zip(heads, rests)
        )

    return lax.fori_loop(0, W // unit, block, tuple(matrices))


def exact(left, right):
    return jnp.dot(left, right, precision=lax.Precision.HIGHEST, preferred_element_type=F32)


def solve_kernel(ridge, where, own, r1, r2, r3, new_transition, new_sensing, parts):
    at = where[2]
    core = where[3]
    for k, ref in enumerate((own, r1, r2, r3)):
        parts[at ^ k] = ref[...]
    rows = lax.broadcasted_iota(jnp.int32, (W, W), 0)
    lanes = lax.broadcasted_iota(jnp.int32, (W, W), 1)
    eye = jnp.where(rows == lanes, ridge, 0.0).astype(F32)
    slabs = [parts[j, W : W + SLAB] for j in range(4)]
    far = [parts[j, W + SLAB + 8 :] for j in range(4)]
    lag_here = jnp.concatenate(slabs, axis=0)
    lag_far = jnp.concatenate(far, axis=0)
    lag_a = jnp.where(core == 0, lag_here, lag_far)
    lag_b = jnp.where(core == 0, lag_far, lag_here)

    def upper(tile):
        return jnp.where(rows <= lanes, tile, 0.0) + jnp.where(rows < lanes, tile, 0.0).T

    def lower(tile, diagonal):
        below = jnp.where(rows > lanes, tile, 0.0)
        return below + below.T + jnp.where(rows == lanes, diagonal, 0.0)

    grams = [upper(lag_a)]
    for tile in range(2):
        grams.append(upper(parts[tile, 0:W]))
        grams.append(lower(parts[tile, 0:W], parts[0, W + SLAB + tile : W + SLAB + tile + 1]))
    done = inverses([gram + eye for gram in grams])
    lag_cross_t = jnp.where(rows > lanes, lag_a, lag_b)
    new_transition[...] = exact(lag_cross_t.T, done[0])
    for tile in range(2):
        cross = parts[2 + tile, 0:W].T
        for half in range(2):
            g = 2 * tile + half
            new_sensing[g * 64 : (g + 1) * 64] = exact(cross[half * 64 : (half + 1) * 64], done[1 + g])


STRIDE = {"x": 1, "z": 4, "y": 16}


def swap(value, axis, k):
    stride = STRIDE[axis]
    pairs = []
    for i in range(64):
        at = (i // stride) % 4
        pairs.append((i, i + ((at ^ k) - at) * stride))
    return lax.ppermute(value, "tm", pairs)


def swap_core(value):
    return lax.ppermute(value, "sens", [(0, 1), (1, 0)])


def three(value, axis):
    return [swap(value, axis, k) for k in (1, 2, 3)]


def on_device(telemetry, present, transition, sensing, filter_gain, smooth_gain, initial_state):
    device = lax.axis_index("tm")
    core = lax.axis_index("sens")
    at_y, at_z, at_x = device // 16, (device // 4) % 4, device % 4
    where = jnp.stack([at_y, at_z, at_x, core]).astype(jnp.int32)
    flags = present.astype(F32)

    other_gain = swap_core(filter_gain)
    other_sensing = swap_core(sensing)
    other_flags = swap_core(flags)
    mine, theirs = call(push_kernel, [shape(ROWS, W)] * 2, 1, 3)(where, telemetry, flags, filter_gain)
    received = swap_core(theirs)
    powers, tree, whole = call(
        maps_kernel,
        [shape(SEGS, 5, W, 2 * W, dtype=BF16), shape(SEGS - 1, W, 2 * W, dtype=BF16), shape(2 * SEGS - 1, W, W)],
        3, 5,
        scratch=[pltpu.VMEM((8, W, W), F32), pltpu.VMEM((W, W), F32)],
    )(where, flags, other_flags, transition, filter_gain, other_gain, sensing, other_sensing)
    inputs, ends, packed = call(
        shift_kernel, [shape(ROWS, W), shape(32, W), shape(PACK, W)], 0, 5
    )(mine, received, powers, tree, whole)

    gain_powers, drive_map = call(
        gain_kernel, [shape(15, W, 2 * W, dtype=BF16), shape(W, 2 * W, dtype=BF16)], 0, 2
    )(smooth_gain, transition)

    by_core = [packed, swap_core(packed)]
    chip = call(pair_kernel, shape(PACK, W), 1, 2)(where, *by_core)
    ordered = [pltpu.VMEM((4, PACK, W), F32)]
    by_x = [chip] + three(chip, "x")
    row = call(functools.partial(four_kernel, 2), shape(PACK, W), 1, 4, ordered)(where, *by_x)
    by_z = [row] + three(row, "z")
    plane = call(functools.partial(four_kernel, 1), shape(PACK, W), 1, 4, ordered)(where, *by_z)
    by_y = [plane] + three(plane, "y")

    drives, final, shift = call(
        filter_kernel, [shape(ROWS, W), shape(8, W), shape(8, W)], 1, 14 + 8,
        [pltpu.VMEM((16, PACK, W), F32)],
    )(
        where, *by_y, *by_z, *by_x, *by_core, initial_state.reshape(1, W), inputs, ends, powers, tree,
        gain_powers, drive_map, transition,
    )
    gathered = shift[:1]
    gathered = jnp.concatenate([gathered, swap_core(gathered)], axis=0)
    for axis in ("x", "z", "y"):
        gathered = jnp.concatenate([gathered] + three(gathered, axis), axis=0)
    smoothed, incoming = call(smooth_kernel, [shape(ROWS, W), shape(8, W)], 1, 4)(
        where, gathered, drives, final, gain_powers
    )
    both = jnp.concatenate([smoothed, incoming], axis=0)
    other_both = swap_core(both)
    smoothed_out, *chunks = call(
        stats_kernel, [shape(2 * ROWS, W)] + [shape(CHUNK, W)] * 4, 1, 4,
        [pltpu.VMEM((2 * ROWS, W), F32), pltpu.VMEM((4, CHUNK, W), F32)],
    )(where, telemetry, flags, both, other_both)

    got = [swap(chunks[k], "x", k) for k in (1, 2, 3)]
    part = (chunks[0] + got[0]) + (got[1] + got[2])
    for axis in ("z", "y"):
        got = three(part, axis)
        part = (part + got[0]) + (got[1] + got[2])
    part = jnp.concatenate([part, swap_core(part[W : W + SLAB])], axis=0)
    ridge = RIDGE * telemetry.shape[0] * lax.axis_size("tm")
    new_transition, new_sensing = call(
        functools.partial(solve_kernel, ridge), [shape(W, W), shape(2 * W, W)], 1, 4,
        [pltpu.VMEM((4, CHUNK + SLAB, W), F32)],
    )(where, part, *three(part, "x"))
    return new_transition, new_sensing, smoothed_out


def solution(mesh):
    placed = (P("tm", "sens"), P("tm", "sens"), P(), P("sens", None), P(None, "sens"), P(), P())
    return jax.shard_map(
        on_device,
        mesh=mesh,
        in_specs=placed,
        out_specs=(P(), P("sens", None), P("tm", None)),
        check_vma=False,
    )
```

```python
import functools

import jax
import jax.numpy as jnp
from jax import lax
from jax.experimental import pallas as pl
from jax.experimental.pallas import tpu as pltpu
from jax.sharding import PartitionSpec as P

RIDGE = 0.001
F32 = jnp.float32
BF16 = jnp.bfloat16
W = 128
SEGS = 16
LEN = 16
ROWS = SEGS * LEN
PACK = W + 8
SLAB = W // 4
CHUNK = W + SLAB + 8
VMEM_LIMIT = 24 * 1024 * 1024


def halves(value):
    high = value.astype(BF16)
    low = (value - high.astype(F32)).astype(BF16)
    return high, low


def wide(value):
    high, low = halves(value)
    return jnp.concatenate([high, low], axis=1)


def times(left_wide, right_wide):
    stacked = jnp.concatenate([right_wide, right_wide], axis=0)
    out = jnp.dot(left_wide, stacked, preferred_element_type=F32)
    return out[:, :W] + out[:, W:]


def moved(rows, dev):
    return rows + times(wide(rows), dev)


def chained(first, second, second_wide):
    return first + second + times(wide(first), second_wide)


def identity():
    rows = lax.broadcasted_iota(jnp.int32, (W, W), 0)
    cols = lax.broadcasted_iota(jnp.int32, (W, W), 1)
    return jnp.where(rows == cols, 1.0, 0.0).astype(F32)


def call(kernel, out_shapes, n_smem, n_in, scratch=()):
    smem = [pl.BlockSpec(memory_space=pltpu.SMEM)] * n_smem
    vmem = [pl.BlockSpec(memory_space=pltpu.VMEM)] * n_in
    outs = [out if leaves else pltpu.VMEM(out.shape, out.dtype) for out, leaves in out_shapes]
    run = pl.pallas_call(
        kernel,
        out_shape=tuple(outs),
        in_specs=smem + vmem,
        out_specs=tuple([pl.BlockSpec(memory_space=pltpu.VMEM)] * len(outs)),
        scratch_shapes=list(scratch),
        compiler_params=pltpu.CompilerParams(vmem_limit_bytes=VMEM_LIMIT),
    )

    def placed(*operands):
        near = [pltpu.with_memory_space_constraint(v, pltpu.VMEM) for v in operands[n_smem:]]
        return run(*operands[:n_smem], *near)

    return placed


def shape(*dims, dtype=F32, leaves=False):
    return jax.ShapeDtypeStruct(dims, dtype), leaves


def mask_of(flags, rows, segs):
    cols = flags.shape[1] * 64
    spread = (
        lax.broadcasted_iota(jnp.int32, (flags.shape[1], cols), 0)
        == lax.broadcasted_iota(jnp.int32, (flags.shape[1], cols), 1) // 64
    )
    by_sensor = jnp.dot(flags.astype(BF16), spread.astype(BF16), preferred_element_type=F32)
    repeat = (
        lax.broadcasted_iota(jnp.int32, (rows, segs), 0) // LEN
        == lax.broadcasted_iota(jnp.int32, (rows, segs), 1)
    )
    return jnp.dot(repeat.astype(BF16), by_sensor.astype(BF16), preferred_element_type=F32)


def push_kernel(where, tel, flags, gain, mine, theirs):
    gain_t = gain[...].T
    packed = wide(gain_t)
    fl = flags[...]
    for out, core in ((theirs, 1 - where[3]), (mine, where[3])):
        start = pl.multiple_of(core * ROWS, ROWS)
        seg_start = pl.multiple_of(core * SEGS, SEGS)
        mask = mask_of(flags[pl.ds(seg_start, SEGS), :], ROWS, SEGS)
        high, low = halves(tel[pl.ds(start, ROWS), :] * mask)
        total = jnp.dot(high, packed, preferred_element_type=F32) + jnp.dot(
            low, packed, preferred_element_type=F32
        )
        out[...] = total[:, :W] + total[:, W:]


def maps_kernel(
    where, flags_own, flags_other, trans, gain_own, gain_other, sense_own, sense_other,
    powers, tree, whole, removed, single,
):
    a = trans[...]
    a_wide = wide(a)
    lane = lax.broadcasted_iota(jnp.int32, (W, 2 * W), 1) // 64
    for side, (gain, sense) in enumerate(((gain_own, sense_own), (gain_other, sense_other))):
        seen = times(wide(sense[...]), a_wide)
        seen_high, seen_low = halves(seen.T)
        gain_wide = wide(gain[...].T)
        for g in range(4):
            zero = jnp.zeros_like(seen_high)
            part = jnp.dot(
                jnp.where(lane == g, seen_high, zero), gain_wide, preferred_element_type=F32
            ) + jnp.dot(jnp.where(lane == g, seen_low, zero), gain_wide, preferred_element_type=F32)
            removed[side * 4 + g] = part[:, :W] + part[:, W:]
    base = a.T - identity()
    single[...] = base
    batch = 4

    def group(i, carry):
        devs = []
        for j in range(batch):
            k = i * batch + j
            row = where[3] * SEGS + k
            dev = single[...]
            for g in range(4):
                dev = dev - flags_own[row, g] * removed[g]
                dev = dev - flags_other[row, g] * removed[4 + g]
            devs.append(dev)
        for level in range(4):
            for j in range(batch):
                packed = wide(devs[j])
                powers[i * batch + j, level] = packed
                devs[j] = 2.0 * devs[j] + times(packed, packed)
        for j in range(batch):
            powers[i * batch + j, 4] = wide(devs[j])
            whole[i * batch + j] = devs[j]
        return carry

    lax.fori_loop(0, SEGS // batch, group, 0)
    count, base_at, source_at = SEGS, SEGS, 0
    while count > 1:
        for p in range(count // 2):
            second = whole[source_at + 2 * p + 1]
            joined = chained(whole[source_at + 2 * p], second, wide(second))
            whole[base_at + p] = joined
            tree[base_at - SEGS + p] = wide(joined)
        source_at = base_at
        count //= 2
        base_at += count


def seg_scan(rows, powers):
    row_at = lax.broadcasted_iota(jnp.int32, (ROWS, W), 0) % LEN
    for level in range(4):
        reach = 1 << level
        before = jnp.where(row_at >= reach, pltpu.roll(rows, reach, 0), 0.0)
        packed = wide(before)
        parts = [
            times(packed[k * LEN : (k + 1) * LEN], powers[k, level]) for k in range(SEGS)
        ]
        rows = rows + before + jnp.concatenate(parts, axis=0)
    return rows


def shift_kernel(mine, received, powers, tree, whole, inputs, ends, packed):
    rows = mine[...] + received[...]
    inputs[...] = rows
    reached = seg_scan(rows, powers)
    level = [reached[k * LEN + LEN - 1 : (k + 1) * LEN] for k in range(SEGS)]
    ends[0:SEGS] = jnp.concatenate(level, axis=0)
    maps = [powers[k, 4] for k in range(SEGS)]
    at, tree_at = SEGS, 0
    while len(level) > 1:
        level = [
            moved(jnp.broadcast_to(level[2 * p], (8, W)), maps[2 * p + 1])[0:1] + level[2 * p + 1]
            for p in range(len(level) // 2)
        ]
        maps = [tree[tree_at + p] for p in range(len(level))]
        tree_at += len(level)
        for p, row in enumerate(level):
            ends[at + p : at + p + 1] = row
        at += len(level)
    packed[0:W] = whole[2 * SEGS - 2]
    packed[W:PACK] = jnp.broadcast_to(level[0], (8, W))


def join2(first, second):
    second_dev = second[0:W]
    second_wide = wide(second_dev)
    dev = chained(first[0:W], second_dev, second_wide)
    row = moved(first[W:PACK], second_wide) + second[W:PACK]
    return dev, row


def pair_kernel(where, own, other, out):
    core = where[3]
    mine, theirs = own[...], other[...]
    first = jnp.where(core == 0, mine, theirs)
    second = jnp.where(core == 0, theirs, mine)
    dev, row = join2(first, second)
    out[0:W] = dev
    out[W:PACK] = row


def four_kernel(axis, where, own, r1, r2, r3, out, ordered):
    at = where[axis]
    for k, ref in enumerate((own, r1, r2, r3)):
        ordered[at ^ k] = ref[...]
    dev0, row0 = join2(ordered[0], ordered[1])
    dev1, row1 = join2(ordered[2], ordered[3])
    wide1 = wide(dev1)
    out[0:W] = chained(dev0, dev1, wide1)
    out[W:PACK] = moved(row0, wide1) + row1


def filter_kernel(
    where, y0, y1, y2, y3, z0, z1, z2, z3, x0, x1, x2, x3, c0, c1,
    initial, inputs, ends, powers, tree, gain_powers, drive_map, trans,
    drives, final, shift, ordered,
):
    state = jnp.broadcast_to(initial[...], (8, W))
    for axis, refs in ((0, (y0, y1, y2, y3)), (1, (z0, z1, z2, z3)), (2, (x0, x1, x2, x3)), (3, (c0, c1))):
        at = where[axis]
        for k, ref in enumerate(refs):
            ordered[4 * axis + (at ^ k)] = ref[...]
        for j in range(len(refs) - 1):
            slot = 4 * axis + j
            ahead = moved(state, wide(ordered[slot, 0:W])) + ordered[slot, W:PACK]
            state = jnp.where(j < at, ahead, state)
    starts = {0: state}
    for span, maps_at, ends_at in ((8, 12, 28), (4, 8, 24), (2, 0, 16), (1, -1, 0)):
        for begin in range(0, SEGS, 2 * span):
            p = begin // span
            dev = powers[p, 4] if span == 1 else tree[maps_at + p]
            starts[begin + span] = moved(starts[begin], dev) + ends[ends_at + p : ends_at + p + 1]
    entry = [moved(starts[k], powers[k, 0]) for k in range(SEGS)]
    spread = jnp.concatenate(
        [part for k in range(SEGS) for part in (entry[k], jnp.zeros((8, W), F32))], axis=0
    )
    row_at = lax.broadcasted_iota(jnp.int32, (ROWS, W), 0) % LEN
    rows = inputs[...] + jnp.where(row_at == 0, spread, 0.0)
    rows = seg_scan(rows, powers)
    drive = times(wide(rows), drive_map[...])
    drives[...] = drive
    last = jnp.broadcast_to(rows[ROWS - 1 : ROWS], (8, W))
    final_row = last + times(wide(last), wide(trans[...].T - identity()))
    final[...] = final_row
    top = (where[0] == 3) & (where[1] == 3) & (where[2] == 3) & (where[3] == 1)
    part = drive
    for level in (7, 6, 5, 4, 3):
        half = 1 << level
        part = part[:half] + moved(part[half:], gain_powers[level])
    for level in (2, 1, 0):
        half = 1 << level
        behind = pltpu.roll(part, 8 - half, 0)
        part = part + moved(behind, gain_powers[level])
    from_top = moved(final_row, gain_powers[8])
    shift[...] = jnp.broadcast_to(part[0:1], (8, W)) + jnp.where(top, from_top, 0.0)


def gain_kernel(smooth_gain, trans, gain_powers, drive_map):
    dev = smooth_gain[...].T - identity()
    adev = trans[...].T - identity()
    dev_wide = wide(dev)
    drive_map[...] = wide(-chained(adev, dev, dev_wide))
    for level in range(15):
        gain_powers[level] = dev_wide
        if level < 14:
            dev = 2.0 * dev + times(dev_wide, dev_wide)
            dev_wide = wide(dev)


def smooth_kernel(where, gathered, drives, final, gain_powers, smoothed, incoming):
    rows = gathered[...]
    bits = (
        where[3], where[2] & 1, where[2] >> 1, where[1] & 1, where[1] >> 1, where[0] & 1, where[0] >> 1
    )
    later = []
    for level in range(7):
        dist = 1 << level
        ahead = moved(rows, gain_powers[8 + level])
        later.append(rows[dist : dist + 1])
        other = pltpu.roll(rows, W - dist, 0)
        other_ahead = pltpu.roll(ahead, W - dist, 0)
        rows = jnp.where(bits[level] == 0, rows + other_ahead, other + ahead)
    state = jnp.zeros((8, W), F32)
    top = bits[0]
    for level in (6, 5, 4, 3, 2, 1, 0):
        nxt = moved(state, gain_powers[8 + level]) + later[level]
        state = jnp.where(bits[level] == 0, nxt, state)
        top = top & bits[level]
    state = jnp.where(top == 1, final[...], state)
    incoming[...] = state
    entry = moved(state, gain_powers[0])
    row_at = lax.broadcasted_iota(jnp.int32, (ROWS, W), 0)
    part = drives[...]
    part = part + jnp.where(row_at == ROWS - 1, jnp.broadcast_to(entry[0:1], (ROWS, W)), 0.0)
    for level in range(8):
        reach = 1 << level
        behind = jnp.where(row_at < ROWS - reach, pltpu.roll(part, ROWS - reach, 0), 0.0)
        part = part + moved(behind, gain_powers[level])
    smoothed[...] = part


def stats_kernel(where, tel, flags, own, other, smoothed, out0, out1, out2, out3, full, parts):
    core = where[3]
    full[pl.ds(pl.multiple_of(core * ROWS, ROWS), ROWS)] = own[0:ROWS]
    full[pl.ds(pl.multiple_of((1 - core) * ROWS, ROWS), ROWS)] = other[0:ROWS]
    rows = full[...]
    smoothed[...] = rows
    count = 2 * ROWS
    after = jnp.where(core == 1, own[ROWS : ROWS + 8], other[ROWS : ROWS + 8])
    row_at = lax.broadcasted_iota(jnp.int32, (count, W), 0)
    following = jnp.where(
        row_at == count - 1, jnp.broadcast_to(after[0:1], (count, W)), pltpu.roll(rows, count - 1, 0)
    )
    packed = wide(rows)
    packed_t = jnp.concatenate([rows.T.astype(BF16), (rows - rows.astype(BF16).astype(F32)).T.astype(BF16)], axis=0)
    last_chip = (where[0] == 3) & (where[1] == 3) & (where[2] == 3)
    lane_at = lax.broadcasted_iota(jnp.int32, (2 * W, count), 1)
    kept = jnp.where(last_chip & (lane_at == count - 1), jnp.zeros_like(packed_t), packed_t)

    def fold(out):
        return (out[:W, :W] + out[:W, W:]) + (out[W:, :W] + out[W:, W:])

    upper = lax.broadcasted_iota(jnp.int32, (W, W), 0) - lax.broadcasted_iota(jnp.int32, (W, W), 1)
    lag_gram = fold(jnp.dot(kept, packed, preferred_element_type=F32))
    lag_cross_t = fold(jnp.dot(kept, wide(following), preferred_element_type=F32))
    lag = jnp.where(jnp.logical_and(upper <= 0, core == 0), lag_gram, lag_cross_t)
    for j in range(4):
        parts[j, W : W + SLAB] = lag[j * SLAB : (j + 1) * SLAB]
        parts[j, W + SLAB :] = jnp.zeros((8, W), F32)
    fl = flags[...]
    repeat = (
        lax.broadcasted_iota(jnp.int32, (2 * SEGS, count), 0)
        == lax.broadcasted_iota(jnp.int32, (2 * SEGS, count), 1) // LEN
    )
    lane_flags = lax.dot_general(
        fl.astype(BF16), repeat.astype(BF16), (((0,), (0,)), ((), ())), preferred_element_type=F32
    )
    grams = []
    for g in range(4):
        masked_t = packed_t * lane_flags[g : g + 1].astype(BF16)
        grams.append(fold(jnp.dot(masked_t, packed, preferred_element_type=F32)))
    for tile in range(2):
        parts[tile, 0:W] = jnp.where(upper <= 0, grams[2 * tile], grams[2 * tile + 1])
        parts[0, W + SLAB + tile : W + SLAB + tile + 1] = jnp.sum(
            jnp.where(upper == 0, grams[2 * tile + 1], 0.0), axis=0, keepdims=True
        )
    high, low = halves(tel[...] * mask_of(fl, count, 2 * SEGS))
    cross = jnp.dot(packed_t, high, preferred_element_type=F32) + jnp.dot(
        packed_t, low, preferred_element_type=F32
    )
    cross = cross[:W] + cross[W:]
    parts[2, 0:W] = cross[:, :W]
    parts[3, 0:W] = cross[:, W:]
    for k, out in enumerate((out0, out1, out2, out3)):
        out[...] = parts[where[2] ^ k]


def inverses(matrices):
    unit = 8
    lane = lax.broadcasted_iota(jnp.int32, (W, W), 1)
    lane_head = lane[:unit]
    row_head = lax.broadcasted_iota(jnp.int32, (unit, W), 0)

    def block(b, held):
        heads = [m[:unit] for m in held]
        rests = [m[unit:] for m in held]
        for j in range(unit):
            for p in range(len(held)):
                head, rest = heads[p], rests[p]
                row = head[j : j + 1]
                scale = 1.0 / row[:, j : j + 1]
                row = jnp.where(lane_head[:1] == j, scale, row * scale)
                head_next = jnp.where(lane_head == j, 0.0, head) - head[:, j : j + 1] * row
                heads[p] = jnp.where(row_head == j, row, head_next)
                rests[p] = jnp.where(lane[unit:] == j, 0.0, rest) - rest[:, j : j + 1] * row
        return tuple(
            pltpu.roll(jnp.concatenate([rest, head], axis=0), W - unit, 1)
            for head, rest in zip(heads, rests)
        )

    return lax.fori_loop(0, W // unit, block, tuple(matrices))


def exact(left, right):
    return jnp.dot(left, right, precision=lax.Precision.HIGHEST, preferred_element_type=F32)


def solve_kernel(ridge, where, own, r1, r2, r3, new_transition, new_sensing, parts):
    at = where[2]
    core = where[3]
    for k, ref in enumerate((own, r1, r2, r3)):
        parts[at ^ k] = ref[...]
    rows = lax.broadcasted_iota(jnp.int32, (W, W), 0)
    lanes = lax.broadcasted_iota(jnp.int32, (W, W), 1)
    eye = jnp.where(rows == lanes, ridge, 0.0).astype(F32)
    slabs = [parts[j, W : W + SLAB] for j in range(4)]
    far = [parts[j, W + SLAB + 8 :] for j in range(4)]
    lag_here = jnp.concatenate(slabs, axis=0)
    lag_far = jnp.concatenate(far, axis=0)
    lag_a = jnp.where(core == 0, lag_here, lag_far)
    lag_b = jnp.where(core == 0, lag_far, lag_here)

    def upper(tile):
        return jnp.where(rows <= lanes, tile, 0.0) + jnp.where(rows < lanes, tile, 0.0).T

    def lower(tile, diagonal):
        below = jnp.where(rows > lanes, tile, 0.0)
        return below + below.T + jnp.where(rows == lanes, diagonal, 0.0)

    grams = [upper(lag_a)]
    for tile in range(2):
        grams.append(upper(parts[tile, 0:W]))
        grams.append(lower(parts[tile, 0:W], parts[0, W + SLAB + tile : W + SLAB + tile + 1]))
    done = inverses([gram + eye for gram in grams])
    lag_cross_t = jnp.where(rows > lanes, lag_a, lag_b)
    new_transition[...] = exact(lag_cross_t.T, done[0])
    for tile in range(2):
        cross = parts[2 + tile, 0:W].T
        for half in range(2):
            g = 2 * tile + half
            new_sensing[g * 64 : (g + 1) * 64] = exact(cross[half * 64 : (half + 1) * 64], done[1 + g])


STRIDE = {"x": 1, "z": 4, "y": 16}


def swap(value, axis, k):
    stride = STRIDE[axis]
    pairs = []
    for i in range(64):
        at = (i // stride) % 4
        pairs.append((i, i + ((at ^ k) - at) * stride))
    return lax.ppermute(value, "tm", pairs)


def swap_core(value):
    return lax.ppermute(value, "sens", [(0, 1), (1, 0)])


def three(value, axis):
    return [swap(value, axis, k) for k in (1, 2, 3)]


def on_device(telemetry, present, transition, sensing, filter_gain, smooth_gain, initial_state):
    device = lax.axis_index("tm")
    core = lax.axis_index("sens")
    at_y, at_z, at_x = device // 16, (device // 4) % 4, device % 4
    where = jnp.stack([at_y, at_z, at_x, core]).astype(jnp.int32)
    flags = present.astype(F32)

    other_gain = swap_core(filter_gain)
    other_sensing = swap_core(sensing)
    other_flags = swap_core(flags)
    mine, theirs = call(push_kernel, [shape(ROWS, W)] * 2, 1, 3)(where, telemetry, flags, filter_gain)
    received = swap_core(theirs)
    powers, tree, whole = call(
        maps_kernel,
        [shape(SEGS, 5, W, 2 * W, dtype=BF16), shape(SEGS - 1, W, 2 * W, dtype=BF16), shape(2 * SEGS - 1, W, W)],
        3, 5,
        scratch=[pltpu.VMEM((8, W, W), F32), pltpu.VMEM((W, W), F32)],
    )(where, flags, other_flags, transition, filter_gain, other_gain, sensing, other_sensing)
    inputs, ends, packed = call(
        shift_kernel, [shape(ROWS, W), shape(32, W), shape(PACK, W)], 0, 5
    )(mine, received, powers, tree, whole)

    gain_powers, drive_map = call(
        gain_kernel, [shape(15, W, 2 * W, dtype=BF16), shape(W, 2 * W, dtype=BF16)], 0, 2
    )(smooth_gain, transition)

    by_core = [packed, swap_core(packed)]
    (chip,) = call(pair_kernel, [shape(PACK, W)], 1, 2)(where, *by_core)
    ordered = [pltpu.VMEM((4, PACK, W), F32)]
    by_x = [chip] + three(chip, "x")
    (row,) = call(functools.partial(four_kernel, 2), [shape(PACK, W)], 1, 4, ordered)(where, *by_x)
    by_z = [row] + three(row, "z")
    (plane,) = call(functools.partial(four_kernel, 1), [shape(PACK, W)], 1, 4, ordered)(where, *by_z)
    by_y = [plane] + three(plane, "y")

    drives, final, shift = call(
        filter_kernel, [shape(ROWS, W), shape(8, W), shape(8, W)], 1, 14 + 8,
        [pltpu.VMEM((16, PACK, W), F32)],
    )(
        where, *by_y, *by_z, *by_x, *by_core, initial_state.reshape(1, W), inputs, ends, powers, tree,
        gain_powers, drive_map, transition,
    )
    gathered = shift[:1]
    gathered = jnp.concatenate([gathered, swap_core(gathered)], axis=0)
    for axis in ("x", "z", "y"):
        gathered = jnp.concatenate([gathered] + three(gathered, axis), axis=0)
    smoothed, incoming = call(smooth_kernel, [shape(ROWS, W), shape(8, W)], 1, 4)(
        where, gathered, drives, final, gain_powers
    )
    both = jnp.concatenate([smoothed, incoming], axis=0)
    other_both = swap_core(both)
    smoothed_out, *chunks = call(
        stats_kernel, [shape(2 * ROWS, W, leaves=True)] + [shape(CHUNK, W)] * 4, 1, 4,
        [pltpu.VMEM((2 * ROWS, W), F32), pltpu.VMEM((4, CHUNK, W), F32)],
    )(where, telemetry, flags, both, other_both)

    got = [swap(chunks[k], "x", k) for k in (1, 2, 3)]
    part = (chunks[0] + got[0]) + (got[1] + got[2])
    for axis in ("z", "y"):
        got = three(part, axis)
        part = (part + got[0]) + (got[1] + got[2])
    part = jnp.concatenate([part, swap_core(part[W : W + SLAB])], axis=0)
    ridge = RIDGE * telemetry.shape[0] * lax.axis_size("tm")
    new_transition, new_sensing = call(
        functools.partial(solve_kernel, ridge), [shape(W, W, leaves=True), shape(2 * W, W, leaves=True)], 1, 4,
        [pltpu.VMEM((4, CHUNK + SLAB, W), F32)],
    )(where, part, *three(part, "x"))
    return new_transition, new_sensing, smoothed_out


def solution(mesh):
    placed = (P("tm", "sens"), P("tm", "sens"), P(), P("sens", None), P(None, "sens"), P(), P())
    return jax.shard_map(
        on_device,
        mesh=mesh,
        in_specs=placed,
        out_specs=(P(), P("sens", None), P("tm", None)),
        check_vma=False,
    )
```

```python
import functools

import jax
import jax.numpy as jnp
from jax import lax
from jax.experimental import pallas as pl
from jax.experimental.pallas import tpu as pltpu
from jax.sharding import PartitionSpec as P

RIDGE = 0.001
F32 = jnp.float32
BF16 = jnp.bfloat16
W = 128
SEGS = 16
LEN = 16
ROWS = SEGS * LEN
PACK = W + 8
NEAR = 8
FAR = 8
PLANE = 16
PLANES = 4
STATS = 6 * W
SLICE = STATS // PLANE
VMEM_LIMIT = 24 * 1024 * 1024


def halves(value):
    high = value.astype(BF16)
    low = (value - high.astype(F32)).astype(BF16)
    return high, low


def wide(value):
    high, low = halves(value)
    return jnp.concatenate([high, low], axis=1)


def times(left_wide, right_wide):
    stacked = jnp.concatenate([right_wide, right_wide], axis=0)
    out = jnp.dot(left_wide, stacked, preferred_element_type=F32)
    return out[:, :W] + out[:, W:]


def moved(rows, dev):
    return rows + times(wide(rows), dev)


def chained(first, second, second_wide):
    return first + second + times(wide(first), second_wide)


def identity():
    rows = lax.broadcasted_iota(jnp.int32, (W, W), 0)
    cols = lax.broadcasted_iota(jnp.int32, (W, W), 1)
    return jnp.where(rows == cols, 1.0, 0.0).astype(F32)


def call(kernel, out_shapes, n_smem, n_in, scratch=(), far=()):
    smem = [pl.BlockSpec(memory_space=pltpu.SMEM)] * n_smem
    vmem = [pl.BlockSpec(memory_space=pltpu.VMEM)] * n_in
    outs = [out if leaves else pltpu.VMEM(out.shape, out.dtype) for out, leaves in out_shapes]
    run = pl.pallas_call(
        kernel,
        out_shape=tuple(outs),
        in_specs=smem + vmem,
        out_specs=tuple([pl.BlockSpec(memory_space=pltpu.VMEM)] * len(outs)),
        scratch_shapes=list(scratch),
        compiler_params=pltpu.CompilerParams(vmem_limit_bytes=VMEM_LIMIT),
    )

    def placed(*operands):
        near = [
            pltpu.with_memory_space_constraint(v, pltpu.HBM if i in far else pltpu.VMEM)
            for i, v in enumerate(operands[n_smem:])
        ]
        return run(*operands[:n_smem], *near)

    return placed


def shape(*dims, dtype=F32, leaves=False):
    return jax.ShapeDtypeStruct(dims, dtype), leaves


def mask_of(flags, rows, segs):
    cols = flags.shape[1] * 64
    spread = (
        lax.broadcasted_iota(jnp.int32, (flags.shape[1], cols), 0)
        == lax.broadcasted_iota(jnp.int32, (flags.shape[1], cols), 1) // 64
    )
    by_sensor = jnp.dot(flags.astype(BF16), spread.astype(BF16), preferred_element_type=F32)
    repeat = (
        lax.broadcasted_iota(jnp.int32, (rows, segs), 0) // LEN
        == lax.broadcasted_iota(jnp.int32, (rows, segs), 1)
    )
    return jnp.dot(repeat.astype(BF16), by_sensor.astype(BF16), preferred_element_type=F32)


def push_kernel(where, tel, flags, gain, mine, theirs):
    gain_t = gain[...].T
    packed = wide(gain_t)
    fl = flags[...]
    for out, core in ((theirs, 1 - where[1]), (mine, where[1])):
        start = pl.multiple_of(core * ROWS, ROWS)
        seg_start = pl.multiple_of(core * SEGS, SEGS)
        mask = mask_of(flags[pl.ds(seg_start, SEGS), :], ROWS, SEGS)
        high, low = halves(tel[pl.ds(start, ROWS), :] * mask)
        total = jnp.dot(high, packed, preferred_element_type=F32) + jnp.dot(
            low, packed, preferred_element_type=F32
        )
        out[...] = total[:, :W] + total[:, W:]


def gain_maps(dev, trans_dev, gain_powers, drive_map):
    dev_wide = wide(dev)
    drive_map[...] = wide(-chained(trans_dev, dev, dev_wide))
    for level in range(15):
        gain_powers[level] = dev_wide
        if level < 14:
            dev = 2.0 * dev + times(dev_wide, dev_wide)
            dev_wide = wide(dev)


def maps_kernel(
    where, flags_own, flags_other, trans, gain_own, gain_other, sense_own, sense_other, smooth_gain,
    powers, tree, whole, gain_powers, drive_map, removed, single,
):
    a = trans[...]
    a_wide = wide(a)
    lane = lax.broadcasted_iota(jnp.int32, (W, 2 * W), 1) // 64
    for side, (gain, sense) in enumerate(((gain_own, sense_own), (gain_other, sense_other))):
        seen = times(wide(sense[...]), a_wide)
        seen_high, seen_low = halves(seen.T)
        gain_wide = wide(gain[...].T)
        for g in range(4):
            zero = jnp.zeros_like(seen_high)
            part = jnp.dot(
                jnp.where(lane == g, seen_high, zero), gain_wide, preferred_element_type=F32
            ) + jnp.dot(jnp.where(lane == g, seen_low, zero), gain_wide, preferred_element_type=F32)
            removed[side * 4 + g] = part[:, :W] + part[:, W:]
    base = a.T - identity()
    single[...] = base
    batch = 4

    def group(i, carry):
        devs = []
        for j in range(batch):
            k = i * batch + j
            row = where[1] * SEGS + k
            dev = single[...]
            for g in range(4):
                dev = dev - flags_own[row, g] * removed[g]
                dev = dev - flags_other[row, g] * removed[4 + g]
            devs.append(dev)
        for level in range(4):
            for j in range(batch):
                packed = wide(devs[j])
                powers[i * batch + j, level] = packed
                devs[j] = 2.0 * devs[j] + times(packed, packed)
        for j in range(batch):
            powers[i * batch + j, 4] = wide(devs[j])
            whole[i * batch + j] = devs[j]
        return carry

    lax.fori_loop(0, SEGS // batch, group, 0)
    gain_maps(smooth_gain[...].T - identity(), base, gain_powers, drive_map)
    count, base_at, source_at = SEGS, SEGS, 0
    while count > 1:
        for p in range(count // 2):
            second = whole[source_at + 2 * p + 1]
            joined = chained(whole[source_at + 2 * p], second, wide(second))
            whole[base_at + p] = joined
            tree[base_at - SEGS + p] = wide(joined)
        source_at = base_at
        count //= 2
        base_at += count


def seg_scan(rows, powers):
    row_at = lax.broadcasted_iota(jnp.int32, (ROWS, W), 0) % LEN
    for level in range(4):
        reach = 1 << level
        before = jnp.where(row_at >= reach, pltpu.roll(rows, reach, 0), 0.0)
        packed = wide(before)
        parts = [
            times(packed[k * LEN : (k + 1) * LEN], powers[k, level]) for k in range(SEGS)
        ]
        rows = rows + before + jnp.concatenate(parts, axis=0)
    return rows


def shift_kernel(mine, received, powers, tree, whole, inputs, ends, packed):
    rows = mine[...] + received[...]
    inputs[...] = rows
    reached = seg_scan(rows, powers)
    level = [reached[k * LEN + LEN - 1 : (k + 1) * LEN] for k in range(SEGS)]
    ends[0:SEGS] = jnp.concatenate(level, axis=0)
    maps = [powers[k, 4] for k in range(SEGS)]
    at, tree_at = SEGS, 0
    while len(level) > 1:
        level = [
            moved(jnp.broadcast_to(level[2 * p], (8, W)), maps[2 * p + 1])[0:1] + level[2 * p + 1]
            for p in range(len(level) // 2)
        ]
        maps = [tree[tree_at + p] for p in range(len(level))]
        tree_at += len(level)
        for p, row in enumerate(level):
            ends[at + p : at + p + 1] = row
        at += len(level)
    packed[0:W] = whole[2 * SEGS - 2]
    packed[W:PACK] = jnp.broadcast_to(level[0], (PACK - W, W))


def join2(first, second):
    second_dev = second[0:W]
    second_wide = wide(second_dev)
    dev = chained(first[0:W], second_dev, second_wide)
    row = moved(first[W:PACK], second_wide) + second[W:PACK]
    return dev, row


def repeated(out, row, value, copies, rows):
    for j in range(copies):
        out[j * rows + row : j * rows + row + value.shape[0]] = value


def pair_kernel(where, own, other, out):
    core = where[1]
    mine, theirs = own[...], other[...]
    first = jnp.where(core == 0, mine, theirs)
    second = jnp.where(core == 0, theirs, mine)
    dev, row = join2(first, second)
    repeated(out, 0, dev, NEAR, PACK)
    repeated(out, W, row, NEAR, PACK)


def split_maps(raw):
    return [(raw[j * PACK : j * PACK + W], raw[j * PACK + W : (j + 1) * PACK]) for j in range(8)]


def joined(first, second):
    second_wide = wide(second[0])
    return chained(first[0], second[0], second_wide), moved(first[1], second_wide) + second[1]


def eight_kernel(raw, out, early):
    level = split_maps(raw)
    pairs = [joined(level[2 * p], level[2 * p + 1]) for p in range(4)]
    fours = [joined(pairs[0], pairs[1]), joined(pairs[2], pairs[3])]
    dev, row = joined(*fours)
    repeated(out, 0, dev, FAR, PACK)
    repeated(out, W, row, FAR, PACK)
    for slot, (dev, row) in enumerate((fours[0], pairs[0], pairs[2])):
        early[slot, 0:W] = dev
        early[slot, W:PACK] = row


def advance(state, at, raw, early):
    def step(state, used, packed):
        ahead = moved(state, wide(packed[0:W])) + packed[W : W + 8]
        return jnp.where(used, ahead, state)

    state = step(state, at >= 4, early[0])
    state = step(state, (at & 2) != 0, early[1 + (at >> 2)])
    start = pl.multiple_of((at & 6) * PACK, 8)
    return step(state, (at & 1) != 0, raw[pl.ds(start, PACK)])


def filter_kernel(
    where, far, near, early, c1, initial, inputs, ends, powers, tree, gain_powers, drive_map,
    trans, drives, final, shift, far_early,
):
    device, core = where[0], where[1]
    level = split_maps(far)
    pairs = [joined(level[2 * p], level[2 * p + 1]) for p in range(3)]
    for slot, (dev, row) in enumerate((joined(pairs[0], pairs[1]), pairs[0], pairs[2])):
        far_early[slot, 0:W] = dev
        far_early[slot, W:PACK] = row
    state = jnp.broadcast_to(initial[...], (8, W))
    state = advance(state, device // NEAR, far, far_early)
    state = advance(state, device % NEAR, near, early)
    ahead = moved(state, wide(c1[0:W])) + c1[W : W + 8]
    state = jnp.where(core == 1, ahead, state)
    starts = {0: state}
    for span, maps_at, ends_at in ((8, 12, 28), (4, 8, 24), (2, 0, 16), (1, -1, 0)):
        for begin in range(0, SEGS, 2 * span):
            p = begin // span
            dev = powers[p, 4] if span == 1 else tree[maps_at + p]
            starts[begin + span] = moved(starts[begin], dev) + ends[ends_at + p : ends_at + p + 1]
    entry = [moved(starts[k], powers[k, 0]) for k in range(SEGS)]
    spread = jnp.concatenate(
        [part for k in range(SEGS) for part in (entry[k], jnp.zeros((8, W), F32))], axis=0
    )
    row_at = lax.broadcasted_iota(jnp.int32, (ROWS, W), 0) % LEN
    rows = inputs[...] + jnp.where(row_at == 0, spread, 0.0)
    rows = seg_scan(rows, powers)
    drive = times(wide(rows), drive_map[...])
    drives[...] = drive
    last = jnp.broadcast_to(rows[ROWS - 1 : ROWS], (8, W))
    final_row = last + times(wide(last), wide(trans[...].T - identity()))
    final[...] = final_row
    top = (device == NEAR * FAR - 1) & (core == 1)
    part = drive
    for level in (7, 6, 5, 4, 3):
        half = 1 << level
        part = part[:half] + moved(part[half:], gain_powers[level])
    for level in (2, 1, 0):
        half = 1 << level
        behind = pltpu.roll(part, 8 - half, 0)
        part = part + moved(behind, gain_powers[level])
    from_top = moved(final_row, gain_powers[8])
    own = part[0:1] + jnp.where(top, from_top[0:1], 0.0)
    shift[...] = jnp.broadcast_to(own, (W, W))


def smooth_kernel(where, gathered, drives, final, gain_powers, smoothed, incoming, suffix):
    rows = gathered[...]
    place = 2 * where[0] + where[1]
    for level in range(7):
        suffix[level] = rows
        if level < 6:
            ahead = moved(rows, gain_powers[8 + level])
            rows = rows + pltpu.roll(ahead, W - (1 << level), 0)
    state = jnp.zeros((8, W), F32)
    for level in (6, 5, 4, 3, 2, 1, 0):
        sibling = ((place >> level) | 1) << level
        ahead = moved(state, gain_powers[8 + level]) + suffix[level, pl.ds(sibling, 1)]
        state = jnp.where(((place >> level) & 1) == 0, ahead, state)
    top = jnp.where(place == W - 1, 1, 0)
    state = jnp.where(top == 1, final[...], state)
    incoming[...] = state
    entry = moved(state, gain_powers[0])
    row_at = lax.broadcasted_iota(jnp.int32, (ROWS, W), 0)
    part = drives[...]
    part = part + jnp.where(row_at == ROWS - 1, jnp.broadcast_to(entry[0:1], (ROWS, W)), 0.0)
    for level in range(8):
        reach = 1 << level
        behind = jnp.where(row_at < ROWS - reach, pltpu.roll(part, ROWS - reach, 0), 0.0)
        part = part + moved(behind, gain_powers[level])
    smoothed[...] = part


def stats_kernel(where, tel, flags, own, other, smoothed, parts, full):
    core = where[1]
    full[pl.ds(pl.multiple_of(core * ROWS, ROWS), ROWS)] = own[0:ROWS]
    full[pl.ds(pl.multiple_of((1 - core) * ROWS, ROWS), ROWS)] = other[0:ROWS]
    rows = full[...]
    smoothed[...] = rows
    count = 2 * ROWS
    after = jnp.where(core == 1, own[ROWS : ROWS + 8], other[ROWS : ROWS + 8])
    row_at = lax.broadcasted_iota(jnp.int32, (count, W), 0)
    following = jnp.where(
        row_at == count - 1, jnp.broadcast_to(after[0:1], (count, W)), pltpu.roll(rows, count - 1, 0)
    )
    packed = wide(rows)
    packed_t = jnp.concatenate([rows.T.astype(BF16), (rows - rows.astype(BF16).astype(F32)).T.astype(BF16)], axis=0)
    last_chip = where[0] == NEAR * FAR - 1
    lane_at = lax.broadcasted_iota(jnp.int32, (2 * W, count), 1)
    kept = jnp.where(last_chip & (lane_at == count - 1), jnp.zeros_like(packed_t), packed_t)

    def fold(out):
        return (out[:W, :W] + out[:W, W:]) + (out[W:, :W] + out[W:, W:])

    upper = lax.broadcasted_iota(jnp.int32, (W, W), 0) - lax.broadcasted_iota(jnp.int32, (W, W), 1)
    lag_gram = fold(jnp.dot(kept, packed, preferred_element_type=F32))
    lag_cross_t = fold(jnp.dot(kept, wide(following), preferred_element_type=F32))
    fl = flags[...]
    repeat = (
        lax.broadcasted_iota(jnp.int32, (2 * SEGS, count), 0)
        == lax.broadcasted_iota(jnp.int32, (2 * SEGS, count), 1) // LEN
    )
    lane_flags = lax.dot_general(
        fl.astype(BF16), repeat.astype(BF16), (((0,), (0,)), ((), ())), preferred_element_type=F32
    )
    grams = []
    for g in range(4):
        masked_t = packed_t * lane_flags[g : g + 1].astype(BF16)
        grams.append(fold(jnp.dot(masked_t, packed, preferred_element_type=F32)))
    def diagonal(gram):
        return jnp.sum(jnp.where(upper == 0, gram, 0.0), axis=0, keepdims=True)

    for tile in range(2):
        parts[tile * W : (tile + 1) * W] = jnp.where(upper <= 0, grams[2 * tile], grams[2 * tile + 1])
    parts[4 * W : 5 * W] = jnp.where(upper <= 0, lag_gram, lag_cross_t)
    parts[5 * W : 6 * W] = jnp.where(upper <= 0, lag_cross_t, 0.0)
    lane = lax.broadcasted_iota(jnp.int32, (1, W), 1)
    for tile in range(2):
        line = diagonal(grams[2 * tile + 1])
        for half in range(2):
            row = 6 * W - 4 + 2 * tile + half
            moved_line = line if half == 0 else pltpu.roll(line, W // 2, 1)
            parts[row : row + 1] = jnp.where(lane < W // 2, moved_line, parts[row : row + 1])
    high, low = halves(tel[...] * mask_of(fl, count, 2 * SEGS))
    cross = jnp.dot(packed_t, high, preferred_element_type=F32) + jnp.dot(
        packed_t, low, preferred_element_type=F32
    )
    cross = cross[:W] + cross[W:]
    parts[2 * W : 3 * W] = cross[:, :W]
    parts[3 * W : 4 * W] = cross[:, W:]

def sum_kernel(count, copies, parts, out):
    rows = SLICE
    total = parts[0:rows]
    for j in range(1, count):
        total = total + parts[j * rows : (j + 1) * rows]
    for j in range(copies):
        out[j * rows : (j + 1) * rows] = total


def inverses(matrices):
    unit = 8
    lane = lax.broadcasted_iota(jnp.int32, (W, W), 1)
    lane_head = lane[:unit]
    row_head = lax.broadcasted_iota(jnp.int32, (unit, W), 0)

    def block(b, held):
        heads = [m[:unit] for m in held]
        rests = [m[unit:] for m in held]
        for j in range(unit):
            for p in range(len(held)):
                head, rest = heads[p], rests[p]
                row = head[j : j + 1]
                scale = 1.0 / row[:, j : j + 1]
                row = jnp.where(lane_head[:1] == j, scale, row * scale)
                head_next = jnp.where(lane_head == j, 0.0, head) - head[:, j : j + 1] * row
                heads[p] = jnp.where(row_head == j, row, head_next)
                rests[p] = jnp.where(lane[unit:] == j, 0.0, rest) - rest[:, j : j + 1] * row
        return tuple(
            pltpu.roll(jnp.concatenate([rest, head], axis=0), W - unit, 1)
            for head, rest in zip(heads, rests)
        )

    return lax.fori_loop(0, W // unit, block, tuple(matrices))


def exact(left, right):
    return jnp.dot(left, right, precision=lax.Precision.HIGHEST, preferred_element_type=F32)


def solve_kernel(ridge, stats, new_transition, new_sensing):
    rows = lax.broadcasted_iota(jnp.int32, (W, W), 0)
    lanes = lax.broadcasted_iota(jnp.int32, (W, W), 1)
    eye = jnp.where(rows == lanes, ridge, 0.0).astype(F32)
    lag_a = stats[4 * W : 5 * W]
    lag_b = stats[5 * W : 6 * W]
    half = lax.broadcasted_iota(jnp.int32, (1, W), 1) < W // 2
    def upper(tile):
        return jnp.where(rows <= lanes, tile, 0.0) + jnp.where(rows < lanes, tile, 0.0).T

    def lower(tile, diagonal):
        below = jnp.where(rows > lanes, tile, 0.0)
        return below + below.T + jnp.where(rows == lanes, diagonal, 0.0)

    grams = [upper(lag_a)]
    for tile in range(2):
        packed = stats[tile * W : (tile + 1) * W]
        row = 6 * W - 4 + 2 * tile
        line = jnp.where(half, stats[row : row + 1], pltpu.roll(stats[row + 1 : row + 2], W // 2, 1))
        grams.append(upper(packed))
        grams.append(lower(packed, line))
    done = inverses([gram + eye for gram in grams])
    lag_cross_t = jnp.where(rows > lanes, lag_a, lag_b)
    new_transition[...] = exact(lag_cross_t.T, done[0])
    for tile in range(2):
        cross = stats[(2 + tile) * W : (3 + tile) * W].T
        for side in range(2):
            g = 2 * tile + side
            new_sensing[g * 64 : (g + 1) * 64] = exact(cross[side * 64 : (side + 1) * 64], done[1 + g])


def swap_core(value):
    return lax.ppermute(value, "sens", [(0, 1), (1, 0)])


def exchange(value, stride, count):
    groups = [
        [first + stride * j for j in range(count)]
        for first in range(NEAR * FAR)
        if (first // stride) % count == 0
    ]
    return lax.all_to_all(value, "tm", 0, 0, axis_index_groups=groups, tiled=True)


def on_device(telemetry, present, transition, sensing, filter_gain, smooth_gain, initial_state):
    where = jnp.stack([lax.axis_index("tm"), lax.axis_index("sens")]).astype(jnp.int32)
    flags = present.astype(F32)

    other_gain = swap_core(filter_gain)
    other_sensing = swap_core(sensing)
    other_flags = swap_core(flags)
    mine, theirs = call(push_kernel, [shape(ROWS, W)] * 2, 1, 3, far=(0, 2))(
        where, telemetry, flags, filter_gain
    )
    received = swap_core(theirs)
    powers, tree, whole, gain_powers, drive_map = call(
        maps_kernel,
        [
            shape(SEGS, 5, W, 2 * W, dtype=BF16), shape(SEGS - 1, W, 2 * W, dtype=BF16),
            shape(2 * SEGS - 1, W, W), shape(15, W, 2 * W, dtype=BF16), shape(W, 2 * W, dtype=BF16),
        ],
        3, 6,
        scratch=[pltpu.VMEM((8, W, W), F32), pltpu.VMEM((W, W), F32)],
        far=(0, 1, 3, 5),
    )(where, flags, other_flags, transition, filter_gain, other_gain, sensing, other_sensing, smooth_gain)
    inputs, ends, packed = call(
        shift_kernel, [shape(ROWS, W), shape(32, W), shape(PACK, W)], 0, 5
    )(mine, received, powers, tree, whole)

    other_packed = swap_core(packed)
    (chip,) = call(pair_kernel, [shape(NEAR * PACK, W)], 1, 2)(where, packed, other_packed)
    near = exchange(chip, 1, NEAR)
    group, early = call(eight_kernel, [shape(FAR * PACK, W), shape(3, PACK, W)], 0, 1)(near)
    far = exchange(group, NEAR, FAR)
    drives, final, shift = call(
        filter_kernel, [shape(ROWS, W), shape(8, W), shape(W, W)], 1, 12,
        [pltpu.VMEM((3, PACK, W), F32)],
    )(
        where, far, near, early, other_packed, initial_state.reshape(1, W), inputs, ends, powers, tree,
        gain_powers, drive_map, transition,
    )
    gathered = lax.all_to_all(shift, ("tm", "sens"), 0, 0, tiled=True)
    smoothed, incoming = call(
        smooth_kernel, [shape(ROWS, W), shape(8, W)], 1, 4, [pltpu.VMEM((7, W, W), F32)]
    )(where, gathered, drives, final, gain_powers)
    both = jnp.concatenate([smoothed, incoming], axis=0)
    other_both = swap_core(both)
    smoothed_out, stats = call(
        stats_kernel, [shape(2 * ROWS, W, leaves=True), shape(STATS, W)], 1, 4,
        [pltpu.VMEM((2 * ROWS, W), F32)],
    )(where, telemetry, flags, both, other_both)

    stats = exchange(stats, 1, PLANE)
    (stats,) = call(functools.partial(sum_kernel, PLANE, PLANES), [shape(PLANES * SLICE, W)], 0, 1)(stats)
    stats = exchange(stats, PLANE, PLANES)
    (stats,) = call(functools.partial(sum_kernel, PLANES, PLANE), [shape(STATS, W)], 0, 1)(stats)
    stats = exchange(stats, 1, PLANE)
    ridge = RIDGE * telemetry.shape[0] * lax.axis_size("tm")
    new_transition, new_sensing = call(
        functools.partial(solve_kernel, ridge), [shape(W, W, leaves=True), shape(2 * W, W, leaves=True)], 0, 1
    )(stats)
    return new_transition, new_sensing, smoothed_out


def solution(mesh):
    placed = (P("tm", "sens"), P("tm", "sens"), P(), P("sens", None), P(None, "sens"), P(), P())
    return jax.shard_map(
        on_device,
        mesh=mesh,
        in_specs=placed,
        out_specs=(P(), P("sens", None), P("tm", None)),
        check_vma=False,
    )
```

```python
import functools

import jax
import jax.numpy as jnp
from jax import lax
from jax.experimental import pallas as pl
from jax.experimental.pallas import tpu as pltpu
from jax.sharding import PartitionSpec as P

RIDGE = 0.001
F32 = jnp.float32
BF16 = jnp.bfloat16
W = 128
SEGS = 16
LEN = 16
ROWS = SEGS * LEN
PACK = W + 8
NEAR = 8
FAR = 8
PLANE = 16
PLANES = 4
STATS = 6 * W
SLICE = STATS // PLANE
VMEM_LIMIT = 24 * 1024 * 1024


def halves(value):
    high = value.astype(BF16)
    low = (value - high.astype(F32)).astype(BF16)
    return high, low


def wide(value):
    high, low = halves(value)
    return jnp.concatenate([high, low], axis=1)


def times(left_wide, right_wide):
    stacked = jnp.concatenate([right_wide, right_wide], axis=0)
    out = jnp.dot(left_wide, stacked, preferred_element_type=F32)
    return out[:, :W] + out[:, W:]


def moved(rows, dev):
    return rows + times(wide(rows), dev)


def chained(first, second, second_wide):
    return first + second + times(wide(first), second_wide)


def identity():
    rows = lax.broadcasted_iota(jnp.int32, (W, W), 0)
    cols = lax.broadcasted_iota(jnp.int32, (W, W), 1)
    return jnp.where(rows == cols, 1.0, 0.0).astype(F32)


def call(kernel, out_shapes, n_smem, n_in, scratch=(), far=()):
    smem = [pl.BlockSpec(memory_space=pltpu.SMEM)] * n_smem
    vmem = [pl.BlockSpec(memory_space=pltpu.VMEM)] * n_in
    outs = [out if leaves else pltpu.VMEM(out.shape, out.dtype) for out, leaves in out_shapes]
    run = pl.pallas_call(
        kernel,
        out_shape=tuple(outs),
        in_specs=smem + vmem,
        out_specs=tuple([pl.BlockSpec(memory_space=pltpu.VMEM)] * len(outs)),
        scratch_shapes=list(scratch),
        compiler_params=pltpu.CompilerParams(vmem_limit_bytes=VMEM_LIMIT),
    )

    def placed(*operands):
        near = [
            pltpu.with_memory_space_constraint(v, pltpu.HBM if i in far else pltpu.VMEM)
            for i, v in enumerate(operands[n_smem:])
        ]
        return run(*operands[:n_smem], *near)

    return placed


def shape(*dims, dtype=F32, leaves=False):
    return jax.ShapeDtypeStruct(dims, dtype), leaves


def mask_of(flags, rows, segs):
    cols = flags.shape[1] * 64
    spread = (
        lax.broadcasted_iota(jnp.int32, (flags.shape[1], cols), 0)
        == lax.broadcasted_iota(jnp.int32, (flags.shape[1], cols), 1) // 64
    )
    by_sensor = jnp.dot(flags.astype(BF16), spread.astype(BF16), preferred_element_type=F32)
    repeat = (
        lax.broadcasted_iota(jnp.int32, (rows, segs), 0) // LEN
        == lax.broadcasted_iota(jnp.int32, (rows, segs), 1)
    )
    return jnp.dot(repeat.astype(BF16), by_sensor.astype(BF16), preferred_element_type=F32)


def push_kernel(where, tel, flags, gain, mine, theirs):
    gain_t = gain[...].T
    packed = wide(gain_t)
    fl = flags[...]
    for out, core in ((theirs, 1 - where[1]), (mine, where[1])):
        start = pl.multiple_of(core * ROWS, ROWS)
        seg_start = pl.multiple_of(core * SEGS, SEGS)
        mask = mask_of(flags[pl.ds(seg_start, SEGS), :], ROWS, SEGS)
        high, low = halves(tel[pl.ds(start, ROWS), :] * mask)
        total = jnp.dot(high, packed, preferred_element_type=F32) + jnp.dot(
            low, packed, preferred_element_type=F32
        )
        out[...] = total[:, :W] + total[:, W:]


def gain_maps(dev, trans_dev, gain_powers, drive_map):
    dev_wide = wide(dev)
    drive_map[...] = wide(-chained(trans_dev, dev, dev_wide))
    for level in range(15):
        gain_powers[level] = dev_wide
        if level < 14:
            dev = 2.0 * dev + times(dev_wide, dev_wide)
            dev_wide = wide(dev)


def maps_kernel(
    where, flags_own, flags_other, trans, gain_own, gain_other, sense_own, sense_other, smooth_gain,
    powers, tree, whole, gain_powers, drive_map, removed, single,
):
    a = trans[...]
    a_wide = wide(a)
    lane = lax.broadcasted_iota(jnp.int32, (W, 2 * W), 1) // 64
    for side, (gain, sense) in enumerate(((gain_own, sense_own), (gain_other, sense_other))):
        seen = times(wide(sense[...]), a_wide)
        seen_high, seen_low = halves(seen.T)
        gain_wide = wide(gain[...].T)
        for g in range(4):
            zero = jnp.zeros_like(seen_high)
            part = jnp.dot(
                jnp.where(lane == g, seen_high, zero), gain_wide, preferred_element_type=F32
            ) + jnp.dot(jnp.where(lane == g, seen_low, zero), gain_wide, preferred_element_type=F32)
            removed[side * 4 + g] = part[:, :W] + part[:, W:]
    base = a.T - identity()
    single[...] = base
    batch = 4

    def group(i, carry):
        devs = []
        for j in range(batch):
            k = i * batch + j
            row = where[1] * SEGS + k
            dev = single[...]
            for g in range(4):
                dev = dev - flags_own[row, g] * removed[g]
                dev = dev - flags_other[row, g] * removed[4 + g]
            devs.append(dev)
        for level in range(4):
            for j in range(batch):
                packed = wide(devs[j])
                powers[i * batch + j, level] = packed
                devs[j] = 2.0 * devs[j] + times(packed, packed)
        for j in range(batch):
            powers[i * batch + j, 4] = wide(devs[j])
            whole[i * batch + j] = devs[j]
        return carry

    lax.fori_loop(0, SEGS // batch, group, 0)
    gain_maps(smooth_gain[...].T - identity(), base, gain_powers, drive_map)
    count, base_at, source_at = SEGS, SEGS, 0
    while count > 1:
        for p in range(count // 2):
            second = whole[source_at + 2 * p + 1]
            joined = chained(whole[source_at + 2 * p], second, wide(second))
            whole[base_at + p] = joined
            tree[base_at - SEGS + p] = wide(joined)
        source_at = base_at
        count //= 2
        base_at += count


def seg_scan(rows, powers):
    row_at = lax.broadcasted_iota(jnp.int32, (ROWS, W), 0) % LEN
    for level in range(4):
        reach = 1 << level
        before = jnp.where(row_at >= reach, pltpu.roll(rows, reach, 0), 0.0)
        packed = wide(before)
        parts = [
            times(packed[k * LEN : (k + 1) * LEN], powers[k, level]) for k in range(SEGS)
        ]
        rows = rows + before + jnp.concatenate(parts, axis=0)
    return rows


def shift_kernel(mine, received, powers, tree, whole, inputs, ends, packed):
    rows = mine[...] + received[...]
    inputs[...] = rows
    reached = seg_scan(rows, powers)
    level = [reached[k * LEN + LEN - 1 : (k + 1) * LEN] for k in range(SEGS)]
    ends[0:SEGS] = jnp.concatenate(level, axis=0)
    maps = [powers[k, 4] for k in range(SEGS)]
    at, tree_at = SEGS, 0
    while len(level) > 1:
        level = [
            moved(jnp.broadcast_to(level[2 * p], (8, W)), maps[2 * p + 1])[0:1] + level[2 * p + 1]
            for p in range(len(level) // 2)
        ]
        maps = [tree[tree_at + p] for p in range(len(level))]
        tree_at += len(level)
        for p, row in enumerate(level):
            ends[at + p : at + p + 1] = row
        at += len(level)
    packed[0:W] = whole[2 * SEGS - 2]
    packed[W:PACK] = jnp.broadcast_to(level[0], (PACK - W, W))


def join2(first, second):
    second_dev = second[0:W]
    second_wide = wide(second_dev)
    dev = chained(first[0:W], second_dev, second_wide)
    row = moved(first[W:PACK], second_wide) + second[W:PACK]
    return dev, row


def repeated(out, row, value, copies, rows):
    for j in range(copies):
        out[j * rows + row : j * rows + row + value.shape[0]] = value


def pair_kernel(where, own, other, out):
    core = where[1]
    mine, theirs = own[...], other[...]
    first = jnp.where(core == 0, mine, theirs)
    second = jnp.where(core == 0, theirs, mine)
    dev, row = join2(first, second)
    repeated(out, 0, dev, NEAR, PACK)
    repeated(out, W, row, NEAR, PACK)


def split_maps(raw):
    return [(raw[j * PACK : j * PACK + W], raw[j * PACK + W : (j + 1) * PACK]) for j in range(8)]


def joined(first, second):
    second_wide = wide(second[0])
    return chained(first[0], second[0], second_wide), moved(first[1], second_wide) + second[1]


def eight_kernel(raw, out, early):
    level = split_maps(raw)
    pairs = [joined(level[2 * p], level[2 * p + 1]) for p in range(4)]
    fours = [joined(pairs[0], pairs[1]), joined(pairs[2], pairs[3])]
    dev, row = joined(*fours)
    repeated(out, 0, dev, FAR, PACK)
    repeated(out, W, row, FAR, PACK)
    for slot, (dev, row) in enumerate((fours[0], pairs[0], pairs[2])):
        early[slot, 0:W] = dev
        early[slot, W:PACK] = row


def advance(state, at, raw, early):
    def step(state, used, packed):
        ahead = moved(state, wide(packed[0:W])) + packed[W : W + 8]
        return jnp.where(used, ahead, state)

    state = step(state, at >= 4, early[0])
    state = step(state, (at & 2) != 0, early[1 + (at >> 2)])
    start = pl.multiple_of((at & 6) * PACK, 8)
    return step(state, (at & 1) != 0, raw[pl.ds(start, PACK)])


def filter_kernel(
    where, far, near, early, c1, initial, inputs, ends, powers, tree, gain_powers, drive_map,
    trans, drives, final, shift, far_early,
):
    device, core = where[0], where[1]
    level = split_maps(far)
    pairs = [joined(level[2 * p], level[2 * p + 1]) for p in range(3)]
    for slot, (dev, row) in enumerate((joined(pairs[0], pairs[1]), pairs[0], pairs[2])):
        far_early[slot, 0:W] = dev
        far_early[slot, W:PACK] = row
    state = jnp.broadcast_to(initial[...], (8, W))
    state = advance(state, device // NEAR, far, far_early)
    state = advance(state, device % NEAR, near, early)
    ahead = moved(state, wide(c1[0:W])) + c1[W : W + 8]
    state = jnp.where(core == 1, ahead, state)
    starts = {0: state}
    for span, maps_at, ends_at in ((8, 12, 28), (4, 8, 24), (2, 0, 16), (1, -1, 0)):
        for begin in range(0, SEGS, 2 * span):
            p = begin // span
            dev = powers[p, 4] if span == 1 else tree[maps_at + p]
            starts[begin + span] = moved(starts[begin], dev) + ends[ends_at + p : ends_at + p + 1]
    entry = [moved(starts[k], powers[k, 0]) for k in range(SEGS)]
    spread = jnp.concatenate(
        [part for k in range(SEGS) for part in (entry[k], jnp.zeros((8, W), F32))], axis=0
    )
    row_at = lax.broadcasted_iota(jnp.int32, (ROWS, W), 0) % LEN
    rows = inputs[...] + jnp.where(row_at == 0, spread, 0.0)
    rows = seg_scan(rows, powers)
    drive = times(wide(rows), drive_map[...])
    drives[...] = drive
    last = jnp.broadcast_to(rows[ROWS - 1 : ROWS], (8, W))
    final_row = last + times(wide(last), wide(trans[...].T - identity()))
    final[...] = final_row
    top = (device == NEAR * FAR - 1) & (core == 1)
    part = drive
    for level in (7, 6, 5, 4, 3):
        half = 1 << level
        part = part[:half] + moved(part[half:], gain_powers[level])
    for level in (2, 1, 0):
        half = 1 << level
        behind = pltpu.roll(part, 8 - half, 0)
        part = part + moved(behind, gain_powers[level])
    from_top = moved(final_row, gain_powers[8])
    own = part[0:1] + jnp.where(top, from_top[0:1], 0.0)
    shift[...] = jnp.broadcast_to(own, (W, W))


def smooth_kernel(where, gathered, drives, final, gain_powers, smoothed, incoming, suffix):
    rows = gathered[...]
    place = 2 * where[0] + where[1]
    for level in range(7):
        suffix[level] = rows
        if level < 6:
            ahead = moved(rows, gain_powers[8 + level])
            rows = rows + pltpu.roll(ahead, W - (1 << level), 0)
    state = jnp.zeros((8, W), F32)
    for level in (6, 5, 4, 3, 2, 1, 0):
        sibling = ((place >> level) | 1) << level
        ahead = moved(state, gain_powers[8 + level]) + suffix[level, pl.ds(sibling, 1)]
        state = jnp.where(((place >> level) & 1) == 0, ahead, state)
    top = jnp.where(place == W - 1, 1, 0)
    state = jnp.where(top == 1, final[...], state)
    incoming[...] = state
    entry = moved(state, gain_powers[0])
    row_at = lax.broadcasted_iota(jnp.int32, (ROWS, W), 0)
    part = drives[...]
    part = part + jnp.where(row_at == ROWS - 1, jnp.broadcast_to(entry[0:1], (ROWS, W)), 0.0)
    for level in range(8):
        reach = 1 << level
        behind = jnp.where(row_at < ROWS - reach, pltpu.roll(part, ROWS - reach, 0), 0.0)
        part = part + moved(behind, gain_powers[level])
    smoothed[...] = part


def stats_kernel(where, tel, flags, own, other, smoothed, parts, full):
    core = where[1]
    full[pl.ds(pl.multiple_of(core * ROWS, ROWS), ROWS)] = own[0:ROWS]
    full[pl.ds(pl.multiple_of((1 - core) * ROWS, ROWS), ROWS)] = other[0:ROWS]
    rows = full[...]
    smoothed[...] = rows
    count = 2 * ROWS
    after = jnp.where(core == 1, own[ROWS : ROWS + 8], other[ROWS : ROWS + 8])
    row_at = lax.broadcasted_iota(jnp.int32, (count, W), 0)
    following = jnp.where(
        row_at == count - 1, jnp.broadcast_to(after[0:1], (count, W)), pltpu.roll(rows, count - 1, 0)
    )
    packed = wide(rows)
    packed_t = jnp.concatenate([rows.T.astype(BF16), (rows - rows.astype(BF16).astype(F32)).T.astype(BF16)], axis=0)
    last_chip = where[0] == NEAR * FAR - 1
    lane_at = lax.broadcasted_iota(jnp.int32, (2 * W, count), 1)
    kept = jnp.where(last_chip & (lane_at == count - 1), jnp.zeros_like(packed_t), packed_t)

    def fold(out):
        return (out[:W, :W] + out[:W, W:]) + (out[W:, :W] + out[W:, W:])

    upper = lax.broadcasted_iota(jnp.int32, (W, W), 0) - lax.broadcasted_iota(jnp.int32, (W, W), 1)
    lag_gram = fold(jnp.dot(kept, packed, preferred_element_type=F32))
    lag_cross_t = fold(jnp.dot(kept, wide(following), preferred_element_type=F32))
    fl = flags[...]
    repeat = (
        lax.broadcasted_iota(jnp.int32, (2 * SEGS, count), 0)
        == lax.broadcasted_iota(jnp.int32, (2 * SEGS, count), 1) // LEN
    )
    lane_flags = lax.dot_general(
        fl.astype(BF16), repeat.astype(BF16), (((0,), (0,)), ((), ())), preferred_element_type=F32
    )
    grams = []
    for g in range(4):
        masked_t = packed_t * lane_flags[g : g + 1].astype(BF16)
        grams.append(fold(jnp.dot(masked_t, packed, preferred_element_type=F32)))
    def diagonal(gram):
        return jnp.sum(jnp.where(upper == 0, gram, 0.0), axis=0, keepdims=True)

    for tile in range(2):
        parts[tile * W : (tile + 1) * W] = jnp.where(upper <= 0, grams[2 * tile], grams[2 * tile + 1])
    parts[4 * W : 5 * W] = jnp.where(upper <= 0, lag_gram, lag_cross_t)
    parts[5 * W : 6 * W] = jnp.where(upper <= 0, lag_cross_t, 0.0)
    lane = lax.broadcasted_iota(jnp.int32, (1, W), 1)
    for tile in range(2):
        line = diagonal(grams[2 * tile + 1])
        for half in range(2):
            row = 6 * W - 4 + 2 * tile + half
            moved_line = line if half == 0 else pltpu.roll(line, W // 2, 1)
            parts[row : row + 1] = jnp.where(lane < W // 2, moved_line, parts[row : row + 1])
    high, low = halves(tel[...] * mask_of(fl, count, 2 * SEGS))
    cross = jnp.dot(packed_t, high, preferred_element_type=F32) + jnp.dot(
        packed_t, low, preferred_element_type=F32
    )
    cross = cross[:W] + cross[W:]
    parts[2 * W : 3 * W] = cross[:, :W]
    parts[3 * W : 4 * W] = cross[:, W:]

def sum_kernel(count, copies, parts, out):
    rows = SLICE
    total = parts[0:rows]
    for j in range(1, count):
        total = total + parts[j * rows : (j + 1) * rows]
    for j in range(copies):
        out[j * rows : (j + 1) * rows] = total


def exact(left, right):
    return jnp.dot(left, right, precision=lax.Precision.HIGHEST, preferred_element_type=F32)


def sweep(entry, count):
    entry = [list(row) for row in entry]
    for q in range(count):
        scale = 1.0 / entry[q][q]
        row = [entry[q][c] * scale for c in range(count)]
        for r in range(count):
            for c in range(r, count):
                if q not in (r, c):
                    entry[r][c] = entry[r][c] - entry[r][q] * row[c]
        for r in range(count):
            entry[r][q] = entry[q][r] = row[r]
        entry[q][q] = -scale
        for r in range(count):
            for c in range(r):
                entry[r][c] = entry[c][r]
    return entry


def inverses(matrices):
    unit, pivots = 32, 8
    lane = lax.broadcasted_iota(jnp.int32, (W, W), 1)
    lane_tile = lane[:8]
    lane_head = lane[:unit]
    row_head = lax.broadcasted_iota(jnp.int32, (unit, W), 0)
    sublane = lax.broadcasted_iota(jnp.int32, (8, W), 0)

    def panel(b, held):
        heads = [m[:unit] for m in held]
        for j in range(0, unit, pivots):
            stacked = []
            for r in range(pivots):
                rows = jnp.broadcast_to(heads[0][j + r : j + r + 1], (8, W))
                for p in range(1, len(heads)):
                    mine = jnp.broadcast_to(heads[p][j + r : j + r + 1], (8, W))
                    rows = jnp.where(sublane == p, mine, rows)
                stacked.append(rows)
            entry = [[None] * pivots for _ in range(pivots)]
            for r in range(pivots):
                for c in range(r, pivots):
                    value = jnp.broadcast_to(stacked[r][:, j + c : j + c + 1], (8, W))
                    entry[r][c] = entry[c][r] = value
            entry = sweep(entry, pivots)
            fresh = []
            for r in range(pivots):
                total = entry[r][0] * stacked[0]
                for c in range(1, pivots):
                    total = total + entry[r][c] * stacked[c]
                for c in range(pivots):
                    total = jnp.where(lane_tile == j + c, entry[r][c], total)
                fresh.append(-total)
            for p, head in enumerate(heads):
                rows = [
                    jnp.concatenate([jnp.broadcast_to(row[p : p + 1], (8, W))] * (unit // 8), axis=0)
                    for row in fresh
                ]
                after = jnp.where(lane_head // pivots == j // pivots, 0.0, head)
                for r in range(pivots):
                    after = after - jnp.broadcast_to(head[:, j + r : j + r + 1], (unit, W)) * rows[r]
                for r in range(pivots):
                    after = jnp.where(row_head == j + r, rows[r], after)
                heads[p] = after
        turned = []
        for head, m in zip(heads, held):
            rest = m[unit:]
            rest = jnp.where(lane[unit:] < unit, 0.0, rest) - exact(rest[:, :unit], head)
            turned.append(pltpu.roll(jnp.concatenate([rest, head], axis=0), W - unit, 1))
        return tuple(turned)

    return lax.fori_loop(0, W // unit, panel, tuple(matrices))


def solve_kernel(ridge, stats, new_transition, new_sensing):
    rows = lax.broadcasted_iota(jnp.int32, (W, W), 0)
    lanes = lax.broadcasted_iota(jnp.int32, (W, W), 1)
    eye = jnp.where(rows == lanes, ridge, 0.0).astype(F32)
    lag_a = stats[4 * W : 5 * W]
    lag_b = stats[5 * W : 6 * W]
    half = lax.broadcasted_iota(jnp.int32, (1, W), 1) < W // 2
    def upper(tile):
        return jnp.where(rows <= lanes, tile, 0.0) + jnp.where(rows < lanes, tile, 0.0).T

    def lower(tile, diagonal):
        below = jnp.where(rows > lanes, tile, 0.0)
        return below + below.T + jnp.where(rows == lanes, diagonal, 0.0)

    grams = [upper(lag_a)]
    for tile in range(2):
        packed = stats[tile * W : (tile + 1) * W]
        row = 6 * W - 4 + 2 * tile
        line = jnp.where(half, stats[row : row + 1], pltpu.roll(stats[row + 1 : row + 2], W // 2, 1))
        grams.append(upper(packed))
        grams.append(lower(packed, line))
    done = inverses([gram + eye for gram in grams])
    lag_cross_t = jnp.where(rows > lanes, lag_a, lag_b)
    new_transition[...] = exact(lag_cross_t.T, done[0])
    for tile in range(2):
        cross = stats[(2 + tile) * W : (3 + tile) * W].T
        for side in range(2):
            g = 2 * tile + side
            new_sensing[g * 64 : (g + 1) * 64] = exact(cross[side * 64 : (side + 1) * 64], done[1 + g])


def swap_core(value):
    return lax.ppermute(value, "sens", [(0, 1), (1, 0)])


def exchange(value, stride, count):
    groups = [
        [first + stride * j for j in range(count)]
        for first in range(NEAR * FAR)
        if (first // stride) % count == 0
    ]
    return lax.all_to_all(value, "tm", 0, 0, axis_index_groups=groups, tiled=True)


def on_device(telemetry, present, transition, sensing, filter_gain, smooth_gain, initial_state):
    where = jnp.stack([lax.axis_index("tm"), lax.axis_index("sens")]).astype(jnp.int32)
    flags = present.astype(F32)

    other_gain = swap_core(filter_gain)
    other_sensing = swap_core(sensing)
    other_flags = swap_core(flags)
    mine, theirs = call(push_kernel, [shape(ROWS, W)] * 2, 1, 3, far=(0, 2))(
        where, telemetry, flags, filter_gain
    )
    received = swap_core(theirs)
    powers, tree, whole, gain_powers, drive_map = call(
        maps_kernel,
        [
            shape(SEGS, 5, W, 2 * W, dtype=BF16), shape(SEGS - 1, W, 2 * W, dtype=BF16),
            shape(2 * SEGS - 1, W, W), shape(15, W, 2 * W, dtype=BF16), shape(W, 2 * W, dtype=BF16),
        ],
        3, 6,
        scratch=[pltpu.VMEM((8, W, W), F32), pltpu.VMEM((W, W), F32)],
        far=(0, 1, 3, 5),
    )(where, flags, other_flags, transition, filter_gain, other_gain, sensing, other_sensing, smooth_gain)
    inputs, ends, packed = call(
        shift_kernel, [shape(ROWS, W), shape(32, W), shape(PACK, W)], 0, 5
    )(mine, received, powers, tree, whole)

    other_packed = swap_core(packed)
    (chip,) = call(pair_kernel, [shape(NEAR * PACK, W)], 1, 2)(where, packed, other_packed)
    near = exchange(chip, 1, NEAR)
    group, early = call(eight_kernel, [shape(FAR * PACK, W), shape(3, PACK, W)], 0, 1)(near)
    far = exchange(group, NEAR, FAR)
    drives, final, shift = call(
        filter_kernel, [shape(ROWS, W), shape(8, W), shape(W, W)], 1, 12,
        [pltpu.VMEM((3, PACK, W), F32)],
    )(
        where, far, near, early, other_packed, initial_state.reshape(1, W), inputs, ends, powers, tree,
        gain_powers, drive_map, transition,
    )
    gathered = lax.all_to_all(shift, ("tm", "sens"), 0, 0, tiled=True)
    smoothed, incoming = call(
        smooth_kernel, [shape(ROWS, W), shape(8, W)], 1, 4, [pltpu.VMEM((7, W, W), F32)]
    )(where, gathered, drives, final, gain_powers)
    both = jnp.concatenate([smoothed, incoming], axis=0)
    other_both = swap_core(both)
    smoothed_out, stats = call(
        stats_kernel, [shape(2 * ROWS, W, leaves=True), shape(STATS, W)], 1, 4,
        [pltpu.VMEM((2 * ROWS, W), F32)],
    )(where, telemetry, flags, both, other_both)

    stats = exchange(stats, 1, PLANE)
    (stats,) = call(functools.partial(sum_kernel, PLANE, PLANES), [shape(PLANES * SLICE, W)], 0, 1)(stats)
    stats = exchange(stats, PLANE, PLANES)
    (stats,) = call(functools.partial(sum_kernel, PLANES, PLANE), [shape(STATS, W)], 0, 1)(stats)
    stats = exchange(stats, 1, PLANE)
    ridge = RIDGE * telemetry.shape[0] * lax.axis_size("tm")
    new_transition, new_sensing = call(
        functools.partial(solve_kernel, ridge), [shape(W, W, leaves=True), shape(2 * W, W, leaves=True)], 0, 1
    )(stats)
    return new_transition, new_sensing, smoothed_out


def solution(mesh):
    placed = (P("tm", "sens"), P("tm", "sens"), P(), P("sens", None), P(None, "sens"), P(), P())
    return jax.shard_map(
        on_device,
        mesh=mesh,
        in_specs=placed,
        out_specs=(P(), P("sens", None), P("tm", None)),
        check_vma=False,
    )
```

```python
import functools

import jax
import jax.numpy as jnp
from jax import lax
from jax.experimental import pallas as pl
from jax.experimental.pallas import tpu as pltpu
from jax.sharding import PartitionSpec as P

RIDGE = 0.001
F32 = jnp.float32
BF16 = jnp.bfloat16
W = 128
SEGS = 16
LEN = 16
ROWS = SEGS * LEN
PACK = W + 8
NEAR = 8
FAR = 8
PLANE = 16
PLANES = 4
BATCH = 8
STATS = 6 * W
SLICE = STATS // PLANE
VMEM_LIMIT = 24 * 1024 * 1024


def halves(value):
    high = value.astype(BF16)
    low = (value - high.astype(F32)).astype(BF16)
    return high, low


def wide(value):
    high, low = halves(value)
    return jnp.concatenate([high, low], axis=1)


def times(left_wide, right_wide):
    stacked = jnp.concatenate([right_wide, right_wide], axis=0)
    out = jnp.dot(left_wide, stacked, preferred_element_type=F32)
    return out[:, :W] + out[:, W:]


def moved(rows, dev):
    return rows + times(wide(rows), dev)


def chained(first, second, second_wide):
    return first + second + times(wide(first), second_wide)


def identity():
    rows = lax.broadcasted_iota(jnp.int32, (W, W), 0)
    cols = lax.broadcasted_iota(jnp.int32, (W, W), 1)
    return jnp.where(rows == cols, 1.0, 0.0).astype(F32)


def call(kernel, out_shapes, n_smem, n_in, scratch=(), far=()):
    smem = [pl.BlockSpec(memory_space=pltpu.SMEM)] * n_smem
    vmem = [pl.BlockSpec(memory_space=pltpu.VMEM)] * n_in
    outs = [out if leaves else pltpu.VMEM(out.shape, out.dtype) for out, leaves in out_shapes]
    run = pl.pallas_call(
        kernel,
        out_shape=tuple(outs),
        in_specs=smem + vmem,
        out_specs=tuple([pl.BlockSpec(memory_space=pltpu.VMEM)] * len(outs)),
        scratch_shapes=list(scratch),
        compiler_params=pltpu.CompilerParams(vmem_limit_bytes=VMEM_LIMIT),
    )

    def placed(*operands):
        near = [
            pltpu.with_memory_space_constraint(v, pltpu.HBM if i in far else pltpu.VMEM)
            for i, v in enumerate(operands[n_smem:])
        ]
        return run(*operands[:n_smem], *near)

    return placed


def shape(*dims, dtype=F32, leaves=False):
    return jax.ShapeDtypeStruct(dims, dtype), leaves


def mask_of(flags, rows, first):
    blocks, segs = flags.shape
    spread = (
        lax.broadcasted_iota(jnp.int32, (blocks, 64 * blocks), 0)
        == lax.broadcasted_iota(jnp.int32, (blocks, 64 * blocks), 1) // 64
    )
    by_sensor = lax.dot_general(
        flags.astype(F32).astype(BF16), spread.astype(BF16), (((0,), (0,)), ((), ())),
        preferred_element_type=F32,
    )
    repeat = (
        lax.broadcasted_iota(jnp.int32, (rows, segs), 0) // LEN + first
        == lax.broadcasted_iota(jnp.int32, (rows, segs), 1)
    )
    return jnp.dot(repeat.astype(BF16), by_sensor.astype(BF16), preferred_element_type=F32)


def push_kernel(where, tel, flags, gain, mine, theirs):
    gain_t = gain[...].T
    packed = wide(gain_t)
    for out, core in ((theirs, 1 - where[1]), (mine, where[1])):
        start = pl.multiple_of(core * ROWS, ROWS)
        mask = mask_of(flags[...], ROWS, core * SEGS)
        high, low = halves(tel[pl.ds(start, ROWS), :] * mask)
        total = jnp.dot(high, packed, preferred_element_type=F32) + jnp.dot(
            low, packed, preferred_element_type=F32
        )
        out[...] = total[:, :W] + total[:, W:]


def maps_kernel(
    where, flags_own, flags_other, trans, gain_own, gain_other, sense_own, sense_other, smooth_gain,
    powers, tree, whole, gain_powers, drive_map, removed, single,
):
    a = trans[...]
    a_wide = wide(a)
    lane = lax.broadcasted_iota(jnp.int32, (W, 2 * W), 1) // 64
    for side, (gain, sense) in enumerate(((gain_own, sense_own), (gain_other, sense_other))):
        seen = times(wide(sense[...]), a_wide)
        seen_high, seen_low = halves(seen.T)
        gain_wide = wide(gain[...].T)
        for g in range(4):
            zero = jnp.zeros_like(seen_high)
            part = jnp.dot(
                jnp.where(lane == g, seen_high, zero), gain_wide, preferred_element_type=F32
            ) + jnp.dot(jnp.where(lane == g, seen_low, zero), gain_wide, preferred_element_type=F32)
            removed[side * 4 + g] = part[:, :W] + part[:, W:]
    base = a.T - identity()
    single[...] = base
    gain_dev = smooth_gain[...].T - identity()
    drive_map[...] = wide(-chained(base, gain_dev, wide(gain_dev)))
    batch = BATCH

    def group(i, gain_dev):
        devs = []
        for j in range(batch):
            k = i * batch + j
            row = where[1] * SEGS + k
            dev = single[...]
            for g in range(4):
                dev = dev - flags_own[g, row].astype(F32) * removed[g]
                dev = dev - flags_other[g, row].astype(F32) * removed[4 + g]
            devs.append(dev)
        for level in range(4):
            for j in range(batch):
                packed = wide(devs[j])
                powers[i * batch + j, level] = packed
                devs[j] = 2.0 * devs[j] + times(packed, packed)
            for j in range(batch // 4):
                packed = wide(gain_dev)
                gain_powers[(4 * i + level) * (batch // 4) + j] = packed
                gain_dev = 2.0 * gain_dev + times(packed, packed)
        for j in range(batch):
            powers[i * batch + j, 4] = wide(devs[j])
            whole[i * batch + j] = devs[j]
        return gain_dev

    lax.fori_loop(0, SEGS // batch, group, gain_dev)
    count, base_at, source_at = SEGS, SEGS, 0
    while count > 1:
        for p in range(count // 2):
            second = whole[source_at + 2 * p + 1]
            joined = chained(whole[source_at + 2 * p], second, wide(second))
            whole[base_at + p] = joined
            tree[base_at - SEGS + p] = wide(joined)
        source_at = base_at
        count //= 2
        base_at += count


def seg_scan(rows, powers):
    row_at = lax.broadcasted_iota(jnp.int32, (ROWS, W), 0) % LEN
    for level in range(4):
        reach = 1 << level
        before = jnp.where(row_at >= reach, pltpu.roll(rows, reach, 0), 0.0)
        packed = wide(before)
        parts = [
            times(packed[k * LEN : (k + 1) * LEN], powers[k, level]) for k in range(SEGS)
        ]
        rows = rows + before + jnp.concatenate(parts, axis=0)
    return rows


def shift_kernel(mine, received, powers, tree, whole, inputs, ends, packed):
    rows = mine[...] + received[...]
    inputs[...] = rows
    reached = seg_scan(rows, powers)
    level = [reached[k * LEN + LEN - 1 : (k + 1) * LEN] for k in range(SEGS)]
    ends[0:SEGS] = jnp.concatenate(level, axis=0)
    maps = [powers[k, 4] for k in range(SEGS)]
    at, tree_at = SEGS, 0
    while len(level) > 1:
        level = [
            moved(jnp.broadcast_to(level[2 * p], (8, W)), maps[2 * p + 1])[0:1] + level[2 * p + 1]
            for p in range(len(level) // 2)
        ]
        maps = [tree[tree_at + p] for p in range(len(level))]
        tree_at += len(level)
        for p, row in enumerate(level):
            ends[at + p : at + p + 1] = row
        at += len(level)
    packed[0:W] = whole[2 * SEGS - 2]
    packed[W:PACK] = jnp.broadcast_to(level[0], (PACK - W, W))


def join2(first, second):
    second_dev = second[0:W]
    second_wide = wide(second_dev)
    dev = chained(first[0:W], second_dev, second_wide)
    row = moved(first[W:PACK], second_wide) + second[W:PACK]
    return dev, row


def repeated(out, row, value, copies, rows):
    for j in range(copies):
        out[j * rows + row : j * rows + row + value.shape[0]] = value


def pair_kernel(where, own, other, out):
    core = where[1]
    mine, theirs = own[...], other[...]
    first = jnp.where(core == 0, mine, theirs)
    second = jnp.where(core == 0, theirs, mine)
    dev, row = join2(first, second)
    repeated(out, 0, dev, NEAR, PACK)
    repeated(out, W, row, NEAR, PACK)


def split_maps(raw):
    return [(raw[j * PACK : j * PACK + W], raw[j * PACK + W : (j + 1) * PACK]) for j in range(8)]


def joined(first, second):
    second_wide = wide(second[0])
    return chained(first[0], second[0], second_wide), moved(first[1], second_wide) + second[1]


def eight_kernel(raw, out, early):
    level = split_maps(raw)
    pairs = [joined(level[2 * p], level[2 * p + 1]) for p in range(4)]
    fours = [joined(pairs[0], pairs[1]), joined(pairs[2], pairs[3])]
    dev, row = joined(*fours)
    repeated(out, 0, dev, FAR, PACK)
    repeated(out, W, row, FAR, PACK)
    for slot, (dev, row) in enumerate((fours[0], pairs[0], pairs[2])):
        early[slot, 0:W] = dev
        early[slot, W:PACK] = row


def advance(state, at, raw, early):
    def step(state, used, packed):
        ahead = moved(state, wide(packed[0:W])) + packed[W : W + 8]
        return jnp.where(used, ahead, state)

    state = step(state, at >= 4, early[0])
    state = step(state, (at & 2) != 0, early[1 + (at >> 2)])
    start = pl.multiple_of((at & 6) * PACK, 8)
    return step(state, (at & 1) != 0, raw[pl.ds(start, PACK)])


def power_sum(part, powers, first):
    level = part.shape[0].bit_length() - 2
    while level >= 3:
        half = 1 << level
        part = part[:half] + moved(part[half:], powers[first + level])
        level -= 1
    while level >= 0:
        behind = pltpu.roll(part, 8 - (1 << level), 0)
        part = part + moved(behind, powers[first + level])
        level -= 1
    return part


def filter_kernel(
    where, far, near, early, c1, initial, inputs, ends, powers, tree, gain_powers, drive_map,
    trans, drives, final, shift, far_early,
):
    device, core = where[0], where[1]
    level = split_maps(far)
    pairs = [joined(level[2 * p], level[2 * p + 1]) for p in range(3)]
    for slot, (dev, row) in enumerate((joined(pairs[0], pairs[1]), pairs[0], pairs[2])):
        far_early[slot, 0:W] = dev
        far_early[slot, W:PACK] = row
    state = jnp.broadcast_to(initial[...], (8, W))
    state = advance(state, device // NEAR, far, far_early)
    state = advance(state, device % NEAR, near, early)
    ahead = moved(state, wide(c1[0:W])) + c1[W : W + 8]
    state = jnp.where(core == 1, ahead, state)
    starts = {0: state}
    for span, maps_at, ends_at in ((8, 12, 28), (4, 8, 24), (2, 0, 16), (1, -1, 0)):
        for begin in range(0, SEGS, 2 * span):
            p = begin // span
            dev = powers[p, 4] if span == 1 else tree[maps_at + p]
            starts[begin + span] = moved(starts[begin], dev) + ends[ends_at + p : ends_at + p + 1]
    entry = [moved(starts[k], powers[k, 0]) for k in range(SEGS)]
    spread = jnp.concatenate(
        [part for k in range(SEGS) for part in (entry[k], jnp.zeros((8, W), F32))], axis=0
    )
    row_at = lax.broadcasted_iota(jnp.int32, (ROWS, W), 0) % LEN
    rows = inputs[...] + jnp.where(row_at == 0, spread, 0.0)
    rows = seg_scan(rows, powers)
    drive = times(wide(rows), drive_map[...])
    drives[...] = drive
    last = jnp.broadcast_to(rows[ROWS - 1 : ROWS], (8, W))
    final_row = last + times(wide(last), wide(trans[...].T - identity()))
    final[...] = final_row
    top = (device == NEAR * FAR - 1) & (core == 1)
    part = power_sum(drive, gain_powers, 0)
    from_top = moved(final_row, gain_powers[8])
    own = part[0:1] + jnp.where(top, from_top[0:1], 0.0)
    shift[...] = jnp.broadcast_to(own, (W, W))


def smooth_kernel(where, gathered, drives, final, gain_powers, smoothed, incoming):
    place = 2 * where[0] + where[1]
    later = pltpu.roll(gathered[...], W - 1 - place, 0)
    row = lax.broadcasted_iota(jnp.int32, (W, W), 0)
    later = jnp.where(row < W - 1 - place, later, 0.0)
    state = jnp.broadcast_to(power_sum(later, gain_powers, 8)[0:1], (8, W))
    top = jnp.where(place == W - 1, 1, 0)
    state = jnp.where(top == 1, final[...], state)
    incoming[...] = state
    entry = moved(state, gain_powers[0])
    row_at = lax.broadcasted_iota(jnp.int32, (ROWS, W), 0)
    part = drives[...]
    part = part + jnp.where(row_at == ROWS - 1, jnp.broadcast_to(entry[0:1], (ROWS, W)), 0.0)
    for level in range(8):
        reach = 1 << level
        behind = jnp.where(row_at < ROWS - reach, pltpu.roll(part, ROWS - reach, 0), 0.0)
        part = part + moved(behind, gain_powers[level])
    smoothed[...] = part


def stats_kernel(where, tel, flags, own, other, smoothed, parts, full):
    core = where[1]
    full[pl.ds(pl.multiple_of(core * ROWS, ROWS), ROWS)] = own[0:ROWS]
    full[pl.ds(pl.multiple_of((1 - core) * ROWS, ROWS), ROWS)] = other[0:ROWS]
    rows = full[...]
    smoothed[...] = rows
    count = 2 * ROWS
    after = jnp.where(core == 1, own[ROWS : ROWS + 8], other[ROWS : ROWS + 8])
    row_at = lax.broadcasted_iota(jnp.int32, (count, W), 0)
    following = jnp.where(
        row_at == count - 1, jnp.broadcast_to(after[0:1], (count, W)), pltpu.roll(rows, count - 1, 0)
    )
    packed = wide(rows)
    packed_t = jnp.concatenate([rows.T.astype(BF16), (rows - rows.astype(BF16).astype(F32)).T.astype(BF16)], axis=0)
    last_chip = where[0] == NEAR * FAR - 1
    lane_at = lax.broadcasted_iota(jnp.int32, (2 * W, count), 1)
    kept = jnp.where(last_chip & (lane_at == count - 1), jnp.zeros_like(packed_t), packed_t)

    def fold(out):
        return (out[:W, :W] + out[:W, W:]) + (out[W:, :W] + out[W:, W:])

    upper = lax.broadcasted_iota(jnp.int32, (W, W), 0) - lax.broadcasted_iota(jnp.int32, (W, W), 1)
    lag_gram = fold(jnp.dot(kept, packed, preferred_element_type=F32))
    lag_cross_t = fold(jnp.dot(kept, wide(following), preferred_element_type=F32))
    fl = flags[...]
    repeat = (
        lax.broadcasted_iota(jnp.int32, (2 * SEGS, count), 0)
        == lax.broadcasted_iota(jnp.int32, (2 * SEGS, count), 1) // LEN
    )
    lane_flags = jnp.dot(fl.astype(F32).astype(BF16), repeat.astype(BF16), preferred_element_type=F32)
    grams = []
    for g in range(4):
        masked_t = packed_t * lane_flags[g : g + 1].astype(BF16)
        grams.append(fold(jnp.dot(masked_t, packed, preferred_element_type=F32)))
    def diagonal(gram):
        return jnp.sum(jnp.where(upper == 0, gram, 0.0), axis=0, keepdims=True)

    for tile in range(2):
        parts[tile * W : (tile + 1) * W] = jnp.where(upper <= 0, grams[2 * tile], grams[2 * tile + 1])
    parts[4 * W : 5 * W] = jnp.where(upper <= 0, lag_gram, lag_cross_t)
    parts[5 * W : 6 * W] = jnp.where(upper <= 0, lag_cross_t, 0.0)
    lane = lax.broadcasted_iota(jnp.int32, (1, W), 1)
    for tile in range(2):
        line = diagonal(grams[2 * tile + 1])
        for half in range(2):
            row = 6 * W - 4 + 2 * tile + half
            moved_line = line if half == 0 else pltpu.roll(line, W // 2, 1)
            parts[row : row + 1] = jnp.where(lane < W // 2, moved_line, parts[row : row + 1])
    high, low = halves(tel[...] * mask_of(fl, count, 0))
    cross = jnp.dot(packed_t, high, preferred_element_type=F32) + jnp.dot(
        packed_t, low, preferred_element_type=F32
    )
    cross = cross[:W] + cross[W:]
    parts[2 * W : 3 * W] = cross[:, :W]
    parts[3 * W : 4 * W] = cross[:, W:]

def sum_kernel(count, copies, parts, out):
    rows = SLICE
    total = parts[0:rows]
    for j in range(1, count):
        total = total + parts[j * rows : (j + 1) * rows]
    for j in range(copies):
        out[j * rows : (j + 1) * rows] = total


def exact(left, right):
    return jnp.dot(left, right, precision=lax.Precision.HIGHEST, preferred_element_type=F32)


def sweep(entry, count):
    entry = [list(row) for row in entry]
    for q in range(count):
        scale = 1.0 / entry[q][q]
        row = [entry[q][c] * scale for c in range(count)]
        for r in range(count):
            for c in range(r, count):
                if q not in (r, c):
                    entry[r][c] = entry[r][c] - entry[r][q] * row[c]
        for r in range(count):
            entry[r][q] = entry[q][r] = row[r]
        entry[q][q] = -scale
        for r in range(count):
            for c in range(r):
                entry[r][c] = entry[c][r]
    return entry


def inverses(matrices):
    unit, pivots = 32, 8
    lane = lax.broadcasted_iota(jnp.int32, (W, W), 1)
    lane_tile = lane[:8]
    lane_head = lane[:unit]
    row_head = lax.broadcasted_iota(jnp.int32, (unit, W), 0)
    sublane = lax.broadcasted_iota(jnp.int32, (8, W), 0)

    def panel(b, held):
        heads = [m[:unit] for m in held]
        for j in range(0, unit, pivots):
            stacked = []
            for r in range(pivots):
                rows = jnp.broadcast_to(heads[0][j + r : j + r + 1], (8, W))
                for p in range(1, len(heads)):
                    mine = jnp.broadcast_to(heads[p][j + r : j + r + 1], (8, W))
                    rows = jnp.where(sublane == p, mine, rows)
                stacked.append(rows)
            entry = [[None] * pivots for _ in range(pivots)]
            for r in range(pivots):
                for c in range(r, pivots):
                    value = jnp.broadcast_to(stacked[r][:, j + c : j + c + 1], (8, W))
                    entry[r][c] = entry[c][r] = value
            entry = sweep(entry, pivots)
            fresh = []
            for r in range(pivots):
                total = entry[r][0] * stacked[0]
                for c in range(1, pivots):
                    total = total + entry[r][c] * stacked[c]
                for c in range(pivots):
                    total = jnp.where(lane_tile == j + c, entry[r][c], total)
                fresh.append(-total)
            for p, head in enumerate(heads):
                rows = [
                    jnp.concatenate([jnp.broadcast_to(row[p : p + 1], (8, W))] * (unit // 8), axis=0)
                    for row in fresh
                ]
                after = jnp.where(lane_head // pivots == j // pivots, 0.0, head)
                for r in range(pivots):
                    after = after - jnp.broadcast_to(head[:, j + r : j + r + 1], (unit, W)) * rows[r]
                for r in range(pivots):
                    after = jnp.where(row_head == j + r, rows[r], after)
                heads[p] = after
        turned = []
        for head, m in zip(heads, held):
            rest = m[unit:]
            rest = jnp.where(lane[unit:] < unit, 0.0, rest) - exact(rest[:, :unit], head)
            turned.append(pltpu.roll(jnp.concatenate([rest, head], axis=0), W - unit, 1))
        return tuple(turned)

    return lax.fori_loop(0, W // unit, panel, tuple(matrices))


def solve_kernel(ridge, stats, new_transition, new_sensing):
    rows = lax.broadcasted_iota(jnp.int32, (W, W), 0)
    lanes = lax.broadcasted_iota(jnp.int32, (W, W), 1)
    eye = jnp.where(rows == lanes, ridge, 0.0).astype(F32)
    lag_a = stats[4 * W : 5 * W]
    lag_b = stats[5 * W : 6 * W]
    half = lax.broadcasted_iota(jnp.int32, (1, W), 1) < W // 2
    def upper(tile):
        return jnp.where(rows <= lanes, tile, 0.0) + jnp.where(rows < lanes, tile, 0.0).T

    def lower(tile, diagonal):
        below = jnp.where(rows > lanes, tile, 0.0)
        return below + below.T + jnp.where(rows == lanes, diagonal, 0.0)

    grams = [upper(lag_a)]
    for tile in range(2):
        packed = stats[tile * W : (tile + 1) * W]
        row = 6 * W - 4 + 2 * tile
        line = jnp.where(half, stats[row : row + 1], pltpu.roll(stats[row + 1 : row + 2], W // 2, 1))
        grams.append(upper(packed))
        grams.append(lower(packed, line))
    done = inverses([gram + eye for gram in grams])
    lag_cross_t = jnp.where(rows > lanes, lag_a, lag_b)
    new_transition[...] = exact(lag_cross_t.T, done[0])
    for tile in range(2):
        cross = stats[(2 + tile) * W : (3 + tile) * W].T
        for side in range(2):
            g = 2 * tile + side
            new_sensing[g * 64 : (g + 1) * 64] = exact(cross[side * 64 : (side + 1) * 64], done[1 + g])


def swap_core(value):
    return lax.ppermute(value, "sens", [(0, 1), (1, 0)])


def exchange(value, stride, count):
    groups = [
        [first + stride * j for j in range(count)]
        for first in range(NEAR * FAR)
        if (first // stride) % count == 0
    ]
    return lax.all_to_all(value, "tm", 0, 0, axis_index_groups=groups, tiled=True)


def on_device(telemetry, present, transition, sensing, filter_gain, smooth_gain, initial_state):
    where = jnp.stack([lax.axis_index("tm"), lax.axis_index("sens")]).astype(jnp.int32)
    present = present.T
    other_gain = swap_core(filter_gain)
    other_sensing = swap_core(sensing)
    other_present = swap_core(present)
    mine, theirs = call(push_kernel, [shape(ROWS, W)] * 2, 1, 3, far=(0, 1, 2))(
        where, telemetry, present, filter_gain
    )
    received = swap_core(theirs)
    powers, tree, whole, gain_powers, drive_map = call(
        maps_kernel,
        [
            shape(SEGS, 5, W, 2 * W, dtype=BF16), shape(SEGS - 1, W, 2 * W, dtype=BF16),
            shape(2 * SEGS - 1, W, W), shape(16, W, 2 * W, dtype=BF16), shape(W, 2 * W, dtype=BF16),
        ],
        3, 6,
        scratch=[pltpu.VMEM((8, W, W), F32), pltpu.VMEM((W, W), F32)],
        far=(0, 1, 3, 5),
    )(where, present, other_present, transition, filter_gain, other_gain, sensing, other_sensing, smooth_gain)
    inputs, ends, packed = call(
        shift_kernel, [shape(ROWS, W), shape(32, W), shape(PACK, W)], 0, 5
    )(mine, received, powers, tree, whole)

    other_packed = swap_core(packed)
    (chip,) = call(pair_kernel, [shape(NEAR * PACK, W)], 1, 2)(where, packed, other_packed)
    near = exchange(chip, 1, NEAR)
    group, early = call(eight_kernel, [shape(FAR * PACK, W), shape(3, PACK, W)], 0, 1)(near)
    far = exchange(group, NEAR, FAR)
    drives, final, shift = call(
        filter_kernel, [shape(ROWS, W), shape(8, W), shape(W, W)], 1, 12,
        [pltpu.VMEM((3, PACK, W), F32)],
    )(
        where, far, near, early, other_packed, initial_state.reshape(1, W), inputs, ends, powers, tree,
        gain_powers, drive_map, transition,
    )
    gathered = lax.all_to_all(shift, ("tm", "sens"), 0, 0, tiled=True)
    smoothed, incoming = call(
        smooth_kernel, [shape(ROWS, W), shape(8, W)], 1, 4
    )(where, gathered, drives, final, gain_powers)
    both = jnp.concatenate([smoothed, incoming], axis=0)
    other_both = swap_core(both)
    smoothed_out, stats = call(
        stats_kernel, [shape(2 * ROWS, W, leaves=True), shape(STATS, W)], 1, 4,
        [pltpu.VMEM((2 * ROWS, W), F32)],
    )(where, telemetry, present, both, other_both)

    stats = exchange(stats, 1, PLANE)
    (stats,) = call(functools.partial(sum_kernel, PLANE, PLANES), [shape(PLANES * SLICE, W)], 0, 1)(stats)
    stats = exchange(stats, PLANE, PLANES)
    (stats,) = call(functools.partial(sum_kernel, PLANES, PLANE), [shape(STATS, W)], 0, 1)(stats)
    stats = exchange(stats, 1, PLANE)
    ridge = RIDGE * telemetry.shape[0] * lax.axis_size("tm")
    new_transition, new_sensing = call(
        functools.partial(solve_kernel, ridge), [shape(W, W, leaves=True), shape(2 * W, W, leaves=True)], 0, 1
    )(stats)
    return new_transition, new_sensing, smoothed_out


def solution(mesh):
    placed = (P("tm", "sens"), P("tm", "sens"), P(), P("sens", None), P(None, "sens"), P(), P())
    return jax.shard_map(
        on_device,
        mesh=mesh,
        in_specs=placed,
        out_specs=(P(), P("sens", None), P("tm", None)),
        check_vma=False,
    )
```

```python
import functools

import jax
import jax.numpy as jnp
from jax import lax
from jax.experimental import pallas as pl
from jax.experimental.pallas import tpu as pltpu
from jax.sharding import PartitionSpec as P

RIDGE = 0.001
F32 = jnp.float32
BF16 = jnp.bfloat16
W = 128
SEGS = 16
LEN = 16
ROWS = SEGS * LEN
PACK = W + 8
NEAR = 8
FAR = 8
PLANE = 16
PLANES = 4
STATS = 6 * W
SLICE = STATS // PLANE
VMEM_LIMIT = 24 * 1024 * 1024


def halves(value):
    high = value.astype(BF16)
    low = (value - high.astype(F32)).astype(BF16)
    return high, low


def wide(value):
    high, low = halves(value)
    return jnp.concatenate([high, low], axis=1)


def times(left_wide, right_wide):
    stacked = jnp.concatenate([right_wide, right_wide], axis=0)
    out = jnp.dot(left_wide, stacked, preferred_element_type=F32)
    return out[:, :W] + out[:, W:]


def moved(rows, dev):
    return rows + times(wide(rows), dev)


def chained(first, second, second_wide):
    return first + second + times(wide(first), second_wide)


def identity():
    rows = lax.broadcasted_iota(jnp.int32, (W, W), 0)
    cols = lax.broadcasted_iota(jnp.int32, (W, W), 1)
    return jnp.where(rows == cols, 1.0, 0.0).astype(F32)


def call(kernel, out_shapes, n_smem, n_in, scratch=(), far=(), far_scalars=()):
    smem = [pl.BlockSpec(memory_space=pltpu.SMEM)] * n_smem
    vmem = [pl.BlockSpec(memory_space=pltpu.VMEM)] * n_in
    outs = [out if leaves else pltpu.VMEM(out.shape, out.dtype) for out, leaves in out_shapes]
    run = pl.pallas_call(
        kernel,
        out_shape=tuple(outs),
        in_specs=smem + vmem,
        out_specs=tuple([pl.BlockSpec(memory_space=pltpu.VMEM)] * len(outs)),
        scratch_shapes=list(scratch),
        compiler_params=pltpu.CompilerParams(vmem_limit_bytes=VMEM_LIMIT),
    )

    def placed(*operands):
        near = [
            pltpu.with_memory_space_constraint(v, pltpu.HBM if i in far else pltpu.VMEM)
            for i, v in enumerate(operands[n_smem:])
        ]
        scalars = [
            pltpu.with_memory_space_constraint(v, pltpu.HBM) if i in far_scalars else v
            for i, v in enumerate(operands[:n_smem])
        ]
        return run(*scalars, *near)

    return placed


def shape(*dims, dtype=F32, leaves=False):
    return jax.ShapeDtypeStruct(dims, dtype), leaves


def mask_of(flags, rows, first):
    blocks, segs = flags.shape
    spread = (
        lax.broadcasted_iota(jnp.int32, (blocks, 64 * blocks), 0)
        == lax.broadcasted_iota(jnp.int32, (blocks, 64 * blocks), 1) // 64
    )
    by_sensor = lax.dot_general(
        flags.astype(F32).astype(BF16), spread.astype(BF16), (((0,), (0,)), ((), ())),
        preferred_element_type=F32,
    )
    repeat = (
        lax.broadcasted_iota(jnp.int32, (rows, segs), 0) // LEN + first
        == lax.broadcasted_iota(jnp.int32, (rows, segs), 1)
    )
    return jnp.dot(repeat.astype(BF16), by_sensor.astype(BF16), preferred_element_type=F32)


def push_kernel(where, tel, flags, gain, unused, mine, theirs):
    gain_t = gain[...].T
    packed = wide(gain_t)
    for out, core in ((theirs, 1 - where[1]), (mine, where[1])):
        start = pl.multiple_of(core * ROWS, ROWS)
        mask = mask_of(flags[...], ROWS, core * SEGS)
        high, low = halves(tel[pl.ds(start, ROWS), :] * mask)
        total = jnp.dot(high, packed, preferred_element_type=F32) + jnp.dot(
            low, packed, preferred_element_type=F32
        )
        out[...] = total[:, :W] + total[:, W:]


def maps_kernel(
    where, flags_own, flags_other, trans, gain_own, gain_other, sense_own, sense_other, smooth_gain,
    powers, tree, whole, gain_powers, gain_triples, drive_map, removed, single,
):
    a = trans[...]
    a_wide = wide(a)
    lane = lax.broadcasted_iota(jnp.int32, (W, 2 * W), 1) // 64
    for side, (gain, sense) in enumerate(((gain_own, sense_own), (gain_other, sense_other))):
        seen = times(wide(sense[...]), a_wide)
        seen_high, seen_low = halves(seen.T)
        gain_wide = wide(gain[...].T)
        for g in range(4):
            zero = jnp.zeros_like(seen_high)
            part = jnp.dot(
                jnp.where(lane == g, seen_high, zero), gain_wide, preferred_element_type=F32
            ) + jnp.dot(jnp.where(lane == g, seen_low, zero), gain_wide, preferred_element_type=F32)
            removed[side * 4 + g] = part[:, :W] + part[:, W:]
    base = a.T - identity()
    single[...] = base
    gain_dev = smooth_gain[...].T - identity()
    drive_map[...] = wide(-chained(base, gain_dev, wide(gain_dev)))
    batch = 8

    def group(i, gain_dev):
        devs = []
        for j in range(batch):
            k = i * batch + j
            row = where[1] * SEGS + k
            dev = single[...]
            for g in range(4):
                dev = dev - flags_own[g, row].astype(F32) * removed[g]
                dev = dev - flags_other[g, row].astype(F32) * removed[4 + g]
            devs.append(dev)
        for level in range(4):
            for j in range(batch):
                packed = wide(devs[j])
                powers[i * batch + j, level] = packed
                devs[j] = 2.0 * devs[j] + times(packed, packed)
            packed = wide(gain_dev)
            twice = 2.0 * gain_dev + times(packed, packed)
            twice_packed = wide(twice)
            gain_powers[8 * i + 2 * level] = packed
            gain_powers[8 * i + 2 * level + 1] = twice_packed
            gain_triples[4 * i + level] = wide(chained(gain_dev, twice, twice_packed))
            gain_dev = 2.0 * twice + times(twice_packed, twice_packed)
        for j in range(batch):
            powers[i * batch + j, 4] = wide(devs[j])
            whole[i * batch + j] = devs[j]
        return gain_dev

    lax.fori_loop(0, SEGS // batch, group, gain_dev)
    count, base_at, source_at = SEGS, SEGS, 0
    while count > 1:
        for p in range(count // 2):
            second = whole[source_at + 2 * p + 1]
            joined = chained(whole[source_at + 2 * p], second, wide(second))
            whole[base_at + p] = joined
            tree[base_at - SEGS + p] = wide(joined)
        source_at = base_at
        count //= 2
        base_at += count


def seg_scan(rows, powers):
    row_at = lax.broadcasted_iota(jnp.int32, (ROWS, W), 0) % LEN
    for level in range(4):
        reach = 1 << level
        before = jnp.where(row_at >= reach, pltpu.roll(rows, reach, 0), 0.0)
        packed = wide(before)
        parts = [
            times(packed[k * LEN : (k + 1) * LEN], powers[k, level]) for k in range(SEGS)
        ]
        rows = rows + before + jnp.concatenate(parts, axis=0)
    return rows


def shift_kernel(mine, received, powers, tree, whole, inputs, ends, packed):
    rows = mine[...] + received[...]
    inputs[...] = rows
    reached = seg_scan(rows, powers)
    level = [reached[k * LEN + LEN - 1 : (k + 1) * LEN] for k in range(SEGS)]
    ends[0:SEGS] = jnp.concatenate(level, axis=0)
    maps = [powers[k, 4] for k in range(SEGS)]
    at, tree_at = SEGS, 0
    while len(level) > 1:
        level = [
            moved(jnp.broadcast_to(level[2 * p], (8, W)), maps[2 * p + 1])[0:1] + level[2 * p + 1]
            for p in range(len(level) // 2)
        ]
        maps = [tree[tree_at + p] for p in range(len(level))]
        tree_at += len(level)
        for p, row in enumerate(level):
            ends[at + p : at + p + 1] = row
        at += len(level)
    packed[0:W] = whole[2 * SEGS - 2]
    packed[W:PACK] = jnp.broadcast_to(level[0], (PACK - W, W))


def join2(first, second):
    second_dev = second[0:W]
    second_wide = wide(second_dev)
    dev = chained(first[0:W], second_dev, second_wide)
    row = moved(first[W:PACK], second_wide) + second[W:PACK]
    return dev, row


def repeated(out, row, value, copies, rows):
    for j in range(copies):
        out[j * rows + row : j * rows + row + value.shape[0]] = value


def pair_kernel(where, own, other, out):
    core = where[1]
    mine, theirs = own[...], other[...]
    first = jnp.where(core == 0, mine, theirs)
    second = jnp.where(core == 0, theirs, mine)
    dev, row = join2(first, second)
    repeated(out, 0, dev, NEAR, PACK)
    repeated(out, W, row, NEAR, PACK)


def split_maps(raw):
    return [(raw[j * PACK : j * PACK + W], raw[j * PACK + W : (j + 1) * PACK]) for j in range(8)]


def joined(first, second):
    second_wide = wide(second[0])
    return chained(first[0], second[0], second_wide), moved(first[1], second_wide) + second[1]


def eight_kernel(raw, out, early):
    level = split_maps(raw)
    pairs = [joined(level[2 * p], level[2 * p + 1]) for p in range(4)]
    fours = [joined(pairs[0], pairs[1]), joined(pairs[2], pairs[3])]
    dev, row = joined(*fours)
    repeated(out, 0, dev, FAR, PACK)
    repeated(out, W, row, FAR, PACK)
    for slot, (dev, row) in enumerate((fours[0], pairs[0], pairs[2])):
        early[slot, 0:W] = dev
        early[slot, W:PACK] = row


def stages(at, raw, early):
    start = pl.multiple_of((at & 6) * PACK, 8)
    packed = (
        (at >= 4, early[0]), ((at & 2) != 0, early[1 + (at >> 2)]), ((at & 1) != 0, raw[pl.ds(start, PACK)])
    )
    return [masked(used, value) for used, value in packed]


def masked(used, packed):
    packed = jnp.where(used, packed, 0.0)
    return packed[0:W], packed[W : W + 8]


def after_map(state, joined_map):
    return moved(state, wide(joined_map[0])) + joined_map[1]


def moved_sum(first, others, devs):
    total = first
    for rows in others:
        total = total + rows
    left = jnp.concatenate([wide(rows) for rows in others], axis=1)
    right = jnp.concatenate([part for dev in devs for part in (dev, dev)], axis=0)
    out = jnp.dot(left, right, preferred_element_type=F32)
    return total + (out[:, :W] + out[:, W:])


def power_sum(part, powers, triples, first):
    level = part.shape[0].bit_length() - 1
    if level % 2:
        level -= 1
        half = 1 << level
        part = moved_sum(part[:half], [part[half:]], [powers[first + level]])
    while level:
        level -= 2
        span = 1 << level
        devs = [powers[first + level], powers[first + level + 1], triples[(first + level) // 2]]
        if span >= 8:
            pieces = [part[q * span : (q + 1) * span] for q in range(4)]
        elif span == 4:
            near, far = part[:8], part[8:]
            pieces = [near, pltpu.roll(near, 4, 0), far, pltpu.roll(far, 4, 0)]
        else:
            pieces = [part] + [pltpu.roll(part, 8 - q * span, 0) for q in (1, 2, 3)]
        part = moved_sum(pieces[0], pieces[1:], devs)
    return part


def filter_kernel(
    where, far, near, early, c1, initial, inputs, ends, powers, tree, gain_powers, gain_triples, drive_map,
    trans, drives, shift, far_early,
):
    device, core = where[0], where[1]
    level = split_maps(far)
    pairs = [joined(level[2 * p], level[2 * p + 1]) for p in range(3)]
    for slot, (dev, row) in enumerate((joined(pairs[0], pairs[1]), pairs[0], pairs[2])):
        far_early[slot, 0:W] = dev
        far_early[slot, W:PACK] = row
    state = jnp.broadcast_to(initial[...], (8, W))
    for stage in stages(device // NEAR, far, far_early):
        state = after_map(state, stage)
    inner = stages(device % NEAR, near, early)
    inner.append(masked(core == 1, c1[...]))
    state = after_map(state, joined(joined(inner[0], inner[1]), joined(inner[2], inner[3])))
    starts = {0: state}
    for span, maps_at, ends_at in ((8, 12, 28), (4, 8, 24), (2, 0, 16), (1, -1, 0)):
        for begin in range(0, SEGS, 2 * span):
            p = begin // span
            dev = powers[p, 4] if span == 1 else tree[maps_at + p]
            starts[begin + span] = moved(starts[begin], dev) + ends[ends_at + p : ends_at + p + 1]
    entry = [moved(starts[k], powers[k, 0]) for k in range(SEGS)]
    spread = jnp.concatenate(
        [part for k in range(SEGS) for part in (entry[k], jnp.zeros((8, W), F32))], axis=0
    )
    row_at = lax.broadcasted_iota(jnp.int32, (ROWS, W), 0) % LEN
    rows = inputs[...] + jnp.where(row_at == 0, spread, 0.0)
    rows = seg_scan(rows, powers)
    drive = times(wide(rows), drive_map[...])
    drives[0:ROWS] = drive
    last = jnp.broadcast_to(rows[ROWS - 1 : ROWS], (8, W))
    final_row = last + times(wide(last), wide(trans[...].T - identity()))
    drives[ROWS : ROWS + 8] = final_row
    top = (device == NEAR * FAR - 1) & (core == 1)
    part = power_sum(drive, gain_powers, gain_triples, 0)
    from_top = moved(final_row, gain_powers[8])
    own = part[0:1] + jnp.where(top, from_top[0:1], 0.0)
    shift[...] = jnp.broadcast_to(own, (W, W))


def stats_kernel(
    where, gathered, own, other, gain_powers, gain_triples, tel, flags, smoothed, parts, full,
):
    core = where[1]
    count = 2 * ROWS
    place = 2 * where[0] + 1
    later = pltpu.roll(gathered[...], W - 1 - place, 0)
    row = lax.broadcasted_iota(jnp.int32, (W, W), 0)
    later = jnp.where(row < W - 1 - place, later, 0.0)
    state = jnp.broadcast_to(power_sum(later, gain_powers, gain_triples, 8)[0:1], (8, W))
    final = jnp.where(core == 1, own[ROWS : ROWS + 8], other[ROWS : ROWS + 8])
    state = jnp.where(place == W - 1, final, state)
    full[pl.ds(pl.multiple_of(core * ROWS, ROWS), ROWS)] = own[0:ROWS]
    full[pl.ds(pl.multiple_of((1 - core) * ROWS, ROWS), ROWS)] = other[0:ROWS]
    row_at = lax.broadcasted_iota(jnp.int32, (count, W), 0)
    entry = moved(state, gain_powers[0])
    rows = full[...]
    rows = rows + jnp.where(row_at == count - 1, jnp.broadcast_to(entry[0:1], (count, W)), 0.0)

    def behind(rows, reach):
        return jnp.where(row_at < count - reach, pltpu.roll(rows, count - reach, 0), 0.0)

    for level in (0, 2, 4, 6):
        three = [behind(rows, q << level) for q in (1, 2, 3)]
        rows = moved_sum(rows, three, [gain_powers[level], gain_powers[level + 1], gain_triples[level // 2]])
    half = moved(rows[ROWS:], gain_powers[8])
    rows = jnp.concatenate([rows[:ROWS] + half, rows[ROWS:]], axis=0)
    smoothed[...] = rows
    following = jnp.where(
        row_at == count - 1, jnp.broadcast_to(state[0:1], (count, W)), pltpu.roll(rows, count - 1, 0)
    )
    packed = wide(rows)
    high = rows.astype(BF16)
    packed_t = jnp.concatenate([rows.T.astype(BF16), (rows - high.astype(F32)).T.astype(BF16)], axis=0)
    last_chip = where[0] == NEAR * FAR - 1
    lane_at = lax.broadcasted_iota(jnp.int32, (2 * W, count), 1)
    kept = jnp.where(last_chip & (lane_at == count - 1), jnp.zeros_like(packed_t), packed_t)

    def fold(out):
        return (out[:W, :W] + out[:W, W:]) + (out[W:, :W] + out[W:, W:])

    upper = lax.broadcasted_iota(jnp.int32, (W, W), 0) - lax.broadcasted_iota(jnp.int32, (W, W), 1)
    lag_gram = fold(jnp.dot(kept, packed, preferred_element_type=F32))
    lag_cross_t = fold(jnp.dot(kept, wide(following), preferred_element_type=F32))
    fl = flags[...]
    repeat = (
        lax.broadcasted_iota(jnp.int32, (2 * SEGS, count), 0)
        == lax.broadcasted_iota(jnp.int32, (2 * SEGS, count), 1) // LEN
    )
    lane_flags = jnp.dot(fl.astype(F32).astype(BF16), repeat.astype(BF16), preferred_element_type=F32)
    grams = []
    for g in range(4):
        masked_t = packed_t * lane_flags[g : g + 1].astype(BF16)
        grams.append(fold(jnp.dot(masked_t, packed, preferred_element_type=F32)))
    def diagonal(gram):
        return jnp.sum(jnp.where(upper == 0, gram, 0.0), axis=0, keepdims=True)

    for tile in range(2):
        parts[tile * W : (tile + 1) * W] = jnp.where(upper <= 0, grams[2 * tile], grams[2 * tile + 1])
    parts[4 * W : 5 * W] = jnp.where(upper <= 0, lag_gram, lag_cross_t)
    parts[5 * W : 6 * W] = jnp.where(upper <= 0, lag_cross_t, 0.0)
    lane = lax.broadcasted_iota(jnp.int32, (1, W), 1)
    for tile in range(2):
        line = diagonal(grams[2 * tile + 1])
        for half in range(2):
            row = 6 * W - 4 + 2 * tile + half
            moved_line = line if half == 0 else pltpu.roll(line, W // 2, 1)
            parts[row : row + 1] = jnp.where(lane < W // 2, moved_line, parts[row : row + 1])
    high, low = halves(tel[...] * mask_of(fl, count, 0))
    cross = jnp.dot(packed_t, high, preferred_element_type=F32) + jnp.dot(
        packed_t, low, preferred_element_type=F32
    )
    cross = cross[:W] + cross[W:]
    parts[2 * W : 3 * W] = cross[:, :W]
    parts[3 * W : 4 * W] = cross[:, W:]

def sum_kernel(count, copies, parts, out):
    rows = SLICE
    total = parts[0:rows]
    for j in range(1, count):
        total = total + parts[j * rows : (j + 1) * rows]
    for j in range(copies):
        out[j * rows : (j + 1) * rows] = total


def exact(left, right):
    return jnp.dot(left, right, precision=lax.Precision.HIGHEST, preferred_element_type=F32)


def sweep(entry, count):
    entry = [list(row) for row in entry]
    for q in range(count):
        scale = 1.0 / entry[q][q]
        row = [entry[q][c] * scale for c in range(count)]
        for r in range(count):
            for c in range(r, count):
                if q not in (r, c):
                    entry[r][c] = entry[r][c] - entry[r][q] * row[c]
        for r in range(count):
            entry[r][q] = entry[q][r] = row[r]
        entry[q][q] = -scale
        for r in range(count):
            for c in range(r):
                entry[r][c] = entry[c][r]
    return entry


def inverses(matrices):
    unit, pivots = 32, 8
    lane = lax.broadcasted_iota(jnp.int32, (W, W), 1)
    lane_tile = lane[:8]
    lane_head = lane[:unit]
    row_head = lax.broadcasted_iota(jnp.int32, (unit, W), 0)
    sublane = lax.broadcasted_iota(jnp.int32, (8, W), 0)

    def panel(b, held):
        heads = [m[:unit] for m in held]
        for j in range(0, unit, pivots):
            stacked = []
            for r in range(pivots):
                rows = jnp.broadcast_to(heads[0][j + r : j + r + 1], (8, W))
                for p in range(1, len(heads)):
                    mine = jnp.broadcast_to(heads[p][j + r : j + r + 1], (8, W))
                    rows = jnp.where(sublane == p, mine, rows)
                stacked.append(rows)
            entry = [[None] * pivots for _ in range(pivots)]
            for r in range(pivots):
                for c in range(r, pivots):
                    value = jnp.broadcast_to(stacked[r][:, j + c : j + c + 1], (8, W))
                    entry[r][c] = entry[c][r] = value
            entry = sweep(entry, pivots)
            fresh = []
            for r in range(pivots):
                total = entry[r][0] * stacked[0]
                for c in range(1, pivots):
                    total = total + entry[r][c] * stacked[c]
                for c in range(pivots):
                    total = jnp.where(lane_tile == j + c, entry[r][c], total)
                fresh.append(-total)
            for p, head in enumerate(heads):
                rows = [
                    jnp.concatenate([jnp.broadcast_to(row[p : p + 1], (8, W))] * (unit // 8), axis=0)
                    for row in fresh
                ]
                after = jnp.where(lane_head // pivots == j // pivots, 0.0, head)
                for r in range(pivots):
                    after = after - jnp.broadcast_to(head[:, j + r : j + r + 1], (unit, W)) * rows[r]
                for r in range(pivots):
                    after = jnp.where(row_head == j + r, rows[r], after)
                heads[p] = after
        turned = []
        for head, m in zip(heads, held):
            rest = m[unit:]
            rest = jnp.where(lane[unit:] < unit, 0.0, rest) - exact(rest[:, :unit], head)
            turned.append(pltpu.roll(jnp.concatenate([rest, head], axis=0), W - unit, 1))
        return tuple(turned)

    return lax.fori_loop(0, W // unit, panel, tuple(matrices))


def solve_kernel(ridge, stats, new_transition, new_sensing):
    rows = lax.broadcasted_iota(jnp.int32, (W, W), 0)
    lanes = lax.broadcasted_iota(jnp.int32, (W, W), 1)
    eye = jnp.where(rows == lanes, ridge, 0.0).astype(F32)
    lag_a = stats[4 * W : 5 * W]
    lag_b = stats[5 * W : 6 * W]
    half = lax.broadcasted_iota(jnp.int32, (1, W), 1) < W // 2
    def upper(tile):
        return jnp.where(rows <= lanes, tile, 0.0) + jnp.where(rows < lanes, tile, 0.0).T

    def lower(tile, diagonal):
        below = jnp.where(rows > lanes, tile, 0.0)
        return below + below.T + jnp.where(rows == lanes, diagonal, 0.0)

    grams = [upper(lag_a)]
    for tile in range(2):
        packed = stats[tile * W : (tile + 1) * W]
        row = 6 * W - 4 + 2 * tile
        line = jnp.where(half, stats[row : row + 1], pltpu.roll(stats[row + 1 : row + 2], W // 2, 1))
        grams.append(upper(packed))
        grams.append(lower(packed, line))
    done = inverses([gram + eye for gram in grams])
    lag_cross_t = jnp.where(rows > lanes, lag_a, lag_b)
    new_transition[...] = exact(lag_cross_t.T, done[0])
    for tile in range(2):
        cross = stats[(2 + tile) * W : (3 + tile) * W].T
        for side in range(2):
            g = 2 * tile + side
            new_sensing[g * 64 : (g + 1) * 64] = exact(cross[side * 64 : (side + 1) * 64], done[1 + g])


def swap_core(value):
    return lax.ppermute(value, "sens", [(0, 1), (1, 0)])


def exchange(value, stride, count):
    groups = [
        [first + stride * j for j in range(count)]
        for first in range(NEAR * FAR)
        if (first // stride) % count == 0
    ]
    return lax.all_to_all(value, "tm", 0, 0, axis_index_groups=groups, tiled=True)


def on_device(telemetry, present, transition, sensing, filter_gain, smooth_gain, initial_state):
    where = jnp.stack([lax.axis_index("tm"), lax.axis_index("sens")]).astype(jnp.int32)
    present = present.T
    other_gain = swap_core(filter_gain)
    other_sensing = swap_core(sensing)
    other_present = swap_core(present)
    mine, theirs = call(push_kernel, [shape(ROWS, W)] * 2, 1, 4, far=(0, 1, 2))(
        where, telemetry, present, filter_gain, other_present
    )
    received = swap_core(theirs)
    powers, tree, whole, gain_powers, gain_triples, drive_map = call(
        maps_kernel,
        [
            shape(SEGS, 5, W, 2 * W, dtype=BF16), shape(SEGS - 1, W, 2 * W, dtype=BF16),
            shape(2 * SEGS - 1, W, W), shape(16, W, 2 * W, dtype=BF16), shape(8, W, 2 * W, dtype=BF16),
            shape(W, 2 * W, dtype=BF16),
        ],
        3, 6,
        scratch=[pltpu.VMEM((8, W, W), F32), pltpu.VMEM((W, W), F32)],
        far=(0, 1, 3, 5),
        far_scalars=(1,),
    )(where, present, other_present, transition, filter_gain, other_gain, sensing, other_sensing, smooth_gain)
    inputs, ends, packed = call(
        shift_kernel, [shape(ROWS, W), shape(32, W), shape(PACK, W)], 0, 5
    )(mine, received, powers, tree, whole)

    other_packed = swap_core(packed)
    (chip,) = call(pair_kernel, [shape(NEAR * PACK, W)], 1, 2)(where, packed, other_packed)
    near = exchange(chip, 1, NEAR)
    group, early = call(eight_kernel, [shape(FAR * PACK, W), shape(3, PACK, W)], 0, 1)(near)
    far = exchange(group, NEAR, FAR)
    drives, shift = call(
        filter_kernel, [shape(ROWS + 8, W), shape(W, W)], 1, 13, [pltpu.VMEM((3, PACK, W), F32)]
    )(
        where, far, near, early, other_packed, initial_state.reshape(1, W), inputs, ends, powers, tree,
        gain_powers, gain_triples, drive_map, transition,
    )
    other_drives = swap_core(drives)
    gathered = lax.all_to_all(shift, ("tm", "sens"), 0, 0, tiled=True)
    smoothed, stats = call(
        stats_kernel, [shape(2 * ROWS, W, leaves=True), shape(STATS, W)], 1, 7,
        [pltpu.VMEM((2 * ROWS, W), F32)],
    )(where, gathered, drives, other_drives, gain_powers, gain_triples, telemetry, present)

    stats = exchange(stats, 1, PLANE)
    (stats,) = call(functools.partial(sum_kernel, PLANE, PLANES), [shape(PLANES * SLICE, W)], 0, 1)(stats)
    stats = exchange(stats, PLANE, PLANES)
    (stats,) = call(functools.partial(sum_kernel, PLANES, PLANE), [shape(STATS, W)], 0, 1)(stats)
    stats = exchange(stats, 1, PLANE)
    ridge = RIDGE * telemetry.shape[0] * lax.axis_size("tm")
    new_transition, new_sensing = call(
        functools.partial(solve_kernel, ridge), [shape(W, W, leaves=True), shape(2 * W, W, leaves=True)], 0, 1
    )(stats)
    return new_transition, new_sensing, smoothed


def solution(mesh):
    placed = (P("tm", "sens"), P("tm", "sens"), P(), P("sens", None), P(None, "sens"), P(), P())
    return jax.shard_map(
        on_device,
        mesh=mesh,
        in_specs=placed,
        out_specs=(P(), P("sens", None), P("tm", None)),
        check_vma=False,
    )
```

```python
import functools

import jax
import jax.numpy as jnp
from jax import lax
from jax.experimental import pallas as pl
from jax.experimental.pallas import tpu as pltpu
from jax.sharding import PartitionSpec as P

RIDGE = 0.001
F32 = jnp.float32
BF16 = jnp.bfloat16
W = 128
SEGS = 16
LEN = 16
ROWS = SEGS * LEN
PACK = W + 8
NEAR = 8
FAR = 8
PLANE = 16
PLANES = 4
STATS = 6 * W
SLICE = STATS // PLANE
VMEM_LIMIT = 24 * 1024 * 1024


def halves(value):
    high = value.astype(BF16)
    low = (value - high.astype(F32)).astype(BF16)
    return high, low


def wide(value):
    high, low = halves(value)
    return jnp.concatenate([high, low], axis=1)


def times(left_wide, right_wide):
    stacked = jnp.concatenate([right_wide, right_wide], axis=0)
    out = jnp.dot(left_wide, stacked, preferred_element_type=F32)
    return out[:, :W] + out[:, W:]


def moved(rows, dev):
    return rows + times(wide(rows), dev)


def chained(first, second, second_wide):
    return first + second + times(wide(first), second_wide)


def identity():
    rows = lax.broadcasted_iota(jnp.int32, (W, W), 0)
    cols = lax.broadcasted_iota(jnp.int32, (W, W), 1)
    return jnp.where(rows == cols, 1.0, 0.0).astype(F32)


def call(kernel, out_shapes, n_smem, n_in, scratch=(), far=(), far_scalars=()):
    smem = [pl.BlockSpec(memory_space=pltpu.SMEM)] * n_smem
    vmem = [pl.BlockSpec(memory_space=pltpu.VMEM)] * n_in
    outs = [out if leaves else pltpu.VMEM(out.shape, out.dtype) for out, leaves in out_shapes]
    run = pl.pallas_call(
        kernel,
        out_shape=tuple(outs),
        in_specs=smem + vmem,
        out_specs=tuple([pl.BlockSpec(memory_space=pltpu.VMEM)] * len(outs)),
        scratch_shapes=list(scratch),
        compiler_params=pltpu.CompilerParams(vmem_limit_bytes=VMEM_LIMIT),
    )

    def placed(*operands):
        near = [
            pltpu.with_memory_space_constraint(v, pltpu.HBM if i in far else pltpu.VMEM)
            for i, v in enumerate(operands[n_smem:])
        ]
        scalars = [
            pltpu.with_memory_space_constraint(v, pltpu.HBM) if i in far_scalars else v
            for i, v in enumerate(operands[:n_smem])
        ]
        return run(*scalars, *near)

    return placed


def shape(*dims, dtype=F32, leaves=False):
    return jax.ShapeDtypeStruct(dims, dtype), leaves


def mask_of(flags, rows, first):
    blocks, segs = flags.shape
    spread = (
        lax.broadcasted_iota(jnp.int32, (blocks, 64 * blocks), 0)
        == lax.broadcasted_iota(jnp.int32, (blocks, 64 * blocks), 1) // 64
    )
    by_sensor = lax.dot_general(
        flags.astype(F32).astype(BF16), spread.astype(BF16), (((0,), (0,)), ((), ())),
        preferred_element_type=F32,
    )
    repeat = (
        lax.broadcasted_iota(jnp.int32, (rows, segs), 0) // LEN + first
        == lax.broadcasted_iota(jnp.int32, (rows, segs), 1)
    )
    return jnp.dot(repeat.astype(BF16), by_sensor.astype(BF16), preferred_element_type=F32)


def push_kernel(where, tel, flags, gain, unused, mine, theirs):
    gain_t = gain[...].T
    packed = wide(gain_t)
    for out, core in ((theirs, 1 - where[1]), (mine, where[1])):
        start = pl.multiple_of(core * ROWS, ROWS)
        mask = mask_of(flags[...], ROWS, core * SEGS)
        high, low = halves(tel[pl.ds(start, ROWS), :] * mask)
        total = jnp.dot(high, packed, preferred_element_type=F32) + jnp.dot(
            low, packed, preferred_element_type=F32
        )
        out[...] = total[:, :W] + total[:, W:]


def maps_kernel(
    where, flags_own, flags_other, trans, gain_own, gain_other, sense_own, sense_other, smooth_gain,
    powers, whole, gain_powers, gain_triples, drive_map, removed, single,
):
    a = trans[...]
    a_wide = wide(a)
    lane = lax.broadcasted_iota(jnp.int32, (W, 2 * W), 1) // 64
    for side, (gain, sense) in enumerate(((gain_own, sense_own), (gain_other, sense_other))):
        seen = times(wide(sense[...]), a_wide)
        seen_high, seen_low = halves(seen.T)
        gain_wide = wide(gain[...].T)
        zero = jnp.zeros_like(seen_high)
        blocks = [jnp.where(lane == g, part, zero) for g in range(4) for part in (seen_high, seen_low)]
        product = jnp.dot(jnp.concatenate(blocks, axis=0), gain_wide, preferred_element_type=F32)
        for g in range(4):
            part = product[2 * g * W : (2 * g + 1) * W] + product[(2 * g + 1) * W : (2 * g + 2) * W]
            removed[side * 4 + g] = part[:, :W] + part[:, W:]
    base = a.T - identity()
    single[...] = base
    gain_dev = smooth_gain[...].T - identity()
    drive_map[...] = wide(-chained(base, gain_dev, wide(gain_dev)))
    batch = 8

    def group(i, gain_dev):
        devs = []
        for j in range(batch):
            k = i * batch + j
            row = where[1] * SEGS + k
            dev = single[...]
            for g in range(4):
                dev = dev - flags_own[g, row].astype(F32) * removed[g]
                dev = dev - flags_other[g, row].astype(F32) * removed[4 + g]
            devs.append(dev)
        for level in range(4):
            for j in range(batch):
                packed = wide(devs[j])
                powers[i * batch + j, level] = packed
                devs[j] = 2.0 * devs[j] + times(packed, packed)
            packed = wide(gain_dev)
            twice = 2.0 * gain_dev + times(packed, packed)
            twice_packed = wide(twice)
            gain_powers[8 * i + 2 * level] = packed
            gain_powers[8 * i + 2 * level + 1] = twice_packed
            gain_triples[4 * i + level] = wide(chained(gain_dev, twice, twice_packed))
            gain_dev = 2.0 * twice + times(twice_packed, twice_packed)
        for j in range(batch):
            powers[i * batch + j, 4] = wide(devs[j])
            whole[i * batch + j] = devs[j]
        return gain_dev

    lax.fori_loop(0, SEGS // batch, group, gain_dev)


def seg_step(rows, powers, level, starts=None):
    row_at = lax.broadcasted_iota(jnp.int32, (ROWS, W), 0) % LEN
    reach = 1 << level
    before = jnp.where(row_at >= reach, pltpu.roll(rows, reach, 0), 0.0)
    if starts is not None:
        before = jnp.where(row_at == reach - 1, starts, before)
    packed = wide(before)
    parts = [times(packed[k * LEN : (k + 1) * LEN], powers[k, level]) for k in range(SEGS)]
    return rows + before + jnp.concatenate(parts, axis=0)


def shift_kernel(mine, received, powers, whole, inputs, ends, packed, tree):
    rows = mine[...] + received[...]
    inputs[...] = rows
    devs = [whole[k] for k in range(SEGS)]
    at = 0
    composite = []
    reached = rows
    for step in range(4):
        devs = [
            chained(devs[2 * p], devs[2 * p + 1], wide(devs[2 * p + 1])) for p in range(len(devs) // 2)
        ]
        reached = seg_step(reached, powers, step)
        for p, dev in enumerate(devs):
            dev_wide = wide(dev)
            composite.append(dev_wide)
            tree[at + p] = dev_wide
        at += len(devs)
    level = [reached[k * LEN + LEN - 1 : (k + 1) * LEN] for k in range(SEGS)]
    ends[0:SEGS] = jnp.concatenate(level, axis=0)
    maps = [powers[k, 4] for k in range(SEGS)]
    at, tree_at = SEGS, 0
    while len(level) > 1:
        level = [
            moved(jnp.broadcast_to(level[2 * p], (8, W)), maps[2 * p + 1])[0:1] + level[2 * p + 1]
            for p in range(len(level) // 2)
        ]
        maps = composite[tree_at : tree_at + len(level)]
        tree_at += len(level)
        for p, row in enumerate(level):
            ends[at + p : at + p + 1] = row
        at += len(level)
    packed[0:W] = devs[0]
    packed[W:PACK] = jnp.broadcast_to(level[0], (PACK - W, W))


def join2(first, second):
    second_dev = second[0:W]
    second_wide = wide(second_dev)
    dev = chained(first[0:W], second_dev, second_wide)
    row = moved(first[W:PACK], second_wide) + second[W:PACK]
    return dev, row


def repeated(out, row, value, copies, rows):
    for j in range(copies):
        out[j * rows + row : j * rows + row + value.shape[0]] = value


def pair_kernel(where, own, other, out):
    core = where[1]
    mine, theirs = own[...], other[...]
    first = jnp.where(core == 0, mine, theirs)
    second = jnp.where(core == 0, theirs, mine)
    dev, row = join2(first, second)
    repeated(out, 0, dev, NEAR, PACK)
    repeated(out, W, row, NEAR, PACK)


def split_maps(raw):
    return [(raw[j * PACK : j * PACK + W], raw[j * PACK + W : (j + 1) * PACK]) for j in range(8)]


def joined(first, second):
    second_wide = wide(second[0])
    return chained(first[0], second[0], second_wide), moved(first[1], second_wide) + second[1]


def eight_kernel(raw, out, early):
    level = split_maps(raw)
    pairs = [joined(level[2 * p], level[2 * p + 1]) for p in range(4)]
    fours = [joined(pairs[0], pairs[1]), joined(pairs[2], pairs[3])]
    dev, row = joined(*fours)
    repeated(out, 0, dev, FAR, PACK)
    repeated(out, W, row, FAR, PACK)
    for slot, (dev, row) in enumerate((fours[0], pairs[0], pairs[2])):
        early[slot, 0:W] = dev
        early[slot, W:PACK] = row


def stages(at, raw, early):
    start = pl.multiple_of((at & 6) * PACK, 8)
    packed = (
        (at >= 4, early[0]), ((at & 2) != 0, early[1 + (at >> 2)]), ((at & 1) != 0, raw[pl.ds(start, PACK)])
    )
    return [masked(used, value) for used, value in packed]


def masked(used, packed):
    packed = jnp.where(used, packed, 0.0)
    return packed[0:W], packed[W : W + 8]


def after_map(state, joined_map):
    return moved(state, wide(joined_map[0])) + joined_map[1]


def moved_sum(first, others, devs):
    total = first
    for rows in others:
        total = total + rows
    left = jnp.concatenate([wide(rows) for rows in others], axis=1)
    right = jnp.concatenate([part for dev in devs for part in (dev, dev)], axis=0)
    out = jnp.dot(left, right, preferred_element_type=F32)
    return total + (out[:, :W] + out[:, W:])


def power_sum(part, powers, triples, first):
    level = part.shape[0].bit_length() - 1
    if level % 2:
        level -= 1
        half = 1 << level
        part = moved_sum(part[:half], [part[half:]], [powers[first + level]])
    while level:
        level -= 2
        span = 1 << level
        devs = [powers[first + level], powers[first + level + 1], triples[(first + level) // 2]]
        if span >= 8:
            pieces = [part[q * span : (q + 1) * span] for q in range(4)]
        elif span == 4:
            near, far = part[:8], part[8:]
            pieces = [near, pltpu.roll(near, 4, 0), far, pltpu.roll(far, 4, 0)]
        else:
            pieces = [part] + [pltpu.roll(part, 8 - q * span, 0) for q in (1, 2, 3)]
        part = moved_sum(pieces[0], pieces[1:], devs)
    return part


def filter_kernel(
    where, far, near, early, c1, initial, inputs, ends, powers, tree, gain_powers, gain_triples, drive_map,
    trans, drives, shift, far_early,
):
    device, core = where[0], where[1]
    level = split_maps(far)
    pairs = [joined(level[2 * p], level[2 * p + 1]) for p in range(3)]
    for slot, (dev, row) in enumerate((joined(pairs[0], pairs[1]), pairs[0], pairs[2])):
        far_early[slot, 0:W] = dev
        far_early[slot, W:PACK] = row
    state = jnp.broadcast_to(initial[...], (8, W))
    for stage in stages(device // NEAR, far, far_early):
        state = after_map(state, stage)
    inner = stages(device % NEAR, near, early)
    inner.append(masked(core == 1, c1[...]))
    state = after_map(state, joined(joined(inner[0], inner[1]), joined(inner[2], inner[3])))
    starts = {0: state}
    for span, maps_at, ends_at in ((8, 12, 28), (4, 8, 24), (2, 0, 16), (1, -1, 0)):
        for begin in range(0, SEGS, 2 * span):
            p = begin // span
            dev = powers[p, 4] if span == 1 else tree[maps_at + p]
            starts[begin + span] = moved(starts[begin], dev) + ends[ends_at + p : ends_at + p + 1]
    starts[SEGS] = moved(starts[SEGS - 1], powers[SEGS - 1, 4]) + ends[SEGS - 1 : SEGS]

    def spread(first):
        return jnp.concatenate([starts[first + k] for k in range(SEGS) for half in range(2)], axis=0)

    entry = spread(0)
    rows = inputs[...]
    for step in range(4):
        rows = seg_step(rows, powers, step, entry)
    row_at = lax.broadcasted_iota(jnp.int32, (ROWS, W), 0) % LEN
    rows = jnp.where(row_at == LEN - 1, spread(1), rows)
    drive = times(wide(rows), drive_map[...])
    drives[0:ROWS] = drive
    last = jnp.broadcast_to(rows[ROWS - 1 : ROWS], (8, W))
    final_row = last + times(wide(last), wide(trans[...].T - identity()))
    drives[ROWS : ROWS + 8] = final_row
    top = (device == NEAR * FAR - 1) & (core == 1)
    part = power_sum(drive, gain_powers, gain_triples, 0)
    from_top = moved(final_row, gain_powers[8])
    own = part[0:1] + jnp.where(top, from_top[0:1], 0.0)
    shift[...] = jnp.broadcast_to(own, (W, W))


def stats_kernel(
    where, gathered, own, other, gain_powers, gain_triples, tel, flags, smoothed, parts, full,
):
    core = where[1]
    count = 2 * ROWS
    place = 2 * where[0] + 1
    later = pltpu.roll(gathered[...], W - 1 - place, 0)
    row = lax.broadcasted_iota(jnp.int32, (W, W), 0)
    later = jnp.where(row < W - 1 - place, later, 0.0)
    state = jnp.broadcast_to(power_sum(later, gain_powers, gain_triples, 8)[0:1], (8, W))
    final = jnp.where(core == 1, own[ROWS : ROWS + 8], other[ROWS : ROWS + 8])
    state = jnp.where(place == W - 1, final, state)
    full[pl.ds(pl.multiple_of(core * ROWS, ROWS), ROWS)] = own[0:ROWS]
    full[pl.ds(pl.multiple_of((1 - core) * ROWS, ROWS), ROWS)] = other[0:ROWS]
    row_at = lax.broadcasted_iota(jnp.int32, (count, W), 0)
    entry = moved(state, gain_powers[0])
    rows = full[...]
    rows = rows + jnp.where(row_at == count - 1, jnp.broadcast_to(entry[0:1], (count, W)), 0.0)

    def behind(rows, reach):
        return jnp.where(row_at < count - reach, pltpu.roll(rows, count - reach, 0), 0.0)

    for level in (0, 2, 4, 6):
        three = [behind(rows, q << level) for q in (1, 2, 3)]
        rows = moved_sum(rows, three, [gain_powers[level], gain_powers[level + 1], gain_triples[level // 2]])
    half = moved(rows[ROWS:], gain_powers[8])
    rows = jnp.concatenate([rows[:ROWS] + half, rows[ROWS:]], axis=0)
    smoothed[...] = rows
    following = jnp.where(
        row_at == count - 1, jnp.broadcast_to(state[0:1], (count, W)), pltpu.roll(rows, count - 1, 0)
    )
    packed = wide(rows)
    high = rows.astype(BF16)
    packed_t = jnp.concatenate([rows.T.astype(BF16), (rows - high.astype(F32)).T.astype(BF16)], axis=0)
    last_chip = where[0] == NEAR * FAR - 1
    lane_at = lax.broadcasted_iota(jnp.int32, (2 * W, count), 1)
    kept = jnp.where(last_chip & (lane_at == count - 1), jnp.zeros_like(packed_t), packed_t)

    def fold(out):
        return (out[:W, :W] + out[:W, W:]) + (out[W:, :W] + out[W:, W:])

    upper = lax.broadcasted_iota(jnp.int32, (W, W), 0) - lax.broadcasted_iota(jnp.int32, (W, W), 1)
    lag_cross_t = fold(jnp.dot(kept, wide(following), preferred_element_type=F32))
    fl = flags[...]
    repeat = (
        lax.broadcasted_iota(jnp.int32, (2 * SEGS, count), 0)
        == lax.broadcasted_iota(jnp.int32, (2 * SEGS, count), 1) // LEN
    )
    lane_flags = jnp.dot(fl.astype(F32).astype(BF16), repeat.astype(BF16), preferred_element_type=F32)
    flagged = [packed_t * lane_flags[g : g + 1].astype(BF16) for g in range(4)]
    product = jnp.dot(jnp.concatenate([kept] + flagged, axis=0), packed, preferred_element_type=F32)
    lag_gram, *grams = [fold(product[2 * W * g : 2 * W * (g + 1)]) for g in range(5)]
    def diagonal(gram):
        return jnp.sum(jnp.where(upper == 0, gram, 0.0), axis=0, keepdims=True)

    for tile in range(2):
        parts[tile * W : (tile + 1) * W] = jnp.where(upper <= 0, grams[2 * tile], grams[2 * tile + 1])
    parts[4 * W : 5 * W] = jnp.where(upper <= 0, lag_gram, lag_cross_t)
    parts[5 * W : 6 * W] = jnp.where(upper <= 0, lag_cross_t, 0.0)
    lane = lax.broadcasted_iota(jnp.int32, (1, W), 1)
    for tile in range(2):
        line = diagonal(grams[2 * tile + 1])
        for half in range(2):
            row = 6 * W - 4 + 2 * tile + half
            moved_line = line if half == 0 else pltpu.roll(line, W // 2, 1)
            parts[row : row + 1] = jnp.where(lane < W // 2, moved_line, parts[row : row + 1])
    high, low = halves(tel[...] * mask_of(fl, count, 0))
    cross = jnp.dot(packed_t, high, preferred_element_type=F32) + jnp.dot(
        packed_t, low, preferred_element_type=F32
    )
    cross = cross[:W] + cross[W:]
    parts[2 * W : 3 * W] = cross[:, :W]
    parts[3 * W : 4 * W] = cross[:, W:]

def sum_kernel(count, copies, parts, out):
    rows = SLICE
    total = parts[0:rows]
    for j in range(1, count):
        total = total + parts[j * rows : (j + 1) * rows]
    for j in range(copies):
        out[j * rows : (j + 1) * rows] = total


def exact(left, right):
    return jnp.dot(left, right, precision=lax.Precision.HIGHEST, preferred_element_type=F32)


def sweep(entry, count):
    entry = [list(row) for row in entry]
    for q in range(count):
        scale = 1.0 / entry[q][q]
        row = [entry[q][c] * scale for c in range(count)]
        for r in range(count):
            for c in range(r, count):
                if q not in (r, c):
                    entry[r][c] = entry[r][c] - entry[r][q] * row[c]
        for r in range(count):
            entry[r][q] = entry[q][r] = row[r]
        entry[q][q] = -scale
        for r in range(count):
            for c in range(r):
                entry[r][c] = entry[c][r]
    return entry


def inverses(matrices):
    unit, pivots = 32, 8
    lane = lax.broadcasted_iota(jnp.int32, (W, W), 1)
    lane_tile = lane[:8]
    lane_head = lane[:unit]
    row_head = lax.broadcasted_iota(jnp.int32, (unit, W), 0)
    sublane = lax.broadcasted_iota(jnp.int32, (8, W), 0)

    def panel(b, held):
        heads = [m[:unit] for m in held]
        for j in range(0, unit, pivots):
            stacked = []
            for r in range(pivots):
                rows = jnp.broadcast_to(heads[0][j + r : j + r + 1], (8, W))
                for p in range(1, len(heads)):
                    mine = jnp.broadcast_to(heads[p][j + r : j + r + 1], (8, W))
                    rows = jnp.where(sublane == p, mine, rows)
                stacked.append(rows)
            entry = [[None] * pivots for _ in range(pivots)]
            for r in range(pivots):
                for c in range(r, pivots):
                    value = jnp.broadcast_to(stacked[r][:, j + c : j + c + 1], (8, W))
                    entry[r][c] = entry[c][r] = value
            entry = sweep(entry, pivots)
            fresh = []
            for r in range(pivots):
                total = entry[r][0] * stacked[0]
                for c in range(1, pivots):
                    total = total + entry[r][c] * stacked[c]
                for c in range(pivots):
                    total = jnp.where(lane_tile == j + c, entry[r][c], total)
                fresh.append(-total)
            for p, head in enumerate(heads):
                rows = [
                    jnp.concatenate([jnp.broadcast_to(row[p : p + 1], (8, W))] * (unit // 8), axis=0)
                    for row in fresh
                ]
                after = jnp.where(lane_head // pivots == j // pivots, 0.0, head)
                for r in range(pivots):
                    after = after - jnp.broadcast_to(head[:, j + r : j + r + 1], (unit, W)) * rows[r]
                for r in range(pivots):
                    after = jnp.where(row_head == j + r, rows[r], after)
                heads[p] = after
        turned = []
        for head, m in zip(heads, held):
            rest = m[unit:]
            rest = jnp.where(lane[unit:] < unit, 0.0, rest) - exact(rest[:, :unit], head)
            turned.append(pltpu.roll(jnp.concatenate([rest, head], axis=0), W - unit, 1))
        return tuple(turned)

    return lax.fori_loop(0, W // unit, panel, tuple(matrices))


def solve_kernel(ridge, stats, new_transition, new_sensing):
    rows = lax.broadcasted_iota(jnp.int32, (W, W), 0)
    lanes = lax.broadcasted_iota(jnp.int32, (W, W), 1)
    eye = jnp.where(rows == lanes, ridge, 0.0).astype(F32)
    lag_a = stats[4 * W : 5 * W]
    lag_b = stats[5 * W : 6 * W]
    half = lax.broadcasted_iota(jnp.int32, (1, W), 1) < W // 2
    def upper(tile):
        return jnp.where(rows <= lanes, tile, 0.0) + jnp.where(rows < lanes, tile, 0.0).T

    def lower(tile, diagonal):
        below = jnp.where(rows > lanes, tile, 0.0)
        return below + below.T + jnp.where(rows == lanes, diagonal, 0.0)

    grams = [upper(lag_a)]
    for tile in range(2):
        packed = stats[tile * W : (tile + 1) * W]
        row = 6 * W - 4 + 2 * tile
        line = jnp.where(half, stats[row : row + 1], pltpu.roll(stats[row + 1 : row + 2], W // 2, 1))
        grams.append(upper(packed))
        grams.append(lower(packed, line))
    done = inverses([gram + eye for gram in grams])
    lag_cross_t = jnp.where(rows > lanes, lag_a, lag_b)
    new_transition[...] = exact(lag_cross_t.T, done[0])
    for tile in range(2):
        cross = stats[(2 + tile) * W : (3 + tile) * W].T
        for side in range(2):
            g = 2 * tile + side
            new_sensing[g * 64 : (g + 1) * 64] = exact(cross[side * 64 : (side + 1) * 64], done[1 + g])


def swap_core(value):
    return lax.ppermute(value, "sens", [(0, 1), (1, 0)])


def exchange(value, stride, count):
    groups = [
        [first + stride * j for j in range(count)]
        for first in range(NEAR * FAR)
        if (first // stride) % count == 0
    ]
    return lax.all_to_all(value, "tm", 0, 0, axis_index_groups=groups, tiled=True)


def on_device(telemetry, present, transition, sensing, filter_gain, smooth_gain, initial_state):
    where = jnp.stack([lax.axis_index("tm"), lax.axis_index("sens")]).astype(jnp.int32)
    present = present.T
    other_gain = swap_core(filter_gain)
    other_sensing = swap_core(sensing)
    other_present = swap_core(present)
    mine, theirs = call(push_kernel, [shape(ROWS, W)] * 2, 1, 4, far=(0, 1, 2))(
        where, telemetry, present, filter_gain, other_present
    )
    received = swap_core(theirs)
    powers, whole, gain_powers, gain_triples, drive_map = call(
        maps_kernel,
        [
            shape(SEGS, 5, W, 2 * W, dtype=BF16), shape(SEGS, W, W), shape(16, W, 2 * W, dtype=BF16),
            shape(8, W, 2 * W, dtype=BF16), shape(W, 2 * W, dtype=BF16),
        ],
        3, 6,
        scratch=[pltpu.VMEM((8, W, W), F32), pltpu.VMEM((W, W), F32)],
        far=(0, 1, 3, 5),
        far_scalars=(1,),
    )(where, present, other_present, transition, filter_gain, other_gain, sensing, other_sensing, smooth_gain)
    inputs, ends, packed, tree = call(
        shift_kernel,
        [shape(ROWS, W), shape(32, W), shape(PACK, W), shape(SEGS - 1, W, 2 * W, dtype=BF16)], 0, 4
    )(mine, received, powers, whole)

    other_packed = swap_core(packed)
    (chip,) = call(pair_kernel, [shape(NEAR * PACK, W)], 1, 2)(where, packed, other_packed)
    near = exchange(chip, 1, NEAR)
    group, early = call(eight_kernel, [shape(FAR * PACK, W), shape(3, PACK, W)], 0, 1)(near)
    far = exchange(group, NEAR, FAR)
    drives, shift = call(
        filter_kernel, [shape(ROWS + 8, W), shape(W, W)], 1, 13, [pltpu.VMEM((3, PACK, W), F32)]
    )(
        where, far, near, early, other_packed, initial_state.reshape(1, W), inputs, ends, powers, tree,
        gain_powers, gain_triples, drive_map, transition,
    )
    other_drives = swap_core(drives)
    gathered = lax.all_to_all(shift, ("tm", "sens"), 0, 0, tiled=True)
    smoothed, stats = call(
        stats_kernel, [shape(2 * ROWS, W, leaves=True), shape(STATS, W)], 1, 7,
        [pltpu.VMEM((2 * ROWS, W), F32)],
    )(where, gathered, drives, other_drives, gain_powers, gain_triples, telemetry, present)

    stats = exchange(stats, 1, PLANE)
    (stats,) = call(functools.partial(sum_kernel, PLANE, PLANES), [shape(PLANES * SLICE, W)], 0, 1)(stats)
    stats = exchange(stats, PLANE, PLANES)
    (stats,) = call(functools.partial(sum_kernel, PLANES, PLANE), [shape(STATS, W)], 0, 1)(stats)
    stats = exchange(stats, 1, PLANE)
    ridge = RIDGE * telemetry.shape[0] * lax.axis_size("tm")
    new_transition, new_sensing = call(
        functools.partial(solve_kernel, ridge), [shape(W, W, leaves=True), shape(2 * W, W, leaves=True)], 0, 1
    )(stats)
    return new_transition, new_sensing, smoothed


def solution(mesh):
    placed = (P("tm", "sens"), P("tm", "sens"), P(), P("sens", None), P(None, "sens"), P(), P())
    return jax.shard_map(
        on_device,
        mesh=mesh,
        in_specs=placed,
        out_specs=(P(), P("sens", None), P("tm", None)),
        check_vma=False,
    )
```

```python
import functools

import jax
import jax.numpy as jnp
from jax import lax
from jax.experimental import pallas as pl
from jax.experimental.pallas import tpu as pltpu
from jax.sharding import PartitionSpec as P

RIDGE = 0.001
F32 = jnp.float32
BF16 = jnp.bfloat16
W = 128
SEGS = 16
LEN = 16
ROWS = SEGS * LEN
PACK = W + 8
NEAR = 8
FAR = 8
PLANE = 16
PLANES = 4
STATS = 6 * W
SLICE = STATS // PLANE
VMEM_LIMIT = 24 * 1024 * 1024


def halves(value):
    high = value.astype(BF16)
    low = (value - high.astype(F32)).astype(BF16)
    return high, low


def wide(value):
    high, low = halves(value)
    return jnp.concatenate([high, low], axis=1)


def times(left_wide, right_wide):
    stacked = jnp.concatenate([right_wide, right_wide], axis=0)
    out = jnp.dot(left_wide, stacked, preferred_element_type=F32)
    return out[:, :W] + out[:, W:]


def moved(rows, dev):
    return rows + times(wide(rows), dev)


def chained(first, second, second_wide):
    return first + second + times(wide(first), second_wide)


def identity():
    rows = lax.broadcasted_iota(jnp.int32, (W, W), 0)
    cols = lax.broadcasted_iota(jnp.int32, (W, W), 1)
    return jnp.where(rows == cols, 1.0, 0.0).astype(F32)


def call(kernel, out_shapes, n_smem, n_in, scratch=(), far=(), far_scalars=()):
    smem = [pl.BlockSpec(memory_space=pltpu.SMEM)] * n_smem
    vmem = [pl.BlockSpec(memory_space=pltpu.VMEM)] * n_in
    outs = [out if leaves else pltpu.VMEM(out.shape, out.dtype) for out, leaves in out_shapes]
    run = pl.pallas_call(
        kernel,
        out_shape=tuple(outs),
        in_specs=smem + vmem,
        out_specs=tuple([pl.BlockSpec(memory_space=pltpu.VMEM)] * len(outs)),
        scratch_shapes=list(scratch),
        compiler_params=pltpu.CompilerParams(vmem_limit_bytes=VMEM_LIMIT),
    )

    def placed(*operands):
        near = [
            pltpu.with_memory_space_constraint(v, pltpu.HBM if i in far else pltpu.VMEM)
            for i, v in enumerate(operands[n_smem:])
        ]
        scalars = [
            pltpu.with_memory_space_constraint(v, pltpu.HBM) if i in far_scalars else v
            for i, v in enumerate(operands[:n_smem])
        ]
        return run(*scalars, *near)

    return placed


def shape(*dims, dtype=F32, leaves=False):
    return jax.ShapeDtypeStruct(dims, dtype), leaves


def mask_of(flags, rows, first):
    blocks, segs = flags.shape
    spread = (
        lax.broadcasted_iota(jnp.int32, (blocks, 64 * blocks), 0)
        == lax.broadcasted_iota(jnp.int32, (blocks, 64 * blocks), 1) // 64
    )
    by_sensor = lax.dot_general(
        flags.astype(F32).astype(BF16), spread.astype(BF16), (((0,), (0,)), ((), ())),
        preferred_element_type=F32,
    )
    repeat = (
        lax.broadcasted_iota(jnp.int32, (rows, segs), 0) // LEN + first
        == lax.broadcasted_iota(jnp.int32, (rows, segs), 1)
    )
    return jnp.dot(repeat.astype(BF16), by_sensor.astype(BF16), preferred_element_type=F32)


def push_kernel(where, tel, flags, gain, unused, mine, theirs):
    gain_t = gain[...].T
    packed = wide(gain_t)
    for out, core in ((theirs, 1 - where[1]), (mine, where[1])):
        start = pl.multiple_of(core * ROWS, ROWS)
        mask = mask_of(flags[...], ROWS, core * SEGS)
        high, low = halves(tel[pl.ds(start, ROWS), :] * mask)
        total = jnp.dot(high, packed, preferred_element_type=F32) + jnp.dot(
            low, packed, preferred_element_type=F32
        )
        out[...] = total[:, :W] + total[:, W:]


def maps_kernel(
    where, flags_own, flags_other, trans, gain_own, gain_other, sense_own, sense_other, smooth_gain,
    powers, whole, gain_powers, gain_triples, drive_map, removed, single,
):
    a = trans[...]
    a_wide = wide(a)
    lane = lax.broadcasted_iota(jnp.int32, (W, 2 * W), 1) // 64
    for side, (gain, sense) in enumerate(((gain_own, sense_own), (gain_other, sense_other))):
        seen = times(wide(sense[...]), a_wide)
        seen_high, seen_low = halves(seen.T)
        gain_wide = wide(gain[...].T)
        zero = jnp.zeros_like(seen_high)
        blocks = [jnp.where(lane == g, part, zero) for g in range(4) for part in (seen_high, seen_low)]
        product = jnp.dot(jnp.concatenate(blocks, axis=0), gain_wide, preferred_element_type=F32)
        for g in range(4):
            part = product[2 * g * W : (2 * g + 1) * W] + product[(2 * g + 1) * W : (2 * g + 2) * W]
            removed[side * 4 + g] = part[:, :W] + part[:, W:]
    base = a.T - identity()
    single[...] = base
    gain_dev = smooth_gain[...].T - identity()
    drive_map[...] = wide(-chained(base, gain_dev, wide(gain_dev)))
    batch = 8

    def group(i, gain_dev):
        devs = []
        for j in range(batch):
            k = i * batch + j
            row = where[1] * SEGS + k
            dev = single[...]
            for g in range(4):
                dev = dev - flags_own[g, row].astype(F32) * removed[g]
                dev = dev - flags_other[g, row].astype(F32) * removed[4 + g]
            devs.append(dev)
        for level in range(4):
            for j in range(batch):
                packed = wide(devs[j])
                powers[i * batch + j, level] = packed
                devs[j] = 2.0 * devs[j] + times(packed, packed)
            packed = wide(gain_dev)
            twice = 2.0 * gain_dev + times(packed, packed)
            twice_packed = wide(twice)
            gain_powers[8 * i + 2 * level] = packed
            gain_powers[8 * i + 2 * level + 1] = twice_packed
            gain_triples[4 * i + level] = wide(chained(gain_dev, twice, twice_packed))
            gain_dev = 2.0 * twice + times(twice_packed, twice_packed)
        for j in range(batch):
            powers[i * batch + j, 4] = wide(devs[j])
            whole[i * batch + j] = devs[j]
        return gain_dev

    lax.fori_loop(0, SEGS // batch, group, gain_dev)


def seg_step(rows, powers, level, starts=None):
    row_at = lax.broadcasted_iota(jnp.int32, (ROWS, W), 0) % LEN
    reach = 1 << level
    before = jnp.where(row_at >= reach, pltpu.roll(rows, reach, 0), 0.0)
    if starts is not None:
        before = jnp.where(row_at == reach - 1, starts, before)
    packed = wide(before)
    parts = [times(packed[k * LEN : (k + 1) * LEN], powers[k, level]) for k in range(SEGS)]
    return rows + before + jnp.concatenate(parts, axis=0)


def shift_kernel(mine, received, powers, whole, inputs, ends, packed, tree):
    rows = mine[...] + received[...]
    inputs[...] = rows
    devs = [whole[k] for k in range(SEGS)]
    at = 0
    composite = []
    reached = rows
    for step in range(4):
        devs = [
            chained(devs[2 * p], devs[2 * p + 1], wide(devs[2 * p + 1])) for p in range(len(devs) // 2)
        ]
        reached = seg_step(reached, powers, step)
        for p, dev in enumerate(devs):
            dev_wide = wide(dev)
            composite.append(dev_wide)
            tree[at + p] = dev_wide
        at += len(devs)
    level = [reached[k * LEN + LEN - 1 : (k + 1) * LEN] for k in range(SEGS)]
    ends[0:SEGS] = jnp.concatenate(level, axis=0)
    maps = [powers[k, 4] for k in range(SEGS)]
    at, tree_at = SEGS, 0
    while len(level) > 1:
        level = [
            moved(jnp.broadcast_to(level[2 * p], (8, W)), maps[2 * p + 1])[0:1] + level[2 * p + 1]
            for p in range(len(level) // 2)
        ]
        maps = composite[tree_at : tree_at + len(level)]
        tree_at += len(level)
        for p, row in enumerate(level):
            ends[at + p : at + p + 1] = row
        at += len(level)
    packed[0:W] = devs[0]
    packed[W:PACK] = jnp.broadcast_to(level[0], (PACK - W, W))


def join2(first, second):
    second_dev = second[0:W]
    second_wide = wide(second_dev)
    dev = chained(first[0:W], second_dev, second_wide)
    row = moved(first[W:PACK], second_wide) + second[W:PACK]
    return dev, row


def repeated(out, row, value, copies, rows):
    for j in range(copies):
        out[j * rows + row : j * rows + row + value.shape[0]] = value


def pair_kernel(where, own, other, out):
    core = where[1]
    mine, theirs = own[...], other[...]
    first = jnp.where(core == 0, mine, theirs)
    second = jnp.where(core == 0, theirs, mine)
    dev, row = join2(first, second)
    repeated(out, 0, dev, NEAR, PACK)
    repeated(out, W, row, NEAR, PACK)


def split_maps(raw):
    return [(raw[j * PACK : j * PACK + W], raw[j * PACK + W : (j + 1) * PACK]) for j in range(8)]


def joined(first, second):
    second_wide = wide(second[0])
    return chained(first[0], second[0], second_wide), moved(first[1], second_wide) + second[1]


def eight_kernel(raw, out, early):
    level = split_maps(raw)
    pairs = [joined(level[2 * p], level[2 * p + 1]) for p in range(4)]
    fours = [joined(pairs[0], pairs[1]), joined(pairs[2], pairs[3])]
    dev, row = joined(*fours)
    repeated(out, 0, dev, FAR, PACK)
    repeated(out, W, row, FAR, PACK)
    for slot, (dev, row) in enumerate((fours[0], pairs[0], pairs[2])):
        early[slot, 0:W] = dev
        early[slot, W:PACK] = row


def stages(at, raw, early):
    start = pl.multiple_of((at & 6) * PACK, 8)
    packed = (
        (at >= 4, early[0]), ((at & 2) != 0, early[1 + (at >> 2)]), ((at & 1) != 0, raw[pl.ds(start, PACK)])
    )
    return [masked(used, value) for used, value in packed]


def masked(used, packed):
    packed = jnp.where(used, packed, 0.0)
    return packed[0:W], packed[W : W + 8]


def after_map(state, joined_map):
    return moved(state, wide(joined_map[0])) + joined_map[1]


def moved_sum(first, others, devs):
    total = first
    for rows in others:
        total = total + rows
    left = jnp.concatenate([wide(rows) for rows in others], axis=1)
    right = jnp.concatenate([part for dev in devs for part in (dev, dev)], axis=0)
    out = jnp.dot(left, right, preferred_element_type=F32)
    return total + (out[:, :W] + out[:, W:])


def power_sum(part, powers, triples, first):
    level = part.shape[0].bit_length() - 1
    if level % 2:
        level -= 1
        half = 1 << level
        part = moved_sum(part[:half], [part[half:]], [powers[first + level]])
    while level:
        level -= 2
        span = 1 << level
        devs = [powers[first + level], powers[first + level + 1], triples[(first + level) // 2]]
        if span >= 8:
            pieces = [part[q * span : (q + 1) * span] for q in range(4)]
        elif span == 4:
            near, far = part[:8], part[8:]
            pieces = [near, pltpu.roll(near, 4, 0), far, pltpu.roll(far, 4, 0)]
        else:
            pieces = [part] + [pltpu.roll(part, 8 - q * span, 0) for q in (1, 2, 3)]
        part = moved_sum(pieces[0], pieces[1:], devs)
    return part


def filter_kernel(
    where, far, near, early, c1, initial, inputs, ends, powers, tree, gain_powers, gain_triples, drive_map,
    trans, drives, shift, far_early,
):
    device, core = where[0], where[1]
    level = split_maps(far)
    pairs = [joined(level[2 * p], level[2 * p + 1]) for p in range(3)]
    for slot, (dev, row) in enumerate((joined(pairs[0], pairs[1]), pairs[0], pairs[2])):
        far_early[slot, 0:W] = dev
        far_early[slot, W:PACK] = row
    state = jnp.broadcast_to(initial[...], (8, W))
    for stage in stages(device // NEAR, far, far_early):
        state = after_map(state, stage)
    inner = stages(device % NEAR, near, early)
    inner.append(masked(core == 1, c1[...]))
    state = after_map(state, joined(joined(inner[0], inner[1]), joined(inner[2], inner[3])))
    starts = {0: state}
    for span, maps_at, ends_at in ((8, 12, 28), (4, 8, 24), (2, 0, 16), (1, -1, 0)):
        for begin in range(0, SEGS, 2 * span):
            p = begin // span
            dev = powers[p, 4] if span == 1 else tree[maps_at + p]
            starts[begin + span] = moved(starts[begin], dev) + ends[ends_at + p : ends_at + p + 1]
    starts[SEGS] = moved(starts[SEGS - 1], powers[SEGS - 1, 4]) + ends[SEGS - 1 : SEGS]

    def spread(first):
        return jnp.concatenate([starts[first + k] for k in range(SEGS) for half in range(2)], axis=0)

    entry = spread(0)
    rows = inputs[...]
    for step in range(4):
        rows = seg_step(rows, powers, step, entry)
    row_at = lax.broadcasted_iota(jnp.int32, (ROWS, W), 0) % LEN
    rows = jnp.where(row_at == LEN - 1, spread(1), rows)
    drive = times(wide(rows), drive_map[...])
    drives[0:ROWS] = drive
    last = jnp.broadcast_to(rows[ROWS - 1 : ROWS], (8, W))
    final_row = last + times(wide(last), wide(trans[...].T - identity()))
    drives[ROWS : ROWS + 8] = final_row
    top = (device == NEAR * FAR - 1) & (core == 1)
    part = power_sum(drive, gain_powers, gain_triples, 0)
    from_top = moved(final_row, gain_powers[8])
    own = part[0:1] + jnp.where(top, from_top[0:1], 0.0)
    shift[...] = jnp.broadcast_to(own, (W, W))


def stats_kernel(
    where, gathered, own, other, gain_powers, gain_triples, tel, flags, smoothed, parts, full,
):
    core = where[1]
    count = 2 * ROWS
    place = 2 * where[0] + 1
    later = pltpu.roll(gathered[...], W - 1 - place, 0)
    row = lax.broadcasted_iota(jnp.int32, (W, W), 0)
    later = jnp.where(row < W - 1 - place, later, 0.0)
    state = jnp.broadcast_to(power_sum(later, gain_powers, gain_triples, 8)[0:1], (8, W))
    final = jnp.where(core == 1, own[ROWS : ROWS + 8], other[ROWS : ROWS + 8])
    state = jnp.where(place == W - 1, final, state)
    full[pl.ds(pl.multiple_of(core * ROWS, ROWS), ROWS)] = own[0:ROWS]
    full[pl.ds(pl.multiple_of((1 - core) * ROWS, ROWS), ROWS)] = other[0:ROWS]
    row_at = lax.broadcasted_iota(jnp.int32, (count, W), 0)
    entry = moved(state, gain_powers[0])
    rows = full[...]
    rows = rows + jnp.where(row_at == count - 1, jnp.broadcast_to(entry[0:1], (count, W)), 0.0)

    def behind(rows, reach):
        return jnp.where(row_at < count - reach, pltpu.roll(rows, count - reach, 0), 0.0)

    for level in (0, 2, 4, 6):
        three = [behind(rows, q << level) for q in (1, 2, 3)]
        rows = moved_sum(rows, three, [gain_powers[level], gain_powers[level + 1], gain_triples[level // 2]])
    half = moved(rows[ROWS:], gain_powers[8])
    rows = jnp.concatenate([rows[:ROWS] + half, rows[ROWS:]], axis=0)
    smoothed[...] = rows
    following = jnp.where(
        row_at == count - 1, jnp.broadcast_to(state[0:1], (count, W)), pltpu.roll(rows, count - 1, 0)
    )
    packed = wide(rows)
    high = rows.astype(BF16)
    packed_t = jnp.concatenate([rows.T.astype(BF16), (rows - high.astype(F32)).T.astype(BF16)], axis=0)
    last_chip = where[0] == NEAR * FAR - 1
    lane_at = lax.broadcasted_iota(jnp.int32, (2 * W, count), 1)
    kept = jnp.where(last_chip & (lane_at == count - 1), jnp.zeros_like(packed_t), packed_t)

    def fold(out):
        return (out[:W, :W] + out[:W, W:]) + (out[W:, :W] + out[W:, W:])

    upper = lax.broadcasted_iota(jnp.int32, (W, W), 0) - lax.broadcasted_iota(jnp.int32, (W, W), 1)
    lag_cross_t = fold(jnp.dot(kept, wide(following), preferred_element_type=F32))
    fl = flags[...]
    repeat = (
        lax.broadcasted_iota(jnp.int32, (2 * SEGS, count), 0)
        == lax.broadcasted_iota(jnp.int32, (2 * SEGS, count), 1) // LEN
    )
    lane_flags = jnp.dot(fl.astype(F32).astype(BF16), repeat.astype(BF16), preferred_element_type=F32)
    flagged = [packed_t * lane_flags[g : g + 1].astype(BF16) for g in range(4)]
    product = jnp.dot(jnp.concatenate([kept] + flagged, axis=0), packed, preferred_element_type=F32)
    lag_gram, *grams = [fold(product[2 * W * g : 2 * W * (g + 1)]) for g in range(5)]
    def diagonal(gram):
        return jnp.sum(jnp.where(upper == 0, gram, 0.0), axis=0, keepdims=True)

    for tile in range(2):
        parts[tile * W : (tile + 1) * W] = jnp.where(upper <= 0, grams[2 * tile], grams[2 * tile + 1])
    parts[4 * W : 5 * W] = jnp.where(upper <= 0, lag_gram, lag_cross_t)
    parts[5 * W : 6 * W] = jnp.where(upper <= 0, lag_cross_t, 0.0)
    lane = lax.broadcasted_iota(jnp.int32, (1, W), 1)
    for tile in range(2):
        line = diagonal(grams[2 * tile + 1])
        for half in range(2):
            row = 6 * W - 4 + 2 * tile + half
            moved_line = line if half == 0 else pltpu.roll(line, W // 2, 1)
            parts[row : row + 1] = jnp.where(lane < W // 2, moved_line, parts[row : row + 1])
    high, low = halves(tel[...] * mask_of(fl, count, 0))
    cross = jnp.dot(packed_t, high, preferred_element_type=F32) + jnp.dot(
        packed_t, low, preferred_element_type=F32
    )
    cross = cross[:W] + cross[W:]
    parts[2 * W : 3 * W] = cross[:, :W]
    parts[3 * W : 4 * W] = cross[:, W:]

def sum_kernel(count, copies, parts, out):
    rows = SLICE
    total = parts[0:rows]
    for j in range(1, count):
        total = total + parts[j * rows : (j + 1) * rows]
    for j in range(copies):
        out[j * rows : (j + 1) * rows] = total


def exact(left, right):
    return jnp.dot(left, right, precision=lax.Precision.HIGHEST, preferred_element_type=F32)


def sweep(entry, count):
    entry = [list(row) for row in entry]
    for q in range(count):
        scale = 1.0 / entry[q][q]
        row = [entry[q][c] * scale for c in range(count)]
        for r in range(count):
            for c in range(r, count):
                if q not in (r, c):
                    entry[r][c] = entry[r][c] - entry[r][q] * row[c]
        for r in range(count):
            entry[r][q] = entry[q][r] = row[r]
        entry[q][q] = -scale
        for r in range(count):
            for c in range(r):
                entry[r][c] = entry[c][r]
    return entry


def inverses(matrices):
    unit, pivots = 32, 8
    lane = lax.broadcasted_iota(jnp.int32, (W, W), 1)
    lane_tile = lane[:8]
    sublane = lax.broadcasted_iota(jnp.int32, (8, W), 0)

    def panel(b, held):
        heads = [[m[t : t + 8] for t in range(0, unit, 8)] for m in held]
        for here in range(unit // pivots):
            j = here * pivots
            stacked = []
            for r in range(pivots):
                rows = jnp.broadcast_to(heads[0][here][r : r + 1], (8, W))
                for p in range(1, len(heads)):
                    mine = jnp.broadcast_to(heads[p][here][r : r + 1], (8, W))
                    rows = jnp.where(sublane == p, mine, rows)
                stacked.append(rows)
            entry = [[None] * pivots for _ in range(pivots)]
            for r in range(pivots):
                for c in range(r, pivots):
                    value = jnp.broadcast_to(stacked[r][:, j + c : j + c + 1], (8, W))
                    entry[r][c] = entry[c][r] = value
            entry = sweep(entry, pivots)
            fresh = []
            for r in range(pivots):
                total = entry[r][0] * stacked[0]
                for c in range(1, pivots):
                    total = total + entry[r][c] * stacked[c]
                for c in range(pivots):
                    total = jnp.where(lane_tile == j + c, entry[r][c], total)
                fresh.append(-total)
            for p, tiles in enumerate(heads):
                rows = [jnp.broadcast_to(row[p : p + 1], (8, W)) for row in fresh]
                for t, tile in enumerate(tiles):
                    if t == here:
                        after = rows[0]
                        for r in range(1, pivots):
                            after = jnp.where(sublane == r, rows[r], after)
                    else:
                        after = jnp.where(lane_tile // pivots == here, 0.0, tile)
                        for r in range(pivots):
                            after = after - jnp.broadcast_to(tile[:, j + r : j + r + 1], (8, W)) * rows[r]
                    tiles[t] = after
        turned = []
        for tiles, m in zip(heads, held):
            head, rest = jnp.concatenate(tiles, axis=0), m[unit:]
            rest = jnp.where(lane[unit:] < unit, 0.0, rest) - exact(rest[:, :unit], head)
            turned.append(pltpu.roll(jnp.concatenate([rest, head], axis=0), W - unit, 1))
        return tuple(turned)

    return lax.fori_loop(0, W // unit, panel, tuple(matrices))


def solve_kernel(ridge, stats, new_transition, new_sensing):
    rows = lax.broadcasted_iota(jnp.int32, (W, W), 0)
    lanes = lax.broadcasted_iota(jnp.int32, (W, W), 1)
    eye = jnp.where(rows == lanes, ridge, 0.0).astype(F32)
    lag_a = stats[4 * W : 5 * W]
    lag_b = stats[5 * W : 6 * W]
    half = lax.broadcasted_iota(jnp.int32, (1, W), 1) < W // 2
    def upper(tile):
        return jnp.where(rows <= lanes, tile, 0.0) + jnp.where(rows < lanes, tile, 0.0).T

    def lower(tile, diagonal):
        below = jnp.where(rows > lanes, tile, 0.0)
        return below + below.T + jnp.where(rows == lanes, diagonal, 0.0)

    grams = [upper(lag_a)]
    for tile in range(2):
        packed = stats[tile * W : (tile + 1) * W]
        row = 6 * W - 4 + 2 * tile
        line = jnp.where(half, stats[row : row + 1], pltpu.roll(stats[row + 1 : row + 2], W // 2, 1))
        grams.append(upper(packed))
        grams.append(lower(packed, line))
    done = inverses([gram + eye for gram in grams])
    lag_cross_t = jnp.where(rows > lanes, lag_a, lag_b)
    new_transition[...] = exact(lag_cross_t.T, done[0])
    for tile in range(2):
        cross = stats[(2 + tile) * W : (3 + tile) * W].T
        for side in range(2):
            g = 2 * tile + side
            new_sensing[g * 64 : (g + 1) * 64] = exact(cross[side * 64 : (side + 1) * 64], done[1 + g])


def swap_core(value):
    return lax.ppermute(value, "sens", [(0, 1), (1, 0)])


def exchange(value, stride, count):
    groups = [
        [first + stride * j for j in range(count)]
        for first in range(NEAR * FAR)
        if (first // stride) % count == 0
    ]
    return lax.all_to_all(value, "tm", 0, 0, axis_index_groups=groups, tiled=True)


def on_device(telemetry, present, transition, sensing, filter_gain, smooth_gain, initial_state):
    where = jnp.stack([lax.axis_index("tm"), lax.axis_index("sens")]).astype(jnp.int32)
    present = present.T
    other_gain = swap_core(filter_gain)
    other_sensing = swap_core(sensing)
    other_present = swap_core(present)
    mine, theirs = call(push_kernel, [shape(ROWS, W)] * 2, 1, 4, far=(0, 1, 2))(
        where, telemetry, present, filter_gain, other_present
    )
    received = swap_core(theirs)
    powers, whole, gain_powers, gain_triples, drive_map = call(
        maps_kernel,
        [
            shape(SEGS, 5, W, 2 * W, dtype=BF16), shape(SEGS, W, W), shape(16, W, 2 * W, dtype=BF16),
            shape(8, W, 2 * W, dtype=BF16), shape(W, 2 * W, dtype=BF16),
        ],
        3, 6,
        scratch=[pltpu.VMEM((8, W, W), F32), pltpu.VMEM((W, W), F32)],
        far=(0, 1, 3, 5),
        far_scalars=(1,),
    )(where, present, other_present, transition, filter_gain, other_gain, sensing, other_sensing, smooth_gain)
    inputs, ends, packed, tree = call(
        shift_kernel,
        [shape(ROWS, W), shape(32, W), shape(PACK, W), shape(SEGS - 1, W, 2 * W, dtype=BF16)], 0, 4
    )(mine, received, powers, whole)

    other_packed = swap_core(packed)
    (chip,) = call(pair_kernel, [shape(NEAR * PACK, W)], 1, 2)(where, packed, other_packed)
    near = exchange(chip, 1, NEAR)
    group, early = call(eight_kernel, [shape(FAR * PACK, W), shape(3, PACK, W)], 0, 1)(near)
    far = exchange(group, NEAR, FAR)
    drives, shift = call(
        filter_kernel, [shape(ROWS + 8, W), shape(W, W)], 1, 13, [pltpu.VMEM((3, PACK, W), F32)]
    )(
        where, far, near, early, other_packed, initial_state.reshape(1, W), inputs, ends, powers, tree,
        gain_powers, gain_triples, drive_map, transition,
    )
    other_drives = swap_core(drives)
    gathered = lax.all_to_all(shift, ("tm", "sens"), 0, 0, tiled=True)
    smoothed, stats = call(
        stats_kernel, [shape(2 * ROWS, W, leaves=True), shape(STATS, W)], 1, 7,
        [pltpu.VMEM((2 * ROWS, W), F32)],
    )(where, gathered, drives, other_drives, gain_powers, gain_triples, telemetry, present)

    stats = exchange(stats, 1, PLANE)
    (stats,) = call(functools.partial(sum_kernel, PLANE, PLANES), [shape(PLANES * SLICE, W)], 0, 1)(stats)
    stats = exchange(stats, PLANE, PLANES)
    (stats,) = call(functools.partial(sum_kernel, PLANES, PLANE), [shape(STATS, W)], 0, 1)(stats)
    stats = exchange(stats, 1, PLANE)
    ridge = RIDGE * telemetry.shape[0] * lax.axis_size("tm")
    new_transition, new_sensing = call(
        functools.partial(solve_kernel, ridge), [shape(W, W, leaves=True), shape(2 * W, W, leaves=True)], 0, 1
    )(stats)
    return new_transition, new_sensing, smoothed


def solution(mesh):
    placed = (P("tm", "sens"), P("tm", "sens"), P(), P("sens", None), P(None, "sens"), P(), P())
    return jax.shard_map(
        on_device,
        mesh=mesh,
        in_specs=placed,
        out_specs=(P(), P("sens", None), P("tm", None)),
        check_vma=False,
    )
```

```python
import functools

import jax
import jax.numpy as jnp
from jax import lax
from jax.experimental import pallas as pl
from jax.experimental.pallas import tpu as pltpu
from jax.sharding import PartitionSpec as P

RIDGE = 0.001
F32 = jnp.float32
BF16 = jnp.bfloat16
W = 128
SEGS = 16
LEN = 16
ROWS = SEGS * LEN
PACK = W + 8
NEAR = 8
FAR = 8
PLANE = 16
PLANES = 4
STATS = 6 * W
SLICE = STATS // PLANE
VMEM_LIMIT = 24 * 1024 * 1024


def halves(value):
    high = value.astype(BF16)
    low = (value - high.astype(F32)).astype(BF16)
    return high, low


def wide(value):
    high, low = halves(value)
    return jnp.concatenate([high, low], axis=1)


def times(left_wide, right_wide):
    stacked = jnp.concatenate([right_wide, right_wide], axis=0)
    out = jnp.dot(left_wide, stacked, preferred_element_type=F32)
    return out[:, :W] + out[:, W:]


def moved(rows, dev):
    return rows + times(wide(rows), dev)


def chained(first, second, second_wide):
    return first + second + times(wide(first), second_wide)


def identity():
    rows = lax.broadcasted_iota(jnp.int32, (W, W), 0)
    cols = lax.broadcasted_iota(jnp.int32, (W, W), 1)
    return jnp.where(rows == cols, 1.0, 0.0).astype(F32)


def call(kernel, out_shapes, n_smem, n_in, scratch=(), far=(), far_scalars=()):
    smem = [pl.BlockSpec(memory_space=pltpu.SMEM)] * n_smem
    vmem = [pl.BlockSpec(memory_space=pltpu.VMEM)] * n_in
    outs = [out if leaves else pltpu.VMEM(out.shape, out.dtype) for out, leaves in out_shapes]
    run = pl.pallas_call(
        kernel,
        out_shape=tuple(outs),
        in_specs=smem + vmem,
        out_specs=tuple([pl.BlockSpec(memory_space=pltpu.VMEM)] * len(outs)),
        scratch_shapes=list(scratch),
        compiler_params=pltpu.CompilerParams(vmem_limit_bytes=VMEM_LIMIT),
    )

    def placed(*operands):
        near = [
            pltpu.with_memory_space_constraint(v, pltpu.HBM if i in far else pltpu.VMEM)
            for i, v in enumerate(operands[n_smem:])
        ]
        scalars = [
            pltpu.with_memory_space_constraint(v, pltpu.HBM) if i in far_scalars else v
            for i, v in enumerate(operands[:n_smem])
        ]
        return run(*scalars, *near)

    return placed


def shape(*dims, dtype=F32, leaves=False):
    return jax.ShapeDtypeStruct(dims, dtype), leaves


def mask_of(flags, rows, first):
    blocks, segs = flags.shape
    spread = (
        lax.broadcasted_iota(jnp.int32, (blocks, 64 * blocks), 0)
        == lax.broadcasted_iota(jnp.int32, (blocks, 64 * blocks), 1) // 64
    )
    by_sensor = lax.dot_general(
        flags.astype(F32).astype(BF16), spread.astype(BF16), (((0,), (0,)), ((), ())),
        preferred_element_type=F32,
    )
    repeat = (
        lax.broadcasted_iota(jnp.int32, (rows, segs), 0) // LEN + first
        == lax.broadcasted_iota(jnp.int32, (rows, segs), 1)
    )
    return jnp.dot(repeat.astype(BF16), by_sensor.astype(BF16), preferred_element_type=F32)


def push_kernel(where, tel, flags, gain, unused, mine, theirs):
    gain_t = gain[...].T
    packed = wide(gain_t)
    for out, core in ((theirs, 1 - where[1]), (mine, where[1])):
        start = pl.multiple_of(core * ROWS, ROWS)
        mask = mask_of(flags[...], ROWS, core * SEGS)
        high, low = halves(tel[pl.ds(start, ROWS), :] * mask)
        total = jnp.dot(high, packed, preferred_element_type=F32) + jnp.dot(
            low, packed, preferred_element_type=F32
        )
        out[...] = total[:, :W] + total[:, W:]


def maps_kernel(
    where, flags_own, flags_other, trans, gain_own, gain_other, sense_own, sense_other, smooth_gain,
    powers, whole, gain_powers, gain_triples, drive_map, removed, single,
):
    a = trans[...]
    a_wide = wide(a)
    lane = lax.broadcasted_iota(jnp.int32, (W, 2 * W), 1) // 64
    for side, (gain, sense) in enumerate(((gain_own, sense_own), (gain_other, sense_other))):
        seen = times(wide(sense[...]), a_wide)
        seen_high, seen_low = halves(seen.T)
        gain_wide = wide(gain[...].T)
        zero = jnp.zeros_like(seen_high)
        blocks = [jnp.where(lane == g, part, zero) for g in range(4) for part in (seen_high, seen_low)]
        product = jnp.dot(jnp.concatenate(blocks, axis=0), gain_wide, preferred_element_type=F32)
        for g in range(4):
            part = product[2 * g * W : (2 * g + 1) * W] + product[(2 * g + 1) * W : (2 * g + 2) * W]
            removed[side * 4 + g] = part[:, :W] + part[:, W:]
    base = a.T - identity()
    single[...] = base
    gain_dev = smooth_gain[...].T - identity()
    drive_map[...] = wide(-chained(base, gain_dev, wide(gain_dev)))
    batch = 8

    def group(i, gain_dev):
        devs = []
        for j in range(batch):
            k = i * batch + j
            row = where[1] * SEGS + k
            dev = single[...]
            for g in range(4):
                dev = dev - flags_own[g, row].astype(F32) * removed[g]
                dev = dev - flags_other[g, row].astype(F32) * removed[4 + g]
            devs.append(dev)
        for level in range(4):
            for j in range(batch):
                packed = wide(devs[j])
                powers[i * batch + j, level] = packed
                devs[j] = 2.0 * devs[j] + times(packed, packed)
            packed = wide(gain_dev)
            twice = 2.0 * gain_dev + times(packed, packed)
            twice_packed = wide(twice)
            gain_powers[8 * i + 2 * level] = packed
            gain_powers[8 * i + 2 * level + 1] = twice_packed
            gain_triples[4 * i + level] = wide(chained(gain_dev, twice, twice_packed))
            gain_dev = 2.0 * twice + times(twice_packed, twice_packed)
        for j in range(batch):
            powers[i * batch + j, 4] = wide(devs[j])
            whole[i * batch + j] = devs[j]
        return gain_dev

    lax.fori_loop(0, SEGS // batch, group, gain_dev)


def seg_step(rows, powers, level, starts=None):
    row_at = lax.broadcasted_iota(jnp.int32, (ROWS, W), 0) % LEN
    reach = 1 << level
    before = jnp.where(row_at >= reach, pltpu.roll(rows, reach, 0), 0.0)
    if starts is not None:
        before = jnp.where(row_at == reach - 1, starts, before)
    packed = wide(before)
    parts = [times(packed[k * LEN : (k + 1) * LEN], powers[k, level]) for k in range(SEGS)]
    return rows + before + jnp.concatenate(parts, axis=0)


def shift_kernel(mine, received, powers, whole, inputs, ends, packed, tree):
    rows = mine[...] + received[...]
    inputs[...] = rows
    devs = [whole[k] for k in range(SEGS)]
    at = 0
    composite = []
    reached = rows
    for step in range(4):
        devs = [
            chained(devs[2 * p], devs[2 * p + 1], wide(devs[2 * p + 1])) for p in range(len(devs) // 2)
        ]
        reached = seg_step(reached, powers, step)
        for p, dev in enumerate(devs):
            dev_wide = wide(dev)
            composite.append(dev_wide)
            tree[at + p] = dev_wide
        at += len(devs)
    level = [reached[k * LEN + LEN - 1 : (k + 1) * LEN] for k in range(SEGS)]
    ends[0:SEGS] = jnp.concatenate(level, axis=0)
    maps = [powers[k, 4] for k in range(SEGS)]
    at, tree_at = SEGS, 0
    while len(level) > 1:
        level = [
            moved(jnp.broadcast_to(level[2 * p], (8, W)), maps[2 * p + 1])[0:1] + level[2 * p + 1]
            for p in range(len(level) // 2)
        ]
        maps = composite[tree_at : tree_at + len(level)]
        tree_at += len(level)
        for p, row in enumerate(level):
            ends[at + p : at + p + 1] = row
        at += len(level)
    packed[0:W] = devs[0]
    packed[W:PACK] = jnp.broadcast_to(level[0], (PACK - W, W))


def join2(first, second):
    second_dev = second[0:W]
    second_wide = wide(second_dev)
    dev = chained(first[0:W], second_dev, second_wide)
    row = moved(first[W:PACK], second_wide) + second[W:PACK]
    return dev, row


def repeated(out, row, value, copies, rows):
    for j in range(copies):
        out[j * rows + row : j * rows + row + value.shape[0]] = value


def pair_kernel(where, own, other, out):
    core = where[1]
    mine, theirs = own[...], other[...]
    first = jnp.where(core == 0, mine, theirs)
    second = jnp.where(core == 0, theirs, mine)
    dev, row = join2(first, second)
    repeated(out, 0, dev, NEAR, PACK)
    repeated(out, W, row, NEAR, PACK)


def split_maps(raw):
    return [(raw[j * PACK : j * PACK + W], raw[j * PACK + W : (j + 1) * PACK]) for j in range(8)]


def joined(first, second):
    second_wide = wide(second[0])
    return chained(first[0], second[0], second_wide), moved(first[1], second_wide) + second[1]


def eight_kernel(raw, out, early):
    level = split_maps(raw)
    pairs = [joined(level[2 * p], level[2 * p + 1]) for p in range(4)]
    fours = [joined(pairs[0], pairs[1]), joined(pairs[2], pairs[3])]
    dev, row = joined(*fours)
    repeated(out, 0, dev, FAR, PACK)
    repeated(out, W, row, FAR, PACK)
    for slot, (dev, row) in enumerate((fours[0], pairs[0], pairs[2])):
        early[slot, 0:W] = dev
        early[slot, W:PACK] = row


def stages(at, raw, early):
    start = pl.multiple_of((at & 6) * PACK, 8)
    packed = (
        (at >= 4, early[0]), ((at & 2) != 0, early[1 + (at >> 2)]), ((at & 1) != 0, raw[pl.ds(start, PACK)])
    )
    return [masked(used, value) for used, value in packed]


def masked(used, packed):
    packed = jnp.where(used, packed, 0.0)
    return packed[0:W], packed[W : W + 8]


def after_map(state, joined_map):
    return moved(state, wide(joined_map[0])) + joined_map[1]


def moved_sum(first, others, devs):
    total = first
    for rows in others:
        total = total + rows
    left = jnp.concatenate([wide(rows) for rows in others], axis=1)
    right = jnp.concatenate([part for dev in devs for part in (dev, dev)], axis=0)
    out = jnp.dot(left, right, preferred_element_type=F32)
    return total + (out[:, :W] + out[:, W:])


def power_sum(part, powers, triples, first):
    level = part.shape[0].bit_length() - 1
    if level % 2:
        level -= 1
        half = 1 << level
        part = moved_sum(part[:half], [part[half:]], [powers[first + level]])
    while level:
        level -= 2
        span = 1 << level
        devs = [powers[first + level], powers[first + level + 1], triples[(first + level) // 2]]
        if span >= 8:
            pieces = [part[q * span : (q + 1) * span] for q in range(4)]
        elif span == 4:
            near, far = part[:8], part[8:]
            pieces = [near, pltpu.roll(near, 4, 0), far, pltpu.roll(far, 4, 0)]
        else:
            pieces = [part] + [pltpu.roll(part, 8 - q * span, 0) for q in (1, 2, 3)]
        part = moved_sum(pieces[0], pieces[1:], devs)
    return part


def filter_kernel(
    where, far, near, early, c1, initial, inputs, ends, powers, tree, gain_powers, gain_triples, drive_map,
    trans, drives, shift, far_early,
):
    device, core = where[0], where[1]
    level = split_maps(far)
    pairs = [joined(level[2 * p], level[2 * p + 1]) for p in range(3)]
    inner = stages(device % NEAR, near, early)
    inner.append(masked(core == 1, c1[...]))
    inner = joined(inner[0], inner[1]), joined(inner[2], inner[3])
    for slot, (dev, row) in enumerate((joined(pairs[0], pairs[1]), pairs[0], pairs[2])):
        far_early[slot, 0:W] = dev
        far_early[slot, W:PACK] = row
    inner = joined(*inner)
    state = jnp.broadcast_to(initial[...], (8, W))
    for stage in stages(device // NEAR, far, far_early):
        state = after_map(state, stage)
    state = after_map(state, inner)
    starts = {0: state}
    for span, maps_at, ends_at in ((8, 12, 28), (4, 8, 24), (2, 0, 16), (1, -1, 0)):
        for begin in range(0, SEGS, 2 * span):
            p = begin // span
            dev = powers[p, 4] if span == 1 else tree[maps_at + p]
            starts[begin + span] = moved(starts[begin], dev) + ends[ends_at + p : ends_at + p + 1]
    starts[SEGS] = moved(starts[SEGS - 1], powers[SEGS - 1, 4]) + ends[SEGS - 1 : SEGS]

    def spread(first):
        return jnp.concatenate([starts[first + k] for k in range(SEGS) for half in range(2)], axis=0)

    entry = spread(0)
    rows = inputs[...]
    for step in range(4):
        rows = seg_step(rows, powers, step, entry)
    row_at = lax.broadcasted_iota(jnp.int32, (ROWS, W), 0) % LEN
    rows = jnp.where(row_at == LEN - 1, spread(1), rows)
    drive = times(wide(rows), drive_map[...])
    drives[0:ROWS] = drive
    last = jnp.broadcast_to(rows[ROWS - 1 : ROWS], (8, W))
    final_row = last + times(wide(last), wide(trans[...].T - identity()))
    drives[ROWS : ROWS + 8] = final_row
    top = (device == NEAR * FAR - 1) & (core == 1)
    part = power_sum(drive, gain_powers, gain_triples, 0)
    from_top = moved(final_row, gain_powers[8])
    own = part[0:1] + jnp.where(top, from_top[0:1], 0.0)
    shift[...] = jnp.broadcast_to(own, (W, W))


def stats_kernel(
    where, gathered, own, other, gain_powers, gain_triples, tel, flags, smoothed, parts, full,
):
    core = where[1]
    count = 2 * ROWS
    place = 2 * where[0] + 1
    later = pltpu.roll(gathered[...], W - 1 - place, 0)
    row = lax.broadcasted_iota(jnp.int32, (W, W), 0)
    later = jnp.where(row < W - 1 - place, later, 0.0)
    state = jnp.broadcast_to(power_sum(later, gain_powers, gain_triples, 8)[0:1], (8, W))
    final = jnp.where(core == 1, own[ROWS : ROWS + 8], other[ROWS : ROWS + 8])
    state = jnp.where(place == W - 1, final, state)
    full[pl.ds(pl.multiple_of(core * ROWS, ROWS), ROWS)] = own[0:ROWS]
    full[pl.ds(pl.multiple_of((1 - core) * ROWS, ROWS), ROWS)] = other[0:ROWS]
    row_at = lax.broadcasted_iota(jnp.int32, (count, W), 0)
    entry = moved(state, gain_powers[0])
    rows = full[...]
    rows = rows + jnp.where(row_at == count - 1, jnp.broadcast_to(entry[0:1], (count, W)), 0.0)

    def behind(rows, reach):
        return jnp.where(row_at < count - reach, pltpu.roll(rows, count - reach, 0), 0.0)

    for level in (0, 2, 4, 6):
        three = [behind(rows, q << level) for q in (1, 2, 3)]
        rows = moved_sum(rows, three, [gain_powers[level], gain_powers[level + 1], gain_triples[level // 2]])
    half = moved(rows[ROWS:], gain_powers[8])
    rows = jnp.concatenate([rows[:ROWS] + half, rows[ROWS:]], axis=0)
    smoothed[...] = rows
    following = jnp.where(
        row_at == count - 1, jnp.broadcast_to(state[0:1], (count, W)), pltpu.roll(rows, count - 1, 0)
    )
    packed = wide(rows)
    high = rows.astype(BF16)
    packed_t = jnp.concatenate([rows.T.astype(BF16), (rows - high.astype(F32)).T.astype(BF16)], axis=0)
    last_chip = where[0] == NEAR * FAR - 1
    lane_at = lax.broadcasted_iota(jnp.int32, (2 * W, count), 1)
    kept = jnp.where(last_chip & (lane_at == count - 1), jnp.zeros_like(packed_t), packed_t)

    def fold(out):
        return (out[:W, :W] + out[:W, W:]) + (out[W:, :W] + out[W:, W:])

    upper = lax.broadcasted_iota(jnp.int32, (W, W), 0) - lax.broadcasted_iota(jnp.int32, (W, W), 1)
    lag_cross_t = fold(jnp.dot(kept, wide(following), preferred_element_type=F32))
    fl = flags[...]
    repeat = (
        lax.broadcasted_iota(jnp.int32, (2 * SEGS, count), 0)
        == lax.broadcasted_iota(jnp.int32, (2 * SEGS, count), 1) // LEN
    )
    lane_flags = jnp.dot(fl.astype(F32).astype(BF16), repeat.astype(BF16), preferred_element_type=F32)
    flagged = [packed_t * lane_flags[g : g + 1].astype(BF16) for g in range(4)]
    product = jnp.dot(jnp.concatenate([kept] + flagged, axis=0), packed, preferred_element_type=F32)
    lag_gram, *grams = [fold(product[2 * W * g : 2 * W * (g + 1)]) for g in range(5)]
    def diagonal(gram):
        return jnp.sum(jnp.where(upper == 0, gram, 0.0), axis=0, keepdims=True)

    for tile in range(2):
        parts[tile * W : (tile + 1) * W] = jnp.where(upper <= 0, grams[2 * tile], grams[2 * tile + 1])
    parts[4 * W : 5 * W] = jnp.where(upper <= 0, lag_gram, lag_cross_t)
    parts[5 * W : 6 * W] = jnp.where(upper <= 0, lag_cross_t, 0.0)
    lane = lax.broadcasted_iota(jnp.int32, (1, W), 1)
    for tile in range(2):
        line = diagonal(grams[2 * tile + 1])
        for half in range(2):
            row = 6 * W - 4 + 2 * tile + half
            moved_line = line if half == 0 else pltpu.roll(line, W // 2, 1)
            parts[row : row + 1] = jnp.where(lane < W // 2, moved_line, parts[row : row + 1])
    high, low = halves(tel[...] * mask_of(fl, count, 0))
    cross = jnp.dot(packed_t, high, preferred_element_type=F32) + jnp.dot(
        packed_t, low, preferred_element_type=F32
    )
    cross = cross[:W] + cross[W:]
    parts[2 * W : 3 * W] = cross[:, :W]
    parts[3 * W : 4 * W] = cross[:, W:]

def sum_kernel(count, copies, parts, out):
    rows = SLICE
    total = parts[0:rows]
    for j in range(1, count):
        total = total + parts[j * rows : (j + 1) * rows]
    for j in range(copies):
        out[j * rows : (j + 1) * rows] = total


def exact(left, right):
    return jnp.dot(left, right, precision=lax.Precision.HIGHEST, preferred_element_type=F32)


def sweep(entry, count):
    entry = [list(row) for row in entry]
    for q in range(count):
        scale = 1.0 / entry[q][q]
        row = [entry[q][c] * scale for c in range(count)]
        for r in range(count):
            for c in range(r, count):
                if q not in (r, c):
                    entry[r][c] = entry[r][c] - entry[r][q] * row[c]
        for r in range(count):
            entry[r][q] = entry[q][r] = row[r]
        entry[q][q] = -scale
        for r in range(count):
            for c in range(r):
                entry[r][c] = entry[c][r]
    return entry


def inverses(matrices):
    unit, pivots = 32, 8
    lane = lax.broadcasted_iota(jnp.int32, (W, W), 1)
    lane_tile = lane[:8]
    sublane = lax.broadcasted_iota(jnp.int32, (8, W), 0)

    def panel(b, held):
        heads = [[m[t : t + 8] for t in range(0, unit, 8)] for m in held]
        for here in range(unit // pivots):
            j = here * pivots
            stacked = []
            for r in range(pivots):
                rows = jnp.broadcast_to(heads[0][here][r : r + 1], (8, W))
                for p in range(1, len(heads)):
                    mine = jnp.broadcast_to(heads[p][here][r : r + 1], (8, W))
                    rows = jnp.where(sublane == p, mine, rows)
                stacked.append(rows)
            entry = [[None] * pivots for _ in range(pivots)]
            for r in range(pivots):
                for c in range(r, pivots):
                    value = jnp.broadcast_to(stacked[r][:, j + c : j + c + 1], (8, W))
                    entry[r][c] = entry[c][r] = value
            entry = sweep(entry, pivots)
            fresh = []
            for r in range(pivots):
                total = entry[r][0] * stacked[0]
                for c in range(1, pivots):
                    total = total + entry[r][c] * stacked[c]
                for c in range(pivots):
                    total = jnp.where(lane_tile == j + c, entry[r][c], total)
                fresh.append(-total)
            for p, tiles in enumerate(heads):
                rows = [jnp.broadcast_to(row[p : p + 1], (8, W)) for row in fresh]
                for t, tile in enumerate(tiles):
                    if t == here:
                        after = rows[0]
                        for r in range(1, pivots):
                            after = jnp.where(sublane == r, rows[r], after)
                    else:
                        after = jnp.where(lane_tile // pivots == here, 0.0, tile)
                        for r in range(pivots):
                            after = after - jnp.broadcast_to(tile[:, j + r : j + r + 1], (8, W)) * rows[r]
                    tiles[t] = after
        turned = []
        for tiles, m in zip(heads, held):
            head, rest = jnp.concatenate(tiles, axis=0), m[unit:]
            rest = jnp.where(lane[unit:] < unit, 0.0, rest) - exact(rest[:, :unit], head)
            turned.append(pltpu.roll(jnp.concatenate([rest, head], axis=0), W - unit, 1))
        return tuple(turned)

    return lax.fori_loop(0, W // unit, panel, tuple(matrices))


def solve_kernel(ridge, stats, new_transition, new_sensing):
    rows = lax.broadcasted_iota(jnp.int32, (W, W), 0)
    lanes = lax.broadcasted_iota(jnp.int32, (W, W), 1)
    eye = jnp.where(rows == lanes, ridge, 0.0).astype(F32)
    lag_a = stats[4 * W : 5 * W]
    lag_b = stats[5 * W : 6 * W]
    half = lax.broadcasted_iota(jnp.int32, (1, W), 1) < W // 2
    def upper(tile):
        return jnp.where(rows <= lanes, tile, 0.0) + jnp.where(rows < lanes, tile, 0.0).T

    def lower(tile, diagonal):
        below = jnp.where(rows > lanes, tile, 0.0)
        return below + below.T + jnp.where(rows == lanes, diagonal, 0.0)

    grams = [upper(lag_a)]
    for tile in range(2):
        packed = stats[tile * W : (tile + 1) * W]
        row = 6 * W - 4 + 2 * tile
        line = jnp.where(half, stats[row : row + 1], pltpu.roll(stats[row + 1 : row + 2], W // 2, 1))
        grams.append(upper(packed))
        grams.append(lower(packed, line))
    done = inverses([gram + eye for gram in grams])
    lag_cross_t = jnp.where(rows > lanes, lag_a, lag_b)
    new_transition[...] = exact(lag_cross_t.T, done[0])
    for tile in range(2):
        cross = stats[(2 + tile) * W : (3 + tile) * W].T
        for side in range(2):
            g = 2 * tile + side
            new_sensing[g * 64 : (g + 1) * 64] = exact(cross[side * 64 : (side + 1) * 64], done[1 + g])


def swap_core(value):
    return lax.ppermute(value, "sens", [(0, 1), (1, 0)])


def exchange(value, stride, count):
    groups = [
        [first + stride * j for j in range(count)]
        for first in range(NEAR * FAR)
        if (first // stride) % count == 0
    ]
    return lax.all_to_all(value, "tm", 0, 0, axis_index_groups=groups, tiled=True)


def on_device(telemetry, present, transition, sensing, filter_gain, smooth_gain, initial_state):
    where = jnp.stack([lax.axis_index("tm"), lax.axis_index("sens")]).astype(jnp.int32)
    present = present.T
    other_gain = swap_core(filter_gain)
    other_sensing = swap_core(sensing)
    other_present = swap_core(present)
    mine, theirs = call(push_kernel, [shape(ROWS, W)] * 2, 1, 4, far=(0, 1, 2))(
        where, telemetry, present, filter_gain, other_present
    )
    received = swap_core(theirs)
    powers, whole, gain_powers, gain_triples, drive_map = call(
        maps_kernel,
        [
            shape(SEGS, 5, W, 2 * W, dtype=BF16), shape(SEGS, W, W), shape(16, W, 2 * W, dtype=BF16),
            shape(8, W, 2 * W, dtype=BF16), shape(W, 2 * W, dtype=BF16),
        ],
        3, 6,
        scratch=[pltpu.VMEM((8, W, W), F32), pltpu.VMEM((W, W), F32)],
        far=(0, 1, 3, 5),
        far_scalars=(1,),
    )(where, present, other_present, transition, filter_gain, other_gain, sensing, other_sensing, smooth_gain)
    inputs, ends, packed, tree = call(
        shift_kernel,
        [shape(ROWS, W), shape(32, W), shape(PACK, W), shape(SEGS - 1, W, 2 * W, dtype=BF16)], 0, 4
    )(mine, received, powers, whole)

    other_packed = swap_core(packed)
    (chip,) = call(pair_kernel, [shape(NEAR * PACK, W)], 1, 2)(where, packed, other_packed)
    near = exchange(chip, 1, NEAR)
    group, early = call(eight_kernel, [shape(FAR * PACK, W), shape(3, PACK, W)], 0, 1)(near)
    far = exchange(group, NEAR, FAR)
    drives, shift = call(
        filter_kernel, [shape(ROWS + 8, W), shape(W, W)], 1, 13, [pltpu.VMEM((3, PACK, W), F32)]
    )(
        where, far, near, early, other_packed, initial_state.reshape(1, W), inputs, ends, powers, tree,
        gain_powers, gain_triples, drive_map, transition,
    )
    other_drives = swap_core(drives)
    gathered = lax.all_to_all(shift, ("tm", "sens"), 0, 0, tiled=True)
    smoothed, stats = call(
        stats_kernel, [shape(2 * ROWS, W, leaves=True), shape(STATS, W)], 1, 7,
        [pltpu.VMEM((2 * ROWS, W), F32)],
    )(where, gathered, drives, other_drives, gain_powers, gain_triples, telemetry, present)

    stats = exchange(stats, 1, PLANE)
    (stats,) = call(functools.partial(sum_kernel, PLANE, PLANES), [shape(PLANES * SLICE, W)], 0, 1)(stats)
    stats = exchange(stats, PLANE, PLANES)
    (stats,) = call(functools.partial(sum_kernel, PLANES, PLANE), [shape(STATS, W)], 0, 1)(stats)
    stats = exchange(stats, 1, PLANE)
    ridge = RIDGE * telemetry.shape[0] * lax.axis_size("tm")
    new_transition, new_sensing = call(
        functools.partial(solve_kernel, ridge), [shape(W, W, leaves=True), shape(2 * W, W, leaves=True)], 0, 1
    )(stats)
    return new_transition, new_sensing, smoothed


def solution(mesh):
    placed = (P("tm", "sens"), P("tm", "sens"), P(), P("sens", None), P(None, "sens"), P(), P())
    return jax.shard_map(
        on_device,
        mesh=mesh,
        in_specs=placed,
        out_specs=(P(), P("sens", None), P("tm", None)),
        check_vma=False,
    )
```
